256 devices in a mesh: gx: 32 (over y, z), gy: 8 (over x, core).
Axes of the slice: x: 4, y: 4, z: 8, core: 2. Of those that a mesh axis runs over, the one named last changes fastest.
Arguments:
- rhs: bfloat16 [512, 262144], P(None, ('gy', 'gx')), may hold values from -6 to 6
- leaf_inverse: bfloat16 [256, 1024, 1024], P(('gy', 'gx')), may hold values from -0.1875 to 0.1875
- up_basis: bfloat16 [8, 128, 262144], P(None, None, ('gy', 'gx')), may hold values from -0.25 to 0.25
- projection: bfloat16 [8, 256, 262144], P(None, None, ('gy', 'gx')), may hold values from -0.13258252 to 0.13258252, as said below
Outputs:
- solution: float32 [512, 262144], P(None, ('gy', 'gx'))
The draws below stay inside these ranges and needn't reach their ends.
Inputs may be any that keep to these rules, and one draw needn't show every extreme that they name: `projection`: rows of level h (counted from 1) have entries of order (2^h * 1024)^(-1/2).
All inputs are finite; a program needn't handle non-finite values.
Results may differ from the reference program's by a relative error of at most 0.0095.
Values sent between devices are 32-bit elements; how exact they have to be, the bound alone decides.
No kernel may reach another device: no remote copies, remote signals or barrier semaphores. Data moves between devices by JAX's collectives and lax.ppermute only.
A program may use at most 64 MiB of HBM per device.

```python
import jax
import jax.numpy as jnp
from jax import lax

LEAF = 1024
RANK = 128
RHS = 512
LEVELS = 8
POINTS = 262144


def draw_projection(key, part):
    heights = jnp.arange(1, LEVELS + 1).astype(jnp.float32)
    scales = 1.0 / jnp.sqrt(LEAF * 2.0 ** heights)
    values = jnp.clip(jax.random.normal(key, (LEVELS, 2 * RANK, POINTS), jnp.float32), -6.0, 6.0)
    return (values * scales[:, None, None]).astype(jnp.bfloat16)


def shard_levels(rng, shape, pieces, least, high):
    level, own = 1.0, jax.random.fold_in(rng, 6)
    for position, shards_of in pieces:
        draws = jnp.exp(jax.random.uniform(jax.random.fold_in(own, position), (shards_of,), jnp.float32, least / len(pieces), high / len(pieces)))
        level = level * jnp.repeat(draws, shape[position] // shards_of).reshape([-1 if axis == position else 1 for axis in range(len(shape))])
    return level


def gaussian(key, dims, deviation, limit, shards=(), dtype=jnp.bfloat16):
    factor_of = shard_levels(key, dims, shards, -0.22, 0.18) if shards else 1.0
    array = jax.random.normal(key, dims, jnp.float32) * deviation * factor_of
    return jnp.minimum(jnp.maximum(array, -limit), limit).astype(dtype)


def setup_inputs(seed: int = 0) -> dict:
    arg_keys = jax.random.split(jax.random.key(seed), 5)
    return {
        "rhs": gaussian(arg_keys[0], (RHS, POINTS), 1.0, 6.0, ((1, 256),)),
        "leaf_inverse": gaussian(arg_keys[1], (POINTS // LEAF, LEAF, LEAF), LEAF ** -0.5, 0.1875, ((0, 256),)),
        "up_basis": gaussian(arg_keys[2], (LEVELS, RANK, POINTS), (4 * RANK) ** -0.5, 0.25, ((2, 256),)),
        "projection": draw_projection(jax.random.fold_in(arg_keys[4], 71), 0),
    }


def leaf_apply(operands):
    return jnp.dot(operands[0], operands[1], preferred_element_type=jnp.float32)


def project_leaf(operands):
    return lax.dot_general(operands[0], operands[1], (((1,), (1,)), ((), ())), preferred_element_type=jnp.float32)


def reference(rhs, leaf_inverse, up_basis, projection):
    leaves = leaf_inverse.shape[0]
    blocks = rhs.reshape(RHS, leaves, LEAF).transpose(1, 0, 2)
    state = lax.map(leaf_apply, (blocks, leaf_inverse))
    for height in range(1, LEVELS + 1):
        rounded = state.astype(jnp.bfloat16)
        basis_rows = projection[height - 1].reshape(2 * RANK, leaves, LEAF).transpose(1, 0, 2)
        up_rows = up_basis[height - 1].reshape(RANK, leaves, LEAF).transpose(1, 0, 2)
        partial_value = lax.map(project_leaf, (rounded, basis_rows))
        groups = leaves // (2 ** height)
        node_total = partial_value.reshape(groups, 2 ** height, RHS, 2, RANK).sum(axis=1)
        node_total = jnp.moveaxis(node_total, 2, 1)
        half_count = 2 ** (height - 1)
        coefficient = jnp.broadcast_to(node_total[:, :, None], (groups, 2, half_count, RHS, RANK))
        coefficient = coefficient.reshape(leaves, RHS, RANK).astype(jnp.bfloat16)
        state = state - lax.map(leaf_apply, (coefficient, up_rows))
    return state.transpose(1, 0, 2).reshape(RHS, leaves * LEAF)
```

```python
import functools

import jax
import jax.numpy as jnp
from jax import lax
from jax.experimental import pallas as pl
from jax.experimental.pallas import tpu as pltpu
from jax.sharding import PartitionSpec as P

AXES = ("gy", "gx")
STEPS = 4
VMEM_BYTES = 32 * 1024 * 1024


def dot(a, b):
    return jnp.dot(a, b, preferred_element_type=jnp.float32)


def dot_t(a, b):
    return lax.dot_general(a, b, (((1,), (1,)), ((), ())), preferred_element_type=jnp.float32)


def exact_dot(a, b):
    return jnp.dot(a, b, precision=lax.Precision.HIGHEST, preferred_element_type=jnp.float32)


def swap(value, axis, mask, size):
    return lax.ppermute(value, axis, [(source, source ^ mask) for source in range(size)])


def exchange(value, groups):
    return lax.all_to_all(value, AXES, 0, 0, tiled=True, axis_index_groups=groups)


def half(value, which, rank):
    return lax.dynamic_slice_in_dim(value, which * rank, rank, value.ndim - 1)


def whole(shape):
    return pl.BlockSpec(shape, lambda j, bits: (0,) * len(shape))


def columns(rows, width):
    return pl.BlockSpec((rows, width), lambda j, bits: (0, j))


def level(index, rows, width):
    return pl.BlockSpec((None, rows, width), lambda j, bits: (index, 0, j))


def run(body, bits, args, in_specs, out_shape, out_specs, scratch, flops, nbytes):
    return pl.pallas_call(
        body,
        out_shape=out_shape,
        grid_spec=pltpu.PrefetchScalarGridSpec(
            num_scalar_prefetch=1,
            grid=(STEPS,),
            in_specs=in_specs,
            out_specs=out_specs,
            scratch_shapes=scratch,
        ),
        compiler_params=pltpu.CompilerParams(
            dimension_semantics=("arbitrary",), vmem_limit_bytes=VMEM_BYTES
        ),
        cost_estimate=pl.CostEstimate(flops=flops, bytes_accessed=nbytes, transcendentals=0),
    )(bits, *args)


def f32(*shape):
    return jax.ShapeDtypeStruct(shape, jnp.float32)


def accumulate(ref, value):
    @pl.when(pl.program_id(0) == 0)
    def _():
        ref[...] = value

    @pl.when(pl.program_id(0) > 0)
    def _():
        ref[...] += value


def gram_body(pairs, bits, *refs):
    ups, projs, outs = refs[: len(pairs)], refs[len(pairs) : 2 * len(pairs)], refs[2 * len(pairs) :]
    for up, proj, out in zip(ups, projs, outs, strict=True):
        accumulate(out, dot_t(up[...], proj[...]))


def grams(pairs, bits, up_basis, projection):
    rank, leaf = up_basis.shape[1:]
    width = leaf // STEPS
    count = len(pairs)
    return run(
        functools.partial(gram_body, pairs),
        bits,
        [up_basis] * count + [projection] * count,
        [level(k - 1, rank, width) for k, _ in pairs]
        + [level(h - 1, 2 * rank, width) for _, h in pairs],
        [f32(rank, 2 * rank)] * count,
        [whole((rank, 2 * rank))] * count,
        [],
        4 * count * rank * rank * leaf,
        6 * count * rank * leaf,
    )


def leaf_body(bits, rhs, inverse, own_rows, other_rows, state, own, other):
    block = dot(rhs[...], inverse[...])
    state[...] = block
    rounded = block.astype(jnp.bfloat16)
    accumulate(own, dot_t(rounded, own_rows[...]))
    accumulate(other, dot_t(rounded, other_rows[...]))


def leaf_solve(bits, rhs, leaf_inverse, projection):
    rows, leaf = rhs.shape
    rank = projection.shape[1] // 2
    width = leaf // STEPS
    return run(
        leaf_body,
        bits,
        [rhs, leaf_inverse, projection, projection],
        [
            whole((rows, leaf)),
            pl.BlockSpec((None, leaf, width), lambda j, bits: (0, 0, j)),
            pl.BlockSpec((None, rank, width), lambda j, bits: (0, bits[0], j)),
            pl.BlockSpec((None, rank, width), lambda j, bits: (0, 1 - bits[0], j)),
        ],
        [f32(rows, leaf), f32(rows, rank), f32(rows, rank)],
        [columns(rows, width), whole((rows, rank)), whole((rows, rank))],
        [],
        2 * rows * leaf * (leaf + 2 * rank),
        leaf * (6 * rows + 2 * leaf),
    )


def step_body(n_coef, n_up, n_proj, fill, emit, bits, state, *refs):
    coefs, refs = refs[:n_coef], refs[n_coef:]
    ups, refs = refs[:n_up], refs[n_up:]
    projs, refs = refs[:n_proj], refs[n_proj:]
    extra, outs, coef = refs[0], refs[1:-2], refs[-2]
    new_state, sums = outs[0], refs[-1]

    @pl.when(pl.program_id(0) == 0)
    def _():
        fill(bits, coef, *coefs)

    basis = jnp.concatenate([up[...] for up in ups], axis=0)
    block = state[...] - dot(coef[...], basis)
    new_state[...] = block
    if n_proj:
        rows = jnp.concatenate([proj[...] for proj in projs], axis=0)
        accumulate(sums, dot_t(block.astype(jnp.bfloat16), rows))

        @pl.when(pl.program_id(0) == STEPS - 1)
        def _():
            emit(bits, sums, extra, *outs[1:])


def step(bits, state, coefs, up_levels, proj_levels, up_basis, projection, extra, fill, emit, out_shape):
    rows, leaf = state.shape
    rank = up_basis.shape[1]
    width = leaf // STEPS
    depth, wide = rank * len(up_levels), 2 * rank * len(proj_levels)
    return run(
        functools.partial(step_body, len(coefs), len(up_levels), len(proj_levels), fill, emit),
        bits,
        [state, *coefs] + [up_basis] * len(up_levels) + [projection] * len(proj_levels) + [extra],
        [columns(rows, width)]
        + [whole(c.shape) for c in coefs]
        + [level(k - 1, rank, width) for k in up_levels]
        + [level(h - 1, 2 * rank, width) for h in proj_levels]
        + [whole(extra.shape)],
        [f32(rows, leaf), *out_shape],
        [columns(rows, width)] + [whole(s.shape) for s in out_shape],
        [
            pltpu.VMEM((rows, depth), jnp.bfloat16),
            pltpu.VMEM((rows, wide) if wide else (8, 128), jnp.float32),
        ],
        2 * rows * leaf * (depth + wide),
        leaf * (8 * rows + 2 * depth + 2 * wide),
    )


def fill_sum(bits, coef, mine, received):
    coef[...] = (mine[...] + received[...]).astype(jnp.bfloat16)


def fill_pair(bits, coef, mine, received):
    count = mine.shape[0]
    coef[pl.ds(pl.multiple_of(bits[0] * count, count), count)] = mine[...].astype(jnp.bfloat16)
    coef[pl.ds(pl.multiple_of((1 - bits[0]) * count, count), count)] = received[...].astype(jnp.bfloat16)


def fill_row(count, bits, coef, packed):
    coef[...] = packed[:, :count, :].reshape(coef.shape).astype(jnp.bfloat16)


def fill_top(bits, coef, mine, received):
    count = mine.shape[0]
    rank = received.shape[1] // 3
    depth = coef.shape[1]
    coef[pl.ds(pl.multiple_of(bits[1] * count, count), count), :] = mine[:, :depth].astype(jnp.bfloat16)
    there = pl.ds(pl.multiple_of((1 - bits[1]) * count, count), count)
    coef[there, :rank] = received[:, 2 * rank :].astype(jnp.bfloat16)
    coef[there, rank:] = received[:, : 2 * rank].astype(jnp.bfloat16)


def emit_halves(which, bits, sums, extra, keep, send):
    count = keep.shape[0]
    keep[...] = sums[pl.ds(pl.multiple_of(bits[which] * count, count), count)]
    send[...] = sums[pl.ds(pl.multiple_of((1 - bits[which]) * count, count), count)]


def emit_rows(bits, sums, extra, packed):
    parts, _, wide = packed.shape
    count = sums.shape[0] // parts
    packed[:, :count, :] = sums[:, :wide].reshape(parts, count, wide)
    packed[:, count : 2 * count, :] = sums[:, wide:].reshape(parts, count, wide)
    pieces = extra.shape[1] // parts
    for i in range(extra.shape[0]):
        start = 2 * count + i * pieces
        packed[:, start : start + pieces, :] = extra[i].reshape(parts, pieces, wide)


def shards(groups_z, groups_zy, rhs, leaf_inverse, up_basis, projection):
    size_x, size_y = lax.axis_size("gx"), lax.axis_size("gy")
    rows, leaf = rhs.shape
    rank = up_basis.shape[1]
    wide = 2 * rank
    gx, gy = lax.axis_index("gx"), lax.axis_index("gy")
    z0, z1, z2, y0, y1 = (gx >> i & 1 for i in range(5))
    core, x0, x1 = (gy >> i & 1 for i in range(3))
    bits = jnp.stack([z0, core])
    over_x = functools.partial(swap, axis="gx", size=size_x)
    over_y = functools.partial(swap, axis="gy", size=size_y)
    nothing = jnp.zeros((8, 128), jnp.float32)

    low = jnp.concatenate(grams(((2, 3), (4, 5)), bits, up_basis, projection), axis=0)
    low = low + over_x(low, mask=1)
    gram_23 = low[:rank].astype(jnp.bfloat16)
    gram_45 = low[rank:]
    gram_45 = gram_45 + over_x(gram_45, mask=2)
    gram_45 = gram_45 + over_x(gram_45, mask=6)
    gram_45 = gram_45.astype(jnp.bfloat16)

    state, own, other = leaf_solve(bits, rhs, leaf_inverse, projection)
    received = over_x(other, mask=1)
    high = jnp.stack(grams(((6, 7), (6, 8), (7, 8)), bits, up_basis, projection))

    pair_rows = rows // 2
    state, keep, send = step(
        bits, state, [own, received], (1,), (2, 3), up_basis, projection, nothing,
        fill_sum, functools.partial(emit_halves, 0), [f32(pair_rows, 2 * wide)] * 2,
    )
    value = keep + over_x(send, mask=1)
    c2 = half(value[:, :wide], z1, rank) + over_x(half(value[:, :wide], 1 - z1, rank), mask=2)
    value = value[:, wide:] - dot(c2.astype(jnp.bfloat16), gram_23)
    c3 = half(value, z2, rank) + over_x(half(value, 1 - z2, rank), mask=6)
    c3 = c3 + over_x(c3, mask=2)
    mine = jnp.concatenate([c2, c3], axis=1)
    received = over_x(mine, mask=1)

    ring = len(groups_z[0])
    count, pieces = rows // ring, rank // ring
    state, packed = step(
        bits, state, [mine, received], (2, 3), (4, 5), up_basis, projection, high,
        fill_pair, emit_rows, [f32(ring, 2 * count + 3 * pieces, wide)],
    )
    value = exchange(packed, groups_z).sum(axis=0)
    high = value[2 * count :]
    high = high + over_x(high, mask=8)
    high = high + over_x(high, mask=24)
    c4 = half(value[:count], y0, rank) + over_x(half(value[:count], 1 - y0, rank), mask=8)
    value = value[count : 2 * count] - dot(c4.astype(jnp.bfloat16), gram_45)
    c5 = half(value, y1, rank) + over_x(half(value, 1 - y1, rank), mask=24)
    c5 = c5 + over_x(c5, mask=8)
    packed = jnp.concatenate([jnp.concatenate([c4, c5], axis=1), high], axis=0)
    packed = exchange(jnp.broadcast_to(packed, (ring, *packed.shape)), groups_z)
    high = packed[:, count:].reshape(ring, 3, pieces, wide).transpose(1, 0, 2, 3).reshape(3, rank, wide)
    high_there = over_y(high, mask=1)

    half_rows = rows // 2
    state, keep, send = step(
        bits, state, [packed], (4, 5), (6, 7, 8), up_basis, projection, nothing,
        functools.partial(fill_row, count), functools.partial(emit_halves, 1), [f32(half_rows, 3 * wide)] * 2,
    )
    value = keep + over_y(send, mask=1)
    share = half_rows // size_x
    value = exchange(value.reshape(size_x, share, 3 * wide), groups_zy).sum(axis=0)
    c6, c6_there = half(value[:, :wide], core, rank), half(value[:, :wide], 1 - core, rank)
    z7 = value[:, wide : 2 * wide] - exact_dot(c6, high[0]) - exact_dot(c6_there, high_there[0])
    z8 = value[:, 2 * wide :] - exact_dot(c6, high[1]) - exact_dot(c6_there, high_there[1])
    c7 = half(z7, x0, rank) + over_y(half(z7, 1 - x0, rank), mask=2)
    z8 = z8 - exact_dot(c7, high[2] + high_there[2])
    c8 = half(z8, x1, rank) + over_y(half(z8, 1 - x1, rank), mask=6)
    c8 = c8 + over_y(c8, mask=2)
    packed = jnp.concatenate([c6, c7, c8, c6_there], axis=1)
    packed = exchange(jnp.broadcast_to(packed, (size_x, *packed.shape)), groups_zy)
    packed = packed.reshape(half_rows, 4 * rank)
    received = over_y(packed[:, rank:], mask=1)
    return step(
        bits, state, [packed, received], (6, 7, 8), (), up_basis, projection, nothing,
        fill_top, None, [],
    )[0]


def solution(mesh):
    size_x, size_y = mesh.shape["gx"], mesh.shape["gy"]
    ring = 8
    groups_z = [
        [gy * size_x + start + i for i in range(ring)]
        for gy in range(size_y)
        for start in range(0, size_x, ring)
    ]
    groups_zy = [[gy * size_x + i for i in range(size_x)] for gy in range(size_y)]
    return jax.shard_map(
        functools.partial(shards, groups_z, groups_zy),
        mesh=mesh,
        in_specs=(
            P(None, ("gy", "gx")),
            P(("gy", "gx"), None, None),
            P(None, None, ("gy", "gx")),
            P(None, None, ("gy", "gx")),
        ),
        out_specs=P(None, ("gy", "gx")),
        check_vma=False,
    )
```

```python
import functools

import jax
import jax.numpy as jnp
from jax import lax
from jax.experimental import pallas as pl
from jax.experimental.pallas import tpu as pltpu
from jax.sharding import PartitionSpec as P

AXES = ("gy", "gx")
STEPS = 4
VMEM_BYTES = 58 * 1024 * 1024


def dot(a, b):
    return jnp.dot(a, b, preferred_element_type=jnp.float32)


def dot_t(a, b):
    return lax.dot_general(a, b, (((1,), (1,)), ((), ())), preferred_element_type=jnp.float32)


def exact_dot(a, b):
    return jnp.dot(a, b, precision=lax.Precision.HIGHEST, preferred_element_type=jnp.float32)


def swap(value, axis, mask, size):
    return lax.ppermute(value, axis, [(source, source ^ mask) for source in range(size)])


def exchange(value, groups):
    return lax.all_to_all(value, AXES, 0, 0, tiled=True, axis_index_groups=groups)


def half(value, which, rank):
    return lax.dynamic_slice_in_dim(value, which * rank, rank, value.ndim - 1)


def split(value, bit):
    count = value.shape[0] // 2
    mine = lax.dynamic_slice_in_dim(value, bit * count, count, 0)
    return mine, lax.dynamic_slice_in_dim(value, (1 - bit) * count, count, 0)


def join(mine, other, bit):
    return jnp.where(bit == 0, jnp.concatenate([mine, other]), jnp.concatenate([other, mine]))


def hbm(value):
    return pltpu.with_memory_space_constraint(value, pltpu.HBM)


def whole(shape):
    return pl.BlockSpec(shape, lambda j, bits: (0,) * len(shape))


def block(shape, *index):
    return pl.BlockSpec(shape, lambda j, bits: index)


def columns(rows, width):
    return pl.BlockSpec((rows, width), lambda j, bits: (0, j))


def run(body, steps, bits, args, in_specs, out_shape, out_specs, scratch, flops, nbytes):
    return pl.pallas_call(
        body,
        out_shape=out_shape,
        grid_spec=pltpu.PrefetchScalarGridSpec(
            num_scalar_prefetch=1,
            grid=(steps,),
            in_specs=in_specs,
            out_specs=out_specs,
            scratch_shapes=scratch,
        ),
        compiler_params=pltpu.CompilerParams(
            dimension_semantics=("arbitrary",), vmem_limit_bytes=VMEM_BYTES
        ),
        cost_estimate=pl.CostEstimate(flops=flops, bytes_accessed=nbytes, transcendentals=0),
    )(bits, *args)


def f32(*shape):
    return jax.ShapeDtypeStruct(shape, jnp.float32)


def bf16(*shape):
    return jax.ShapeDtypeStruct(shape, jnp.bfloat16)


def leaf_body(bits, rhs, inverse, own_rows, other_rows, state, own, other, sums):
    rank = own.shape[1]
    rounded = dot(rhs[...], inverse[...]).astype(jnp.bfloat16)
    state[...] = rounded
    part = dot_t(rounded, jnp.concatenate([own_rows[...], other_rows[...]], axis=0))

    @pl.when(pl.program_id(0) == 0)
    def _():
        sums[...] = part

    @pl.when(pl.program_id(0) > 0)
    def _():
        sums[...] += part

    @pl.when(pl.program_id(0) == STEPS - 1)
    def _():
        own[...] = sums[:, :rank]
        other[...] = sums[:, rank:]


def leaf_solve(bits, rhs, leaf_inverse, projection):
    rows, leaf = rhs.shape
    rank = projection.shape[1] // 2
    width = leaf // STEPS
    return run(
        leaf_body,
        STEPS,
        bits,
        [hbm(rhs), hbm(leaf_inverse), hbm(projection), hbm(projection)],
        [
            whole((rows, leaf)),
            pl.BlockSpec((None, leaf, width), lambda j, bits: (0, 0, j)),
            pl.BlockSpec((None, rank, width), lambda j, bits: (0, bits[0], j)),
            pl.BlockSpec((None, rank, width), lambda j, bits: (0, 1 - bits[0], j)),
        ],
        [bf16(rows, leaf), f32(rows, rank), f32(rows, rank)],
        [columns(rows, width), whole((rows, rank)), whole((rows, rank))],
        [pltpu.VMEM((rows, 2 * rank), jnp.float32)],
        2 * rows * leaf * (leaf + 2 * rank),
        leaf * (4 * rows + 2 * leaf),
    )


PAIRS = ((2, 3), (4, 5), (6, 7), (6, 8), (7, 8))


def project_body(levels, bits, state, up, proj, value, gram, kept):
    rank = up.shape[1]
    value[...] = dot_t(state[...], proj[...])
    for h in range(2, levels + 1):

        @pl.when(pl.program_id(0) == h - 2)
        def _(h=h):
            depth = (h - 1) * rank
            full = dot_t(up[: h - 1].reshape(depth, up.shape[2]), proj[...])
            gram[:depth, :] = full.astype(jnp.bfloat16)
            for i, (k, of) in enumerate(PAIRS):
                if of == h:
                    kept[i] = full[(k - 1) * rank : k * rank]


def project(bits, state, up_basis, projection):
    rows, leaf = state.shape
    levels, rank = up_basis.shape[:2]
    wide, count = 2 * rank, levels - 1
    return run(
        functools.partial(project_body, levels),
        count,
        bits,
        [state, up_basis, projection],
        [
            whole((rows, leaf)),
            whole((count, rank, leaf)),
            pl.BlockSpec((None, wide, leaf), lambda j, bits: (j + 1, 0, 0)),
        ],
        [f32(count, rows, wide), bf16(count, count * rank, wide), f32(len(PAIRS), rank, wide)],
        [
            pl.BlockSpec((None, rows, wide), lambda j, bits: (j, 0, 0)),
            pl.BlockSpec((None, count * rank, wide), lambda j, bits: (j, 0, 0)),
            whole((len(PAIRS), rank, wide)),
        ],
        [],
        2 * leaf * wide * (count * rows + rank * count * (count + 1) // 2),
        2 * leaf * (rows + count * 3 * rank),
    )


def emit_halves(which, parts, keep, send):
    count, wide = keep.shape[0], parts[0].shape[1]
    for bit in range(2):

        @pl.when(which == bit)
        def _(bit=bit):
            for i, part in enumerate(parts):
                keep[:, i * wide : (i + 1) * wide] = part[bit * count : (bit + 1) * count]
                send[:, i * wide : (i + 1) * wide] = part[(1 - bit) * count : (2 - bit) * count]


def second_body(bits, mine, received, value, gram, keep, send, coef):
    c1 = (mine[...] + received[...]).astype(jnp.bfloat16)
    coef[...] = c1
    emit_halves(bits[0], [value[i] - dot(c1, gram[i]) for i in range(2)], keep, send)


def second(bits, mine, received, value, gram):
    rows, rank = mine.shape
    wide = 2 * rank
    return run(
        second_body,
        1,
        bits,
        [mine, received, value, gram],
        [whole(mine.shape)] * 2 + [block((2, rows, wide), 0, 0, 0), block((2, rank, wide), 0, 0, 0)],
        [f32(rows // 2, 2 * wide)] * 2 + [bf16(rows, rank)],
        [whole((rows // 2, 2 * wide))] * 2 + [whole((rows, rank))],
        [],
        4 * rows * rank * wide,
        16 * rows * wide,
    )


def fourth_body(bits, c1, mine, received, value, gram, low, high, packed, coef):
    count, rank = mine.shape[0], c1.shape[1]
    for bit in range(2):

        @pl.when(bits[0] == bit)
        def _(bit=bit):
            coef[bit * count : (bit + 1) * count] = mine[...].astype(jnp.bfloat16)
            coef[(1 - bit) * count : (2 - bit) * count] = received[...].astype(jnp.bfloat16)

    parts, total, _ = packed.shape
    share = value.shape[1] // parts
    lhs = jnp.concatenate([c1[...], coef[...]], axis=1)
    for i in range(2):
        left = value[i] - dot(lhs, gram[i])
        for j in range(2):
            start = (2 * i + j) * share
            packed[:, start : start + share, :] = left[:, j * rank : (j + 1) * rank].reshape(parts, share, rank)
    start = 4 * share
    for j in range(2):
        packed[:, start : start + low.shape[0], :] = jnp.broadcast_to(
            low[:, j * rank : (j + 1) * rank], (parts, low.shape[0], rank)
        )
        start += low.shape[0]
    packed[:, start:total, :] = high[...].reshape(parts, total - start, rank)


def fourth(bits, c1, mine, received, value, gram, low, high, parts):
    rows, rank = c1.shape
    wide = 2 * rank
    total = 4 * rows // parts + 2 * low.shape[0] + high.shape[0] // parts
    return run(
        fourth_body,
        1,
        bits,
        [c1, mine, received, value, gram, low, high],
        [whole(c1.shape), whole(mine.shape), whole(received.shape)]
        + [block((2, rows, wide), 1, 0, 0), block((2, 3 * rank, wide), 1, 0, 0)]
        + [whole(low.shape), whole(high.shape)],
        [f32(parts, total, rank), bf16(rows, wide)],
        [whole((parts, total, rank)), whole((rows, wide))],
        [],
        12 * rows * rank * wide,
        16 * rows * wide,
    )


def gather_body(places, bits, packed, own, other, fifth, gram, high):
    parts, total, rank = packed.shape
    share, piece = own.shape[0], gram.shape[0] // parts
    for ref, bit in ((own, 0), (other, 1)):
        for b in range(2):

            @pl.when(bits[2] == b)
            def _(ref=ref, start=(bit ^ b) * share):
                ref[...] = packed[:, start : start + share, :].sum(axis=0)

    for j in range(2):
        start = (2 + j) * share
        fifth[:, j * rank : (j + 1) * rank] = packed[:, start : start + share, :].sum(axis=0)
    for i, place in enumerate(places):
        for j in range(2):
            start = 4 * share + j * piece
            gram[place * piece : (place + 1) * piece, j * rank : (j + 1) * rank] = packed[i, start : start + piece, :]
    high[...] = packed[:, 4 * share + 2 * piece :, :].sum(axis=0)


def gather_rows(bits, packed, places, share):
    parts, total, rank = packed.shape
    rest = total - 4 * share - 2 * rank // parts
    shapes = [(share, rank), (share, rank), (share, 2 * rank), (rank, 2 * rank), (rest, rank)]
    return run(
        functools.partial(gather_body, places),
        1,
        bits,
        [packed],
        [whole(packed.shape)],
        [f32(*s) for s in shapes],
        [whole(s) for s in shapes],
        [],
        parts * total * rank,
        4 * parts * total * rank,
    )


def sixth_body(bits, c1, c23, packed, value, gram, keep, send, coef):
    rank = c1.shape[1]
    share = c1.shape[0] // packed.shape[0]
    for j in range(2):
        coef[:, j * rank : (j + 1) * rank] = (
            packed[:, j * share : (j + 1) * share, :].reshape(c1.shape).astype(jnp.bfloat16)
        )
    lhs = jnp.concatenate([c1[...], c23[...], coef[...]], axis=1)
    emit_halves(bits[1], [value[i] - dot(lhs, gram[i, : lhs.shape[1], :]) for i in range(3)], keep, send)


def sixth(bits, c1, c23, packed, value, gram):
    rows, rank = c1.shape
    wide = 2 * rank
    value, gram = value[4:], gram[4:]
    return run(
        sixth_body,
        1,
        bits,
        [c1, c23, packed, value, gram],
        [whole(c1.shape), whole(c23.shape), whole(packed.shape), whole(value.shape), whole(gram.shape)],
        [f32(rows // 2, 3 * wide)] * 2 + [bf16(rows, wide)],
        [whole((rows // 2, 3 * wide))] * 2 + [whole((rows, wide))],
        [],
        30 * rows * rank * wide,
        24 * rows * wide,
    )


def last_body(bits, state, c1, c23, c45, mine, received, up, out, coef):
    rank, count = c1.shape[1], mine.shape[0]

    @pl.when(pl.program_id(0) == 0)
    def _():
        coef[:, :rank] = c1[...]
        coef[:, rank : 3 * rank] = c23[...]
        coef[:, 3 * rank : 5 * rank] = c45[...]
        for bit in range(2):

            @pl.when(bits[1] == bit)
            def _(bit=bit):
                here = slice(bit * count, (bit + 1) * count)
                there = slice((1 - bit) * count, (2 - bit) * count)
                coef[here, 5 * rank :] = mine[:, : 3 * rank].astype(jnp.bfloat16)
                coef[there, 5 * rank : 6 * rank] = received[:, 2 * rank :].astype(jnp.bfloat16)
                coef[there, 6 * rank :] = received[:, : 2 * rank].astype(jnp.bfloat16)

    basis = up[...].reshape(coef.shape[1], up.shape[2])
    out[...] = state[...].astype(jnp.float32) - dot(coef[...], basis)


def last(bits, state, c1, c23, c45, mine, received, up_basis):
    rows, leaf = state.shape
    levels, rank = up_basis.shape[:2]
    width = leaf // STEPS
    coefs = [c1, c23, c45, mine, received]
    return run(
        last_body,
        STEPS,
        bits,
        [state, *coefs, up_basis],
        [columns(rows, width)]
        + [whole(c.shape) for c in coefs]
        + [pl.BlockSpec((levels, rank, width), lambda j, bits: (0, 0, j))],
        f32(rows, leaf),
        columns(rows, width),
        [pltpu.VMEM((rows, levels * rank), jnp.bfloat16)],
        2 * rows * leaf * levels * rank,
        6 * rows * leaf + 2 * leaf * levels * rank,
    )


def shards(groups_z, groups_zy, rhs, leaf_inverse, up_basis, projection):
    size_x, size_y = lax.axis_size("gx"), lax.axis_size("gy")
    rows = rhs.shape[0]
    rank = up_basis.shape[1]
    wide = 2 * rank
    gx, gy = lax.axis_index("gx"), lax.axis_index("gy")
    z0, z1, z2, y0, y1 = (gx >> i & 1 for i in range(5))
    core, x0, x1 = (gy >> i & 1 for i in range(3))
    bits = jnp.stack([z0, core, y0])
    over_x = functools.partial(swap, axis="gx", size=size_x)
    over_y = functools.partial(swap, axis="gy", size=size_y)
    ring = len(groups_z[0])
    share = rows // ring

    state, own, other = leaf_solve(bits, rhs, leaf_inverse, projection)
    received = over_x(other, mask=1)
    value, gram, kept = project(bits, state, up_basis, projection)

    keep, send, c1 = second(bits, own, received, value, gram)
    received = over_x(send, mask=1)
    low, low_send = split(kept[1], z0)
    both = over_x(jnp.concatenate([kept[0], low_send]), mask=1)
    gram_23 = (kept[0] + both[:rank]).astype(jnp.bfloat16)
    low, low_send = split(low + both[rank:], z1 ^ z2)
    low, low_send = split(low + over_x(low_send, mask=2), z2)
    low = low + over_x(low_send, mask=6)
    places = [(i & 1) * 4 + (i >> 1 & 1 ^ i >> 2) * 2 + (i >> 2) for i in range(ring)]
    high, high_send = split(kept[2:].reshape(3 * rank, wide), y0 ^ y1)
    high, high_send = split(high + over_x(high_send, mask=8), y1)
    high = high + over_x(high_send, mask=24)
    high = jnp.concatenate([high[:, :rank], high[:, rank:]])

    left = keep + received
    c2 = half(left[:, :wide], z1, rank) + over_x(half(left[:, :wide], 1 - z1, rank), mask=2)
    left = left[:, wide:] - dot(c2.astype(jnp.bfloat16), gram_23)
    c3 = half(left, z2, rank) + over_x(half(left, 1 - z2, rank), mask=6)
    c3 = c3 + over_x(c3, mask=2)
    mine = jnp.concatenate([c2, c3], axis=1)
    received = over_x(mine, mask=1)

    packed, c23 = fourth(bits, c1, mine, received, value, gram, low, high, ring)
    packed = exchange(packed, groups_z)
    own, other, left, gram_45, high = gather_rows(bits, packed, places, share)
    c4 = own + over_x(other, mask=8)
    left = left - dot(c4, gram_45)
    c5 = half(left, y1, rank) + over_x(half(left, 1 - y1, rank), mask=24)
    c5 = c5 + over_x(c5, mask=8)
    packed = jnp.concatenate([c4, c5, high], axis=0)
    packed = exchange(jnp.broadcast_to(packed, (ring, *packed.shape)), groups_z)

    keep, send, c45 = sixth(bits, c1, c23, packed, value, gram)
    left = keep + over_y(send, mask=1)
    high = packed[:, 2 * share :].reshape(2, 3 * wide // ring, rank)
    high = jnp.concatenate([high[0], high[1]], axis=1)
    high = join(high, over_x(high, mask=24), y1)
    high = join(high, over_x(high, mask=8), y0 ^ y1)
    high_there = over_y(high, mask=1)
    left, high, high_there = lax.optimization_barrier((left, high, high_there))
    half_rows = rows // 2
    count = half_rows // size_x
    left = exchange(left.reshape(size_x, count, 3 * wide), groups_zy).sum(axis=0)
    high, high_there = high.reshape(3, rank, wide), high_there.reshape(3, rank, wide)
    c6, c6_there = half(left[:, :wide], core, rank), half(left[:, :wide], 1 - core, rank)
    z7 = left[:, wide : 2 * wide] - exact_dot(c6, high[0]) - exact_dot(c6_there, high_there[0])
    z8 = left[:, 2 * wide :] - exact_dot(c6, high[1]) - exact_dot(c6_there, high_there[1])
    c7 = half(z7, x0, rank) + over_y(half(z7, 1 - x0, rank), mask=2)
    z8 = z8 - exact_dot(c7, high[2] + high_there[2])
    c8 = half(z8, x1, rank) + over_y(half(z8, 1 - x1, rank), mask=6)
    c8 = c8 + over_y(c8, mask=2)
    packed = jnp.concatenate([c6, c7, c8, c6_there], axis=1)
    packed = exchange(jnp.broadcast_to(packed, (size_x, *packed.shape)), groups_zy)
    packed = packed.reshape(half_rows, 4 * rank)
    received = over_y(packed[:, rank:], mask=1)
    return last(bits, state, c1, c23, c45, packed, received, up_basis)


def solution(mesh):
    size_x, size_y = mesh.shape["gx"], mesh.shape["gy"]
    ring = 8
    groups_z = [
        [gy * size_x + start + i for i in range(ring)]
        for gy in range(size_y)
        for start in range(0, size_x, ring)
    ]
    groups_zy = [[gy * size_x + i for i in range(size_x)] for gy in range(size_y)]
    return jax.shard_map(
        functools.partial(shards, groups_z, groups_zy),
        mesh=mesh,
        in_specs=(
            P(None, ("gy", "gx")),
            P(("gy", "gx"), None, None),
            P(None, None, ("gy", "gx")),
            P(None, None, ("gy", "gx")),
        ),
        out_specs=P(None, ("gy", "gx")),
        check_vma=False,
    )
```

```python
import functools

import jax
import jax.numpy as jnp
from jax import lax
from jax.experimental import pallas as pl
from jax.experimental.pallas import tpu as pltpu
from jax.sharding import PartitionSpec as P

AXES = ("gy", "gx")
STEPS = 4
VMEM_BYTES = 16 * 1024 * 1024


def dot(a, b):
    return jnp.dot(a, b, preferred_element_type=jnp.float32)


def dot_t(a, b):
    return lax.dot_general(a, b, (((1,), (1,)), ((), ())), preferred_element_type=jnp.float32)


def exact_dot(a, b):
    return jnp.dot(a, b, precision=lax.Precision.HIGHEST, preferred_element_type=jnp.float32)


def swap(value, axis, mask, size):
    return lax.ppermute(value, axis, [(source, source ^ mask) for source in range(size)])


def exchange(value, groups):
    return lax.all_to_all(value, AXES, 0, 0, tiled=True, axis_index_groups=groups)


def half(value, start):
    return lax.dynamic_slice_in_dim(value, start, value.shape[-1] // 2, value.ndim - 1)


def split(value, starts):
    count = value.shape[0] // 2
    return tuple(lax.dynamic_slice_in_dim(value, start, count, 0) for start in starts)


def join(mine, other, first):
    return jnp.where(first, jnp.concatenate([mine, other]), jnp.concatenate([other, mine]))


def starts(bit, count):
    return (bit * count).astype(jnp.uint32), ((1 - bit) * count).astype(jnp.uint32)


def hbm(value):
    return pltpu.with_memory_space_constraint(value, pltpu.HBM)


def whole(shape):
    return pl.BlockSpec(shape, lambda j, bits: (0,) * len(shape))


def block(shape, *index):
    return pl.BlockSpec(shape, lambda j, bits: index)


def columns(rows, width):
    return pl.BlockSpec((rows, width), lambda j, bits: (0, j))


def run(body, steps, bits, args, in_specs, out_shape, out_specs, scratch, flops, nbytes):
    return pl.pallas_call(
        body,
        out_shape=out_shape,
        grid_spec=pltpu.PrefetchScalarGridSpec(
            num_scalar_prefetch=1,
            grid=(steps,),
            in_specs=in_specs,
            out_specs=out_specs,
            scratch_shapes=scratch,
        ),
        compiler_params=pltpu.CompilerParams(
            dimension_semantics=("arbitrary",), vmem_limit_bytes=VMEM_BYTES
        ),
        cost_estimate=pl.CostEstimate(flops=flops, bytes_accessed=nbytes, transcendentals=0),
    )(bits, *args)


def f32(*shape):
    return jax.ShapeDtypeStruct(shape, jnp.float32)


def bf16(*shape):
    return jax.ShapeDtypeStruct(shape, jnp.bfloat16)


def vmem(*shape, dtype=jnp.float32):
    return pltpu.VMEM(shape, dtype)


def local(body, bits, args, outs, flops, nbytes):
    args = [pltpu.with_memory_space_constraint(a, pltpu.VMEM) for a in args]
    return pl.pallas_call(
        body,
        out_shape=outs,
        in_specs=[pl.BlockSpec(memory_space=pltpu.SMEM)]
        + [pl.BlockSpec(memory_space=pltpu.VMEM)] * len(args),
        out_specs=[pl.BlockSpec(memory_space=pltpu.VMEM)] * len(outs),
        compiler_params=pltpu.CompilerParams(vmem_limit_bytes=VMEM_BYTES),
        cost_estimate=pl.CostEstimate(flops=flops, bytes_accessed=nbytes, transcendentals=0),
    )(bits, *args)


def leaf_body(bits, rhs, inverse, own_rows, other_rows, state, own, other, sums):
    rank = own.shape[1]
    rounded = dot(rhs[...], inverse[...]).astype(jnp.bfloat16)
    state[...] = rounded
    part = dot_t(rounded, jnp.concatenate([own_rows[...], other_rows[...]], axis=0))

    @pl.when(pl.program_id(0) == 0)
    def _():
        sums[...] = part

    @pl.when(pl.program_id(0) > 0)
    def _():
        sums[...] += part

    @pl.when(pl.program_id(0) == STEPS - 1)
    def _():
        own[...] = sums[:, :rank]
        other[...] = sums[:, rank:]


def leaf_solve(bits, rhs, leaf_inverse, projection):
    rows, leaf = rhs.shape
    rank = projection.shape[1] // 2
    width = leaf // STEPS
    return run(
        leaf_body,
        STEPS,
        bits,
        [hbm(rhs), hbm(leaf_inverse), hbm(projection), hbm(projection)],
        [
            whole((rows, leaf)),
            pl.BlockSpec((None, leaf, width), lambda j, bits: (0, 0, j)),
            pl.BlockSpec((None, rank, width), lambda j, bits: (0, bits[0], j)),
            pl.BlockSpec((None, rank, width), lambda j, bits: (0, 1 - bits[0], j)),
        ],
        [vmem(rows, leaf, dtype=jnp.bfloat16), vmem(rows, rank), vmem(rows, rank)],
        [columns(rows, width), whole((rows, rank)), whole((rows, rank))],
        [pltpu.VMEM((rows, 2 * rank), jnp.float32)],
        2 * rows * leaf * (leaf + 2 * rank),
        leaf * (4 * rows + 2 * leaf),
    )


def project_body(heights, depth, pairs, bits, state, up, proj, value, gram, *kept):
    rank = up.shape[1]
    for i, h in enumerate(heights):
        rows = proj[h - 1]
        value[i] = dot_t(state[...], rows)
        gram[i] = dot_t(up[:depth].reshape(depth * rank, up.shape[2]), rows).astype(jnp.bfloat16)
        for j, (k, of) in enumerate(pairs):
            if of == h:
                kept[0][j] = dot_t(up[k - 1], rows)


def project(heights, pairs, bits, state, up_basis, projection):
    rows, leaf = state.shape
    rank = up_basis.shape[1]
    wide, count, depth = 2 * rank, len(heights), heights[0] - 1
    return local(
        functools.partial(project_body, heights, depth, pairs),
        bits,
        [state, up_basis, projection],
        [vmem(count, rows, wide), vmem(count, depth * rank, wide, dtype=jnp.bfloat16)]
        + ([vmem(len(pairs), rank, wide)] if pairs else []),
        2 * leaf * wide * (count * (rows + rank * depth) + rank * len(pairs)),
        2 * leaf * (rows + count * 3 * rank),
    )


def emit_halves(which, parts, keep, send):
    count, wide = keep.shape[0], parts[0].shape[1]
    for bit in range(2):

        @pl.when(which == bit)
        def _(bit=bit):
            for i, part in enumerate(parts):
                keep[:, i * wide : (i + 1) * wide] = part[bit * count : (bit + 1) * count]
                send[:, i * wide : (i + 1) * wide] = part[(1 - bit) * count : (2 - bit) * count]


def second_body(bits, mine, received, value, gram, keep, send, coef):
    c1 = (mine[...] + received[...]).astype(jnp.bfloat16)
    coef[...] = c1
    emit_halves(bits[0], [value[i] - dot(c1, gram[i]) for i in range(2)], keep, send)


def second(bits, mine, received, value, gram):
    rows, rank = mine.shape
    wide = 2 * rank
    return local(
        second_body,
        bits,
        [mine, received, value, gram],
        [vmem(rows // 2, 2 * wide)] * 2 + [vmem(rows, rank, dtype=jnp.bfloat16)],
        4 * rows * rank * wide,
        16 * rows * wide,
    )


def fourth_body(bits, c1, mine, received, value, gram, low, high, packed, coef):
    count, rank = mine.shape[0], c1.shape[1]
    for bit in range(2):

        @pl.when(bits[0] == bit)
        def _(bit=bit):
            coef[bit * count : (bit + 1) * count] = mine[...].astype(jnp.bfloat16)
            coef[(1 - bit) * count : (2 - bit) * count] = received[...].astype(jnp.bfloat16)

    parts, total, _ = packed.shape
    share = value.shape[1] // parts
    lhs = jnp.concatenate([c1[...], coef[...]], axis=1)
    for i in range(2):
        left = value[i] - dot(lhs, gram[i])
        for j in range(2):
            start = (2 * i + j) * share
            packed[:, start : start + share, :] = left[:, j * rank : (j + 1) * rank].reshape(parts, share, rank)
    start = 4 * share
    for j in range(2):
        packed[:, start : start + low.shape[0], :] = jnp.broadcast_to(
            low[:, j * rank : (j + 1) * rank], (parts, low.shape[0], rank)
        )
        start += low.shape[0]
    packed[:, start:total, :] = high[...].reshape(parts, total - start, rank)


def fourth(bits, c1, mine, received, value, gram, low, high, parts):
    rows, rank = c1.shape
    wide = 2 * rank
    total = 4 * rows // parts + 2 * low.shape[0] + high.shape[0] // parts
    return local(
        fourth_body,
        bits,
        [c1, mine, received, value, gram, low, high],
        [vmem(parts, total, rank), vmem(rows, wide, dtype=jnp.bfloat16)],
        12 * rows * rank * wide,
        16 * rows * wide,
    )


def gather_body(places, bits, packed, own, other, fifth, gram, high):
    parts, total, rank = packed.shape
    share, piece = own.shape[0], gram.shape[0] // parts
    for ref, bit in ((own, 0), (other, 1)):
        for b in range(2):

            @pl.when(bits[2] == b)
            def _(ref=ref, start=(bit ^ b) * share):
                ref[...] = packed[:, start : start + share, :].sum(axis=0)

    for j in range(2):
        start = (2 + j) * share
        fifth[:, j * rank : (j + 1) * rank] = packed[:, start : start + share, :].sum(axis=0)
    for i, place in enumerate(places):
        for j in range(2):
            start = 4 * share + j * piece
            gram[place * piece : (place + 1) * piece, j * rank : (j + 1) * rank] = packed[i, start : start + piece, :]
    high[...] = packed[:, 4 * share + 2 * piece :, :].sum(axis=0)


def gather_rows(bits, packed, places, share):
    parts, total, rank = packed.shape
    rest = total - 4 * share - 2 * rank // parts
    shapes = [(share, rank), (share, rank), (share, 2 * rank), (rank, 2 * rank), (rest, rank)]
    return local(
        functools.partial(gather_body, places),
        bits,
        [packed],
        [vmem(*s) for s in shapes],
        parts * total * rank,
        4 * parts * total * rank,
    )


def sixth_body(bits, c1, c23, packed, value, gram, keep, send, coef):
    rank = c1.shape[1]
    share = c1.shape[0] // packed.shape[0]
    for j in range(2):
        coef[:, j * rank : (j + 1) * rank] = (
            packed[:, j * share : (j + 1) * share, :].reshape(c1.shape).astype(jnp.bfloat16)
        )
    lhs = jnp.concatenate([c1[...], c23[...], coef[...]], axis=1)
    emit_halves(bits[1], [value[i] - dot(lhs, gram[i]) for i in range(3)], keep, send)


def sixth(bits, c1, c23, packed, value, gram):
    rows, rank = c1.shape
    wide = 2 * rank
    return local(
        sixth_body,
        bits,
        [c1, c23, packed, value, gram],
        [vmem(rows // 2, 3 * wide)] * 2 + [vmem(rows, wide, dtype=jnp.bfloat16)],
        30 * rows * rank * wide,
        24 * rows * wide,
    )


def add_body(bits, left, right, out):
    out[...] = left[...] + right[...]


def add(bits, left, right):
    return local(add_body, bits, [left, right], [vmem(*left.shape)], left.size, 12 * left.size)[0]


def total_body(bits, parts, out):
    out[...] = parts[...].sum(axis=0)


def total(bits, parts):
    return local(total_body, bits, [parts], [vmem(*parts.shape[1:])], parts.size, 4 * parts.size)[0]


def lower_body(bits, state, c1, c23, c45, up, out):
    coef = jnp.concatenate([c1[...], c23[...], c45[...]], axis=1)
    depth, leaf = coef.shape[1], state.shape[1]
    width = leaf // STEPS
    for i in range(STEPS):
        here = slice(i * width, (i + 1) * width)
        basis = up[: depth // c1.shape[1], :, here].reshape(depth, width)
        out[:, here] = state[:, here].astype(jnp.float32) - dot(coef, basis)


def lower(bits, state, c1, c23, c45, up_basis):
    rows, leaf = state.shape
    return local(
        lower_body,
        bits,
        [state, c1, c23, c45, up_basis],
        [vmem(rows, leaf)],
        10 * rows * leaf * c1.shape[1],
        6 * rows * leaf,
    )[0]


def last_body(bits, state, mine, received, up6, up7, up8, out, coef):
    rank, count = up6.shape[0], mine.shape[0]

    @pl.when(pl.program_id(0) == 0)
    def _():
        for bit in range(2):

            @pl.when(bits[1] == bit)
            def _(bit=bit):
                here = slice(bit * count, (bit + 1) * count)
                there = slice((1 - bit) * count, (2 - bit) * count)
                coef[here, :] = mine[:, : 3 * rank].astype(jnp.bfloat16)
                coef[there, :rank] = received[:, 2 * rank :].astype(jnp.bfloat16)
                coef[there, rank:] = received[:, : 2 * rank].astype(jnp.bfloat16)

    basis = jnp.concatenate([up6[...], up7[...], up8[...]], axis=0)
    out[...] = state[...] - dot(coef[...], basis)


def last(bits, state, mine, received, up_basis):
    rows, leaf = state.shape
    levels, rank = up_basis.shape[:2]
    width = leaf // STEPS
    return run(
        last_body,
        STEPS,
        bits,
        [state, mine, received] + [hbm(up_basis)] * 3,
        [columns(rows, width), whole(mine.shape), whole(received.shape)]
        + [pl.BlockSpec((None, rank, width), lambda j, bits, k=k: (k - 1, 0, j)) for k in (6, 7, 8)],
        f32(rows, leaf),
        columns(rows, width),
        [pltpu.VMEM((rows, 3 * rank), jnp.bfloat16)],
        6 * rows * leaf * rank,
        6 * rows * leaf,
    )


def shards(groups_z, groups_zy, rhs, leaf_inverse, up_basis, projection):
    size_x, size_y = lax.axis_size("gx"), lax.axis_size("gy")
    rows = rhs.shape[0]
    rank = up_basis.shape[1]
    wide = 2 * rank
    gx, gy = lax.axis_index("gx"), lax.axis_index("gy")
    z0, z1, z2, y0, y1 = (gx >> i & 1 for i in range(5))
    core, x0, x1 = (gy >> i & 1 for i in range(3))
    bits = jnp.stack([z0, core, y0])
    over_x = functools.partial(swap, axis="gx", size=size_x)
    over_y = functools.partial(swap, axis="gy", size=size_y)
    ring = len(groups_z[0])
    share = rows // ring
    by_z0, by_z12, by_z2 = starts(z0, rank // 2), starts(z1 ^ z2, rank // 4), starts(z2, rank // 8)
    by_y01, by_y1 = starts(y0 ^ y1, 3 * rank // 2), starts(y1, 3 * rank // 4)
    half_z1, half_z2, half_y1 = starts(z1, rank), starts(z2, rank), starts(y1, rank)
    half_core, half_x0, half_x1 = starts(core, rank), starts(x0, rank), starts(x1, rank)
    indices = (
        bits, by_z0, by_z12, by_z2, by_y01, by_y1, half_z1, half_z2, half_y1,
        half_core, half_x0, half_x1, y1 == 0, (y0 ^ y1) == 0,
    )
    indices, rhs = lax.optimization_barrier((indices, rhs))
    (
        bits, by_z0, by_z12, by_z2, by_y01, by_y1, half_z1, half_z2, half_y1,
        half_core, half_x0, half_x1, first_y1, first_y01,
    ) = indices

    state, own, other = leaf_solve(bits, rhs, leaf_inverse, projection)
    received = over_x(other, mask=1)
    value, gram, kept = project((2, 3), ((2, 3),), bits, state, up_basis, projection)
    value_45, gram_45, kept_45 = project((4, 5), ((4, 5),), bits, state, up_basis, projection)

    keep, send, c1 = second(bits, own, received, value, gram)
    send, later = lax.optimization_barrier((send, state))
    received = over_x(send, mask=1)
    value_678, gram_678, kept_678 = project((6, 7, 8), ((6, 7), (6, 8), (7, 8)), bits, later, up_basis, projection)
    low, low_send = split(kept_45[0], by_z0)
    both = over_x(jnp.concatenate([kept[0], low_send]), mask=1)
    gram_23 = (kept[0] + both[:rank]).astype(jnp.bfloat16)
    low, low_send = split(low + both[rank:], by_z12)
    low, low_send = split(low + over_x(low_send, mask=2), by_z2)
    low = low + over_x(low_send, mask=6)
    places = [(i & 1) * 4 + (i >> 1 & 1 ^ i >> 2) * 2 + (i >> 2) for i in range(ring)]
    high, high_send = split(kept_678.reshape(3 * rank, wide), by_y01)
    high, high_send = split(high + over_x(high_send, mask=8), by_y1)
    high = high + over_x(high_send, mask=24)
    high = jnp.concatenate([high[:, :rank], high[:, rank:]])

    left = keep + received
    c2 = half(left[:, :wide], half_z1[0]) + over_x(half(left[:, :wide], half_z1[1]), mask=2)
    left = left[:, wide:] - dot(c2.astype(jnp.bfloat16), gram_23)
    c3 = half(left, half_z2[0]) + over_x(half(left, half_z2[1]), mask=6)
    c3 = c3 + over_x(c3, mask=2)
    mine = jnp.concatenate([c2, c3], axis=1)
    received = over_x(mine, mask=1)

    packed, c23 = fourth(bits, c1, mine, received, value_45, gram_45, low, high, ring)
    packed = exchange(packed, groups_z)
    own, other, left, gram_45, high = gather_rows(bits, packed, places, share)
    c4 = own + over_x(other, mask=8)
    left = left - dot(c4, gram_45)
    c5 = half(left, half_y1[0]) + over_x(half(left, half_y1[1]), mask=24)
    c5 = c5 + over_x(c5, mask=8)
    packed = jnp.concatenate([c4, c5, high], axis=0)
    packed = exchange(jnp.broadcast_to(packed, (ring, *packed.shape)), groups_z)

    keep, send, c45 = sixth(bits, c1, c23, packed, value_678, gram_678)
    left = add(bits, keep, over_y(send, mask=1))
    high = packed[:, 2 * share :].reshape(2, 3 * wide // ring, rank)
    high = jnp.concatenate([high[0], high[1]], axis=1)
    high = join(high, over_x(high, mask=24), first_y1)
    high = join(high, over_x(high, mask=8), first_y01)
    high_there = over_y(high, mask=1)
    left, high, high_there = lax.optimization_barrier((left, high, high_there))
    half_rows = rows // 2
    count = half_rows // size_x
    left = total(bits, exchange(left.reshape(size_x, count, 3 * wide), groups_zy))
    left, c45 = lax.optimization_barrier((left, c45))
    high, high_there = high.reshape(3, rank, wide), high_there.reshape(3, rank, wide)
    c6, c6_there = half(left[:, :wide], half_core[0]), half(left[:, :wide], half_core[1])
    z7 = left[:, wide : 2 * wide] - exact_dot(c6, high[0]) - exact_dot(c6_there, high_there[0])
    z8 = left[:, 2 * wide :] - exact_dot(c6, high[1]) - exact_dot(c6_there, high_there[1])
    c7 = half(z7, half_x0[0]) + over_y(half(z7, half_x0[1]), mask=2)
    z8 = z8 - exact_dot(c7, high[2] + high_there[2])
    c8 = half(z8, half_x1[0]) + over_y(half(z8, half_x1[1]), mask=6)
    c8 = c8 + over_y(c8, mask=2)
    state = lower(bits, state, c1, c23, c45, up_basis)
    packed = jnp.concatenate([c6, c7, c8, c6_there], axis=1)
    packed, state = lax.optimization_barrier((packed, state))
    packed = exchange(jnp.broadcast_to(packed, (size_x, *packed.shape)), groups_zy)
    packed = packed.reshape(half_rows, 4 * rank)
    received = over_y(packed[:, rank:], mask=1)
    return last(bits, state, packed, received, up_basis)


def solution(mesh):
    size_x, size_y = mesh.shape["gx"], mesh.shape["gy"]
    ring = 8
    groups_z = [
        [gy * size_x + start + i for i in range(ring)]
        for gy in range(size_y)
        for start in range(0, size_x, ring)
    ]
    groups_zy = [[gy * size_x + i for i in range(size_x)] for gy in range(size_y)]
    return jax.shard_map(
        functools.partial(shards, groups_z, groups_zy),
        mesh=mesh,
        in_specs=(
            P(None, ("gy", "gx")),
            P(("gy", "gx"), None, None),
            P(None, None, ("gy", "gx")),
            P(None, None, ("gy", "gx")),
        ),
        out_specs=P(None, ("gy", "gx")),
        check_vma=False,
    )
```

```python
import functools

import jax
import jax.numpy as jnp
from jax import lax
from jax.experimental import pallas as pl
from jax.experimental.pallas import tpu as pltpu
from jax.sharding import PartitionSpec as P

AXES = ("gy", "gx")
STEPS = 4
VMEM_BYTES = 16 * 1024 * 1024


def dot(a, b):
    return jnp.dot(a, b, preferred_element_type=jnp.float32)


def dot_t(a, b):
    return lax.dot_general(a, b, (((1,), (1,)), ((), ())), preferred_element_type=jnp.float32)


def exact_dot(a, b):
    return jnp.dot(a, b, precision=lax.Precision.HIGHEST, preferred_element_type=jnp.float32)


def swap(value, axis, mask, size):
    return lax.ppermute(value, axis, [(source, source ^ mask) for source in range(size)])


def exchange(value, groups):
    return lax.all_to_all(value, AXES, 0, 0, tiled=True, axis_index_groups=groups)


def half(value, start):
    return lax.dynamic_slice_in_dim(value, start, value.shape[-1] // 2, value.ndim - 1)


def split(value, starts):
    count = value.shape[0] // 2
    return tuple(lax.dynamic_slice_in_dim(value, start, count, 0) for start in starts)


def join(mine, other, first):
    return jnp.where(first, jnp.concatenate([mine, other]), jnp.concatenate([other, mine]))


def starts(bit, count):
    return (bit * count).astype(jnp.uint32), ((1 - bit) * count).astype(jnp.uint32)


def hbm(value):
    return pltpu.with_memory_space_constraint(value, pltpu.HBM)


def whole(shape):
    return pl.BlockSpec(shape, lambda j, bits: (0,) * len(shape))


def block(shape, *index):
    return pl.BlockSpec(shape, lambda j, bits: index)


def columns(rows, width):
    return pl.BlockSpec((rows, width), lambda j, bits: (0, j))


def run(body, steps, bits, args, in_specs, out_shape, out_specs, scratch, flops, nbytes):
    return pl.pallas_call(
        body,
        out_shape=out_shape,
        grid_spec=pltpu.PrefetchScalarGridSpec(
            num_scalar_prefetch=1,
            grid=(steps,),
            in_specs=in_specs,
            out_specs=out_specs,
            scratch_shapes=scratch,
        ),
        compiler_params=pltpu.CompilerParams(
            dimension_semantics=("arbitrary",), vmem_limit_bytes=VMEM_BYTES
        ),
        cost_estimate=pl.CostEstimate(flops=flops, bytes_accessed=nbytes, transcendentals=0),
    )(bits, *args)


def f32(*shape):
    return jax.ShapeDtypeStruct(shape, jnp.float32)


def bf16(*shape):
    return jax.ShapeDtypeStruct(shape, jnp.bfloat16)


def vmem(*shape, dtype=jnp.float32):
    return pltpu.VMEM(shape, dtype)


def local(body, bits, args, outs, flops, nbytes):
    args = [pltpu.with_memory_space_constraint(a, pltpu.VMEM) for a in args]
    return pl.pallas_call(
        body,
        out_shape=outs,
        in_specs=[pl.BlockSpec(memory_space=pltpu.SMEM)]
        + [pl.BlockSpec(memory_space=pltpu.VMEM)] * len(args),
        out_specs=[pl.BlockSpec(memory_space=pltpu.VMEM)] * len(outs),
        compiler_params=pltpu.CompilerParams(vmem_limit_bytes=VMEM_BYTES),
        cost_estimate=pl.CostEstimate(flops=flops, bytes_accessed=nbytes, transcendentals=0),
    )(bits, *args)


def leaf_body(bits, rhs, inverse, own_rows, other_rows, state, own, other, sums):
    rank = own.shape[1]
    rounded = dot(rhs[...], inverse[...]).astype(jnp.bfloat16)
    state[...] = rounded
    part = dot_t(rounded, jnp.concatenate([own_rows[...], other_rows[...]], axis=0))

    @pl.when(pl.program_id(0) == 0)
    def _():
        sums[...] = part

    @pl.when(pl.program_id(0) > 0)
    def _():
        sums[...] += part

    @pl.when(pl.program_id(0) == STEPS - 1)
    def _():
        own[...] = sums[:, :rank]
        other[...] = sums[:, rank:]


def leaf_solve(bits, rhs, leaf_inverse, projection):
    rows, leaf = rhs.shape
    rank = projection.shape[1] // 2
    width = leaf // STEPS
    return run(
        leaf_body,
        STEPS,
        bits,
        [hbm(rhs), hbm(leaf_inverse), hbm(projection), hbm(projection)],
        [
            whole((rows, leaf)),
            pl.BlockSpec((None, leaf, width), lambda j, bits: (0, 0, j)),
            pl.BlockSpec((None, rank, width), lambda j, bits: (0, bits[0], j)),
            pl.BlockSpec((None, rank, width), lambda j, bits: (0, 1 - bits[0], j)),
        ],
        [vmem(rows, leaf, dtype=jnp.bfloat16), vmem(rows, rank), vmem(rows, rank)],
        [columns(rows, width), whole((rows, rank)), whole((rows, rank))],
        [pltpu.VMEM((rows, 2 * rank), jnp.float32)],
        2 * rows * leaf * (leaf + 2 * rank),
        leaf * (4 * rows + 2 * leaf),
    )


def project_body(heights, depth, pairs, bits, state, up, proj, value, gram, *kept):
    rank = up.shape[1]
    for i, h in enumerate(heights):
        rows = proj[h - 1]
        value[i] = dot_t(state[...], rows)
        gram[i] = dot_t(up[:depth].reshape(depth * rank, up.shape[2]), rows).astype(jnp.bfloat16)
        for j, (k, of) in enumerate(pairs):
            if of == h:
                kept[0][j] = dot_t(up[k - 1], rows)


def project(heights, pairs, bits, state, up_basis, projection):
    rows, leaf = state.shape
    rank = up_basis.shape[1]
    wide, count, depth = 2 * rank, len(heights), heights[0] - 1
    return local(
        functools.partial(project_body, heights, depth, pairs),
        bits,
        [state, up_basis, projection],
        [vmem(count, rows, wide), vmem(count, depth * rank, wide, dtype=jnp.bfloat16)]
        + ([vmem(len(pairs), rank, wide)] if pairs else []),
        2 * leaf * wide * (count * (rows + rank * depth) + rank * len(pairs)),
        2 * leaf * (rows + count * 3 * rank),
    )


def emit_halves(which, parts, keep, send):
    count, wide = parts[0].shape[0] // 2, parts[0].shape[1]
    for bit in range(2):

        @pl.when(which == bit)
        def _(bit=bit):
            for i, part in enumerate(parts):
                keep[:count, i * wide : (i + 1) * wide] = part[bit * count : (bit + 1) * count]
                send[:count, i * wide : (i + 1) * wide] = part[(1 - bit) * count : (2 - bit) * count]


def second_body(bits, mine, received, value, gram, pair, ring, keep, send, coef):
    c1 = (mine[...] + received[...]).astype(jnp.bfloat16)
    coef[...] = c1
    rows, rank = keep.shape[0] - 3 * pair.shape[1] // 4, mine.shape[1]
    count, wide = pair.shape[1] // 2, 2 * rank
    emit_halves(bits[0], [value[i] - dot(c1, gram[i]) for i in range(2)], keep, send)
    for ref in (keep, send):
        for j in range(2):
            ref[rows : rows + count, j * wide : (j + 1) * wide] = pair[0, j * count : (j + 1) * count]
    for bit in range(2):

        @pl.when(bits[0] == bit)
        def _(bit=bit):
            for ref, first in ((keep, bit * count), (send, (1 - bit) * count)):
                for j in range(2):
                    start = first + j * count // 2
                    ref[rows + count :, j * wide : (j + 1) * wide] = ring[0, start : start + count // 2]


def second(bits, mine, received, value, gram, pair, ring):
    rows, rank = mine.shape
    wide = 2 * rank
    return local(
        second_body,
        bits,
        [mine, received, value, gram, pair, ring],
        [vmem(rows // 2 + 3 * rank // 4, 2 * wide)] * 2 + [vmem(rows, rank, dtype=jnp.bfloat16)],
        4 * rows * rank * wide,
        16 * rows * wide,
    )


def choose(bit, left, right, keep, send):
    for b in range(2):

        @pl.when(bit == b)
        def _(b=b):
            keep[...] = (left, right)[b]
            send[...] = (left, right)[1 - b]


def stack(value, rank):
    return jnp.concatenate([value[:, :rank], value[:, rank:]], axis=0)


def third_body(bits, keep, received, own, send, low, left, gram):
    total = keep[...] + received[...]
    rows, rank = own.shape
    wide, count = 2 * rank, gram.shape[0] // 2
    choose(bits[3], total[:rows, :rank], total[:rows, rank:wide], own, send.at[:rows])
    tail = total[rows + count :]
    choose(bits[4], stack(tail[:, :wide], rank), stack(tail[:, wide:], rank), low, send.at[rows:])
    left[...] = total[:rows, wide:]
    for j in range(2):
        gram[j * count : (j + 1) * count] = total[rows : rows + count, j * wide : (j + 1) * wide].astype(jnp.bfloat16)


def third(bits, keep, received, rank):
    rows = keep.shape[0] - 3 * rank // 4
    return local(
        third_body,
        bits,
        [keep, received],
        [
            vmem(rows, rank), vmem(rows + rank // 2, rank), vmem(rank // 2, rank),
            vmem(rows, 2 * rank), vmem(rank, 2 * rank, dtype=jnp.bfloat16),
        ],
        keep.size,
        12 * keep.size,
    )


def correct_body(bits, own, received, low, left, gram, coef, mine, send, kept):
    rows, rank = own.shape
    count = low.shape[0] // 4
    c2 = own[...] + received[:rows]
    coef[...] = c2
    rest = left[...] - dot(c2.astype(jnp.bfloat16), gram[...])
    choose(bits[5], rest[:, :rank], rest[:, rank:], mine, send.at[:rows])
    total = low[...] + received[rows:]
    parts = [jnp.concatenate([total[i * count : (i + 1) * count], total[(i + 2) * count : (i + 3) * count]]) for i in range(2)]
    choose(bits[5], parts[0], parts[1], kept, send.at[rows:])


def correct(bits, own, received, low, left, gram):
    rows, rank = own.shape
    return local(
        correct_body,
        bits,
        [own, received, low, left, gram],
        [vmem(rows, rank), vmem(rows, rank), vmem(rows + rank // 4, rank), vmem(rank // 4, rank)],
        4 * rows * rank * rank,
        20 * rows * rank,
    )


def fourth_body(bits, c1, mine, received, value, gram, low, high, packed, coef):
    count, rank = mine.shape[0], c1.shape[1]
    for bit in range(2):

        @pl.when(bits[0] == bit)
        def _(bit=bit):
            coef[bit * count : (bit + 1) * count] = mine[...].astype(jnp.bfloat16)
            coef[(1 - bit) * count : (2 - bit) * count] = received[...].astype(jnp.bfloat16)

    parts, total, _ = packed.shape
    share = value.shape[1] // parts
    lhs = jnp.concatenate([c1[...], coef[...]], axis=1)
    for i in range(2):
        left = value[i] - dot(lhs, gram[i])
        for j in range(2):
            start = (2 * i + j) * share
            packed[:, start : start + share, :] = left[:, j * rank : (j + 1) * rank].reshape(parts, share, rank)
    start = 4 * share
    packed[:, start : start + low.shape[0], :] = jnp.broadcast_to(low[...], (parts, *low.shape))
    start += low.shape[0]
    packed[:, start:total, :] = high[...].reshape(parts, total - start, rank)


def fourth(bits, c1, mine, received, value, gram, low, high, parts):
    rows, rank = c1.shape
    wide = 2 * rank
    total = 4 * rows // parts + low.shape[0] + high.shape[0] // parts
    return local(
        fourth_body,
        bits,
        [c1, mine, received, value, gram, low, high],
        [vmem(parts, total, rank), vmem(rows, wide, dtype=jnp.bfloat16)],
        12 * rows * rank * wide,
        16 * rows * wide,
    )


def gather_body(places, bits, packed, own, other, fifth, gram, high):
    parts, total, rank = packed.shape
    share, piece = own.shape[0], gram.shape[0] // parts
    for ref, bit in ((own, 0), (other, 1)):
        for b in range(2):

            @pl.when(bits[2] == b)
            def _(ref=ref, start=(bit ^ b) * share):
                ref[...] = packed[:, start : start + share, :].sum(axis=0)

    for j in range(2):
        start = (2 + j) * share
        fifth[:, j * rank : (j + 1) * rank] = packed[:, start : start + share, :].sum(axis=0)
    for i, place in enumerate(places):
        for j in range(2):
            start = 4 * share + j * piece
            gram[place * piece : (place + 1) * piece, j * rank : (j + 1) * rank] = packed[i, start : start + piece, :]
    high[...] = packed[:, 4 * share + 2 * piece :, :].sum(axis=0)


def gather_rows(bits, packed, places, share):
    parts, total, rank = packed.shape
    rest = total - 4 * share - 2 * rank // parts
    shapes = [(share, rank), (share, rank), (share, 2 * rank), (rank, 2 * rank), (rest, rank)]
    return local(
        functools.partial(gather_body, places),
        bits,
        [packed],
        [vmem(*s) for s in shapes],
        parts * total * rank,
        4 * parts * total * rank,
    )


def sixth_body(bits, c1, c23, packed, value, gram, keep, send, coef):
    rank = c1.shape[1]
    share = c1.shape[0] // packed.shape[0]
    for j in range(2):
        coef[:, j * rank : (j + 1) * rank] = (
            packed[:, j * share : (j + 1) * share, :].reshape(c1.shape).astype(jnp.bfloat16)
        )
    lhs = jnp.concatenate([c1[...], c23[...], coef[...]], axis=1)
    emit_halves(bits[1], [value[i] - dot(lhs, gram[i]) for i in range(3)], keep, send)


def sixth(bits, c1, c23, packed, value, gram):
    rows, rank = c1.shape
    wide = 2 * rank
    return local(
        sixth_body,
        bits,
        [c1, c23, packed, value, gram],
        [vmem(rows // 2, 3 * wide)] * 2 + [vmem(rows, wide, dtype=jnp.bfloat16)],
        30 * rows * rank * wide,
        24 * rows * wide,
    )


def add_body(bits, left, right, out):
    out[...] = left[...] + right[...]


def add(bits, left, right):
    return local(add_body, bits, [left, right], [vmem(*left.shape)], left.size, 12 * left.size)[0]


def total_body(bits, parts, out):
    out[...] = parts[...].sum(axis=0)


def total(bits, parts):
    return local(total_body, bits, [parts], [vmem(*parts.shape[1:])], parts.size, 4 * parts.size)[0]


def lower_body(bits, state, c1, c23, c45, up, out):
    coef = jnp.concatenate([c1[...], c23[...], c45[...]], axis=1)
    depth, leaf = coef.shape[1], state.shape[1]
    width = leaf // STEPS
    for i in range(STEPS):
        here = slice(i * width, (i + 1) * width)
        basis = up[: depth // c1.shape[1], :, here].reshape(depth, width)
        out[:, here] = state[:, here].astype(jnp.float32) - dot(coef, basis)


def lower(bits, state, c1, c23, c45, up_basis):
    rows, leaf = state.shape
    return local(
        lower_body,
        bits,
        [state, c1, c23, c45, up_basis],
        [vmem(rows, leaf)],
        10 * rows * leaf * c1.shape[1],
        6 * rows * leaf,
    )[0]


def last_body(bits, state, mine, received, up, out, coef, block, done):
    rank, count = up.shape[1], mine.shape[0]
    for bit in range(2):

        @pl.when(bits[1] == bit)
        def _(bit=bit):
            here = slice(bit * count, (bit + 1) * count)
            there = slice((1 - bit) * count, (2 - bit) * count)
            coef[here, :] = mine[:, : 3 * rank].astype(jnp.bfloat16)
            coef[there, :rank] = received[:, 2 * rank :].astype(jnp.bfloat16)
            coef[there, rank:] = received[:, : 2 * rank].astype(jnp.bfloat16)

    basis = up[5:8].reshape(3 * rank, up.shape[2])
    share = state.shape[0] // STEPS
    copies = []
    for i in range(STEPS):
        here = pl.ds(i * share, share)
        block[here] = state[here] - dot(coef[here], basis)
        copies.append(pltpu.make_async_copy(block.at[here], out.at[here], done.at[i]))
        copies[-1].start()
    for copy in copies:
        copy.wait()


def last(bits, state, mine, received, up_basis):
    rows, leaf = state.shape
    rank = up_basis.shape[1]
    args = [pltpu.with_memory_space_constraint(a, pltpu.VMEM) for a in (state, mine, received, up_basis)]
    return pl.pallas_call(
        last_body,
        out_shape=f32(rows, leaf),
        in_specs=[pl.BlockSpec(memory_space=pltpu.SMEM)] + [pl.BlockSpec(memory_space=pltpu.VMEM)] * 4,
        out_specs=pl.BlockSpec(memory_space=pltpu.HBM),
        scratch_shapes=[
            pltpu.VMEM((rows, 3 * rank), jnp.bfloat16),
            pltpu.VMEM((rows, leaf), jnp.float32),
            pltpu.SemaphoreType.DMA((STEPS,)),
        ],
        compiler_params=pltpu.CompilerParams(vmem_limit_bytes=VMEM_BYTES),
        cost_estimate=pl.CostEstimate(
            flops=6 * rows * leaf * rank, bytes_accessed=6 * rows * leaf, transcendentals=0
        ),
    )(bits, *args)


def shards(groups_z, groups_zy, rhs, leaf_inverse, up_basis, projection):
    size_x, size_y = lax.axis_size("gx"), lax.axis_size("gy")
    rows = rhs.shape[0]
    rank = up_basis.shape[1]
    wide = 2 * rank
    gx, gy = lax.axis_index("gx"), lax.axis_index("gy")
    z0, z1, z2, y0, y1 = (gx >> i & 1 for i in range(5))
    core, x0, x1 = (gy >> i & 1 for i in range(3))
    bits = jnp.stack([z0, core, y0, z1, z1 ^ z2, z2])
    over_x = functools.partial(swap, axis="gx", size=size_x)
    over_y = functools.partial(swap, axis="gy", size=size_y)
    ring = len(groups_z[0])
    share = rows // ring
    by_y01, by_y1 = starts(y0 ^ y1, 3 * rank // 2), starts(y1, 3 * rank // 4)
    half_y1 = starts(y1, rank)
    half_core, half_x0, half_x1 = starts(core, rank), starts(x0, rank), starts(x1, rank)
    indices = (
        bits, by_y01, by_y1, half_y1,
        half_core, half_x0, half_x1, y1 == 0, (y0 ^ y1) == 0,
    )
    indices, rhs = lax.optimization_barrier((indices, rhs))
    (
        bits, by_y01, by_y1, half_y1,
        half_core, half_x0, half_x1, first_y1, first_y01,
    ) = indices

    state, own, other = leaf_solve(bits, rhs, leaf_inverse, projection)
    received = over_x(other, mask=1)
    value, gram, kept = project((2, 3), ((2, 3),), bits, state, up_basis, projection)
    value_45, gram_45, kept_45 = project((4, 5), ((4, 5),), bits, state, up_basis, projection)

    value_678, gram_678, kept_678 = project((6, 7, 8), ((6, 7), (6, 8), (7, 8)), bits, state, up_basis, projection)
    received, kept, kept_45, kept_678 = lax.optimization_barrier((received, kept, kept_45, kept_678))

    keep, send, c1 = second(bits, own, received, value, gram, kept, kept_45)
    received = over_x(send, mask=1)
    places = [(i & 1) * 4 + (i >> 1 & 1 ^ i >> 2) * 2 + (i >> 2) for i in range(ring)]
    high, high_send = split(kept_678.reshape(3 * rank, wide), by_y01)
    high, high_send = split(high + over_x(high_send, mask=8), by_y1)
    high = high + over_x(high_send, mask=24)
    high = jnp.concatenate([high[:, :rank], high[:, rank:]])

    received, high = lax.optimization_barrier((received, high))
    own, send, low, left, gram_23 = third(bits, keep, received, rank)
    c2, own, send, low = correct(bits, own, over_x(send, mask=2), low, left, gram_23)
    received = over_x(send, mask=6)
    c3, low = own + received[: rows // 2], low + received[rows // 2 :]
    c3 = c3 + over_x(c3, mask=2)
    mine = jnp.concatenate([c2, c3], axis=1)
    received = over_x(mine, mask=1)

    packed, c23 = fourth(bits, c1, mine, received, value_45, gram_45, low, high, ring)
    packed = exchange(packed, groups_z)
    own, other, left, gram_45, high = gather_rows(bits, packed, places, share)
    c4 = own + over_x(other, mask=8)
    left = left - dot(c4, gram_45)
    received = over_x(jnp.concatenate([half(left, half_y1[1]), high]), mask=24)
    c5 = half(left, half_y1[0]) + received[:share]
    high = join(high, received[share:], first_y1)
    received = over_x(jnp.concatenate([c5, high]), mask=8)
    c5 = c5 + received[:share]
    high = join(high, received[share:], first_y01)
    packed = jnp.concatenate([c4, c5, high], axis=0)
    packed = exchange(jnp.broadcast_to(packed, (ring, *packed.shape)), groups_z)

    keep, send, c45 = sixth(bits, c1, c23, packed, value_678, gram_678)
    left = add(bits, keep, over_y(send, mask=1))
    high = packed[:, 2 * share :].reshape(2, ring // 2, 4, 3 * rank // (2 * ring), rank)
    high = jnp.concatenate(list(high.transpose(0, 2, 1, 3, 4).reshape(2, 3 * rank, rank)), axis=1)
    high_there = over_y(high, mask=1)
    left, high, high_there = lax.optimization_barrier((left, high, high_there))
    half_rows = rows // 2
    count = half_rows // size_x
    left = total(bits, exchange(left.reshape(size_x, count, 3 * wide), groups_zy))
    left, c45 = lax.optimization_barrier((left, c45))
    high, high_there = high.reshape(3, rank, wide), high_there.reshape(3, rank, wide)
    c6, c6_there = half(left[:, :wide], half_core[0]), half(left[:, :wide], half_core[1])
    z7 = left[:, wide : 2 * wide] - exact_dot(c6, high[0]) - exact_dot(c6_there, high_there[0])
    z8 = left[:, 2 * wide :] - exact_dot(c6, high[1]) - exact_dot(c6_there, high_there[1])
    c7 = half(z7, half_x0[0]) + over_y(half(z7, half_x0[1]), mask=2)
    z8 = z8 - exact_dot(c7, high[2] + high_there[2])
    c8 = half(z8, half_x1[0]) + over_y(half(z8, half_x1[1]), mask=6)
    c8 = c8 + over_y(c8, mask=2)
    state = lower(bits, state, c1, c23, c45, up_basis)
    packed = jnp.concatenate([c6, c7, c8, c6_there], axis=1)
    packed, state = lax.optimization_barrier((packed, state))
    packed = exchange(jnp.broadcast_to(packed, (size_x, *packed.shape)), groups_zy)
    packed = packed.reshape(half_rows, 4 * rank)
    received = over_y(packed[:, rank:], mask=1)
    return last(bits, state, packed, received, up_basis)


def solution(mesh):
    size_x, size_y = mesh.shape["gx"], mesh.shape["gy"]
    ring = 8
    groups_z = [
        [gy * size_x + start + i for i in range(ring)]
        for gy in range(size_y)
        for start in range(0, size_x, ring)
    ]
    groups_zy = [[gy * size_x + i for i in range(size_x)] for gy in range(size_y)]
    return jax.shard_map(
        functools.partial(shards, groups_z, groups_zy),
        mesh=mesh,
        in_specs=(
            P(None, ("gy", "gx")),
            P(("gy", "gx"), None, None),
            P(None, None, ("gy", "gx")),
            P(None, None, ("gy", "gx")),
        ),
        out_specs=P(None, ("gy", "gx")),
        check_vma=False,
    )
```

```python
import functools

import jax
import jax.numpy as jnp
from jax import lax
from jax.experimental import pallas as pl
from jax.experimental.pallas import tpu as pltpu
from jax.sharding import PartitionSpec as P

AXES = ("gy", "gx")
STEPS = 4
RING = 8
VMEM_BYTES = 16 * 1024 * 1024


def dot(a, b):
    return jnp.dot(a, b, preferred_element_type=jnp.float32)


def dot_t(a, b):
    return lax.dot_general(a, b, (((1,), (1,)), ((), ())), preferred_element_type=jnp.float32)


def exact_dot(a, b):
    return jnp.dot(a, b, precision=lax.Precision.HIGHEST, preferred_element_type=jnp.float32)


def swap(value, axis, mask, size):
    return lax.ppermute(value, axis, [(source, source ^ mask) for source in range(size)])


def exchange(value, groups):
    return lax.all_to_all(value, AXES, 0, 0, tiled=True, axis_index_groups=groups)


def half(value, start):
    return lax.dynamic_slice_in_dim(value, start, value.shape[-1] // 2, value.ndim - 1)


def split(value, starts):
    count = value.shape[0] // 2
    return tuple(lax.dynamic_slice_in_dim(value, start, count, 0) for start in starts)


def join(mine, other, first):
    return jnp.where(first, jnp.concatenate([mine, other]), jnp.concatenate([other, mine]))


def starts(bit, count):
    return (bit * count).astype(jnp.uint32), ((1 - bit) * count).astype(jnp.uint32)


def hbm(value):
    return pltpu.with_memory_space_constraint(value, pltpu.HBM)


def whole(shape):
    return pl.BlockSpec(shape, lambda j, bits: (0,) * len(shape))


def block(shape, *index):
    return pl.BlockSpec(shape, lambda j, bits: index)


def columns(rows, width):
    return pl.BlockSpec((rows, width), lambda j, bits: (0, j))


def run(body, steps, bits, args, in_specs, out_shape, out_specs, scratch, flops, nbytes):
    return pl.pallas_call(
        body,
        out_shape=out_shape,
        grid_spec=pltpu.PrefetchScalarGridSpec(
            num_scalar_prefetch=1,
            grid=(steps,),
            in_specs=in_specs,
            out_specs=out_specs,
            scratch_shapes=scratch,
        ),
        compiler_params=pltpu.CompilerParams(
            dimension_semantics=("arbitrary",), vmem_limit_bytes=VMEM_BYTES
        ),
        cost_estimate=pl.CostEstimate(flops=flops, bytes_accessed=nbytes, transcendentals=0),
    )(bits, *args)


def f32(*shape):
    return jax.ShapeDtypeStruct(shape, jnp.float32)


def bf16(*shape):
    return jax.ShapeDtypeStruct(shape, jnp.bfloat16)


def vmem(*shape, dtype=jnp.float32):
    return pltpu.VMEM(shape, dtype)


def local(body, bits, args, outs, flops, nbytes, scratch=()):
    args = [pltpu.with_memory_space_constraint(a, pltpu.VMEM) for a in args]
    return pl.pallas_call(
        body,
        out_shape=outs,
        in_specs=[pl.BlockSpec(memory_space=pltpu.SMEM)]
        + [pl.BlockSpec(memory_space=pltpu.VMEM)] * len(args),
        out_specs=[pl.BlockSpec(memory_space=pltpu.VMEM)] * len(outs),
        scratch_shapes=scratch,
        compiler_params=pltpu.CompilerParams(vmem_limit_bytes=VMEM_BYTES),
        cost_estimate=pl.CostEstimate(flops=flops, bytes_accessed=nbytes, transcendentals=0),
    )(bits, *args)


def leaf_body(bits, rhs, inverse, own_rows, other_rows, state, own, other, sums):
    rank = own.shape[1]
    rounded = dot(rhs[...], inverse[...]).astype(jnp.bfloat16)
    state[...] = rounded
    part = dot_t(rounded, jnp.concatenate([own_rows[...], other_rows[...]], axis=0))

    @pl.when(pl.program_id(0) == 0)
    def _():
        sums[...] = part

    @pl.when(pl.program_id(0) > 0)
    def _():
        sums[...] += part

    @pl.when(pl.program_id(0) == STEPS - 1)
    def _():
        own[...] = sums[:, :rank]
        other[...] = sums[:, rank:]


def leaf_solve(bits, rhs, leaf_inverse, projection):
    rows, leaf = rhs.shape
    rank = projection.shape[1] // 2
    width = leaf // STEPS
    return run(
        leaf_body,
        STEPS,
        bits,
        [hbm(rhs), hbm(leaf_inverse), hbm(projection), hbm(projection)],
        [
            whole((rows, leaf)),
            pl.BlockSpec((None, leaf, width), lambda j, bits: (0, 0, j)),
            pl.BlockSpec((None, rank, width), lambda j, bits: (0, bits[0], j)),
            pl.BlockSpec((None, rank, width), lambda j, bits: (0, 1 - bits[0], j)),
        ],
        [vmem(rows, leaf, dtype=jnp.bfloat16), vmem(rows, rank), vmem(rows, rank)],
        [columns(rows, width), whole((rows, rank)), whole((rows, rank))],
        [pltpu.VMEM((rows, 2 * rank), jnp.float32)],
        2 * rows * leaf * (leaf + 2 * rank),
        leaf * (4 * rows + 2 * leaf),
    )


def project_body(heights, depth, pairs, bits, state, up, proj, value, gram, *kept):
    rank = up.shape[1]
    for i, h in enumerate(heights):
        rows = proj[h - 1]
        value[i] = dot_t(state[...], rows)
        gram[i] = dot_t(up[:depth].reshape(depth * rank, up.shape[2]), rows).astype(jnp.bfloat16)
        for j, (k, of) in enumerate(pairs):
            if of == h:
                kept[0][j] = dot_t(up[k - 1], rows)


def project(heights, pairs, bits, state, up_basis, projection):
    rows, leaf = state.shape
    rank = up_basis.shape[1]
    wide, count, depth = 2 * rank, len(heights), heights[0] - 1
    return local(
        functools.partial(project_body, heights, depth, pairs),
        bits,
        [state, up_basis, projection],
        [vmem(count, rows, wide), vmem(count, depth * rank, wide, dtype=jnp.bfloat16)]
        + ([vmem(len(pairs), rank, wide)] if pairs else []),
        2 * leaf * wide * (count * (rows + rank * depth) + rank * len(pairs)),
        2 * leaf * (rows + count * 3 * rank),
    )


def emit_halves(which, parts, keep, send):
    count, wide = parts[0].shape[0] // 2, parts[0].shape[1]
    for bit in range(2):

        @pl.when(which == bit)
        def _(bit=bit):
            for i, part in enumerate(parts):
                keep[:count, i * wide : (i + 1) * wide] = part[bit * count : (bit + 1) * count]
                send[:count, i * wide : (i + 1) * wide] = part[(1 - bit) * count : (2 - bit) * count]


def second_body(bits, mine, received, value, gram, pair, ring, keep, send, coef):
    c1 = (mine[...] + received[...]).astype(jnp.bfloat16)
    coef[...] = c1
    rows, rank = keep.shape[0] - 3 * pair.shape[1] // 4, mine.shape[1]
    count, wide = pair.shape[1] // 2, 2 * rank
    emit_halves(bits[0], [value[i] - dot(c1, gram[i]) for i in range(2)], keep, send)
    for ref in (keep, send):
        for j in range(2):
            ref[rows : rows + count, j * wide : (j + 1) * wide] = pair[0, j * count : (j + 1) * count]
    for bit in range(2):

        @pl.when(bits[0] == bit)
        def _(bit=bit):
            for ref, first in ((keep, bit * count), (send, (1 - bit) * count)):
                for j in range(2):
                    start = first + j * count // 2
                    ref[rows + count :, j * wide : (j + 1) * wide] = ring[0, start : start + count // 2]


def second(bits, mine, received, value, gram, pair, ring):
    rows, rank = mine.shape
    wide = 2 * rank
    return local(
        second_body,
        bits,
        [mine, received, value, gram, pair, ring],
        [vmem(rows // 2 + 3 * rank // 4, 2 * wide)] * 2 + [vmem(rows, rank, dtype=jnp.bfloat16)],
        4 * rows * rank * wide,
        16 * rows * wide,
    )


def choose(bit, left, right, keep, send):
    for b in range(2):

        @pl.when(bit == b)
        def _(b=b):
            keep[...] = (left, right)[b]
            send[...] = (left, right)[1 - b]


def stack(value, rank):
    return jnp.concatenate([value[:, :rank], value[:, rank:]], axis=0)


def third_body(bits, keep, received, own, send, low, left, gram):
    total = keep[...] + received[...]
    rows, rank = own.shape
    wide, count = 2 * rank, gram.shape[0] // 2
    choose(bits[3], total[:rows, :rank], total[:rows, rank:wide], own, send.at[:rows])
    tail = total[rows + count :]
    choose(bits[4], stack(tail[:, :wide], rank), stack(tail[:, wide:], rank), low, send.at[rows:])
    left[...] = total[:rows, wide:]
    for j in range(2):
        gram[j * count : (j + 1) * count] = total[rows : rows + count, j * wide : (j + 1) * wide].astype(jnp.bfloat16)


def third(bits, keep, received, rank):
    rows = keep.shape[0] - 3 * rank // 4
    return local(
        third_body,
        bits,
        [keep, received],
        [
            vmem(rows, rank), vmem(rows + rank // 2, rank), vmem(rank // 2, rank),
            vmem(rows, 2 * rank), vmem(rank, 2 * rank, dtype=jnp.bfloat16),
        ],
        keep.size,
        12 * keep.size,
    )


def correct_body(bits, own, received, low, left, gram, coef, mine, send, kept):
    rows, rank = own.shape
    count = low.shape[0] // 4
    c2 = own[...] + received[:rows]
    coef[...] = c2
    rest = left[...] - dot(c2.astype(jnp.bfloat16), gram[...])
    choose(bits[5], rest[:, :rank], rest[:, rank:], mine, send.at[:rows])
    total = low[...] + received[rows:]
    parts = [jnp.concatenate([total[i * count : (i + 1) * count], total[(i + 2) * count : (i + 3) * count]]) for i in range(2)]
    choose(bits[5], parts[0], parts[1], kept, send.at[rows:])


def correct(bits, own, received, low, left, gram):
    rows, rank = own.shape
    return local(
        correct_body,
        bits,
        [own, received, low, left, gram],
        [vmem(rows, rank), vmem(rows, rank), vmem(rows + rank // 4, rank), vmem(rank // 4, rank)],
        4 * rows * rank * rank,
        20 * rows * rank,
    )


def fourth_body(bits, c1, mine, received, value, gram, low, high, keep_a, send_a, keep_b, send_b, coef, sums):
    count, rank = mine.shape[0], c1.shape[1]
    for bit in range(2):

        @pl.when(bits[0] == bit)
        def _(bit=bit):
            coef[bit * count : (bit + 1) * count] = mine[...].astype(jnp.bfloat16)
            coef[(1 - bit) * count : (2 - bit) * count] = received[...].astype(jnp.bfloat16)

    rows, wide = value.shape[1:]
    share = rows // RING
    piece = high.shape[0] // RING
    lhs = jnp.concatenate([c1[...], coef[...]], axis=1)
    for i in range(2):
        sums[i] = value[i] - dot(lhs, gram[i])
    for keep, send, level in ((keep_a, send_a, 0), (keep_b, send_b, 1)):
        for ref, parity in ((keep, bits[0]), (send, 1 - bits[0])):
            for i in range(RING // 2):
                place = 2 * i + parity
                for j in range(2):
                    start = (2 * i + j) * share
                    ref[start : start + share] = sums[
                        level, pl.ds(pl.multiple_of(place * share, share), share), j * rank : (j + 1) * rank
                    ]
                if level == 0:
                    start = rows + i * piece
                    ref[start : start + piece] = high[pl.ds(pl.multiple_of(place * piece, piece), piece)]
    send_a[rows + RING // 2 * piece :] = low[...]


def fourth(bits, c1, mine, received, value, gram, low, high):
    rows, rank = c1.shape
    wide = 2 * rank
    extra = high.shape[0] // 2
    return local(
        fourth_body,
        bits,
        [c1, mine, received, value, gram, low, high],
        [
            vmem(rows + extra, rank), vmem(rows + extra + low.shape[0], rank),
            vmem(rows, rank), vmem(rows, rank), vmem(rows, wide, dtype=jnp.bfloat16),
        ],
        12 * rows * rank * wide,
        16 * rows * wide,
        [pltpu.VMEM((2, rows, wide), jnp.float32)],
    )


def halve_body(steps, bits, *refs):
    (keep_a, got_a, keep_b, got_b, low), (next_a, send_a, next_b, send_b, lows) = refs[:5], refs[5:]
    count = keep_b.shape[0] // (2 * steps)
    piece = (keep_a.shape[0] - keep_b.shape[0]) // (2 * steps)
    rows = keep_b.shape[0]
    for out, to, got, keep, far, near in (
        (next_a, send_a, got_a, keep_a, 1, 3),
        (next_b, send_b, got_b, keep_b, 3, 1),
    ):
        if steps == 2:
            mine = [bits[6], bits[6] ^ near]
            theirs = [bits[6] ^ far, bits[6] ^ far ^ near]
        else:
            mine, theirs = [0], [1]
        for ref, slots in ((out, mine), (to, theirs)):
            for i, slot in enumerate(slots):
                here = pl.ds(slot * count, count)
                ref[i * count : (i + 1) * count] = keep[here] + got[here]
                if keep.shape[0] > rows:
                    there = pl.ds(rows + slot * piece, piece)
                    start = len(slots) * count + i * piece
                    ref[start : start + piece] = keep[there] + got[there]
    done = low.shape[0]
    lows[:done] = low[...]
    lows[done:] = got_a[keep_a.shape[0] :]
    send_a[next_a.shape[0] :] = lows[...]


def halve(bits, steps, keep_a, got_a, keep_b, got_b, low):
    rank = low.shape[1]
    size_a, size_b, lows = keep_a.shape[0] // 2, keep_b.shape[0] // 2, 2 * low.shape[0]
    return local(
        functools.partial(halve_body, steps),
        bits,
        [keep_a, got_a, keep_b, got_b, low],
        [vmem(size_a, rank), vmem(size_a + lows, rank), vmem(size_b, rank), vmem(size_b, rank), vmem(lows, rank)],
        2 * keep_a.size,
        20 * keep_a.size,
    )


def gather_body(bits, keep_a, got_a, keep_b, got_b, low, own, other, fifth, gram, high):
    share, rank = own.shape
    rows = 2 * share
    total = keep_a[...] + got_a[: keep_a.shape[0]]
    choose(bits[2], total[:share], total[share:rows], own, other)
    high[...] = total[rows:]
    for j in range(2):
        here = slice(j * share, (j + 1) * share)
        fifth[:, j * rank : (j + 1) * rank] = keep_b[here] + got_b[here]
    count = gram.shape[0] // RING
    half_list = low.shape[0]
    z0, z1, z2 = bits[0], bits[3], bits[5]
    for i, mask in enumerate((0, 1, 2, 3, 6, 7, 4, 5)):
        p0, p1, p2 = z0 ^ (mask & 1), z1 ^ (mask >> 1 & 1), z2 ^ (mask >> 2)
        place = pl.multiple_of((p0 * 4 + (p1 ^ p2) * 2 + p2) * count, count)
        for j in range(2):
            start = 2 * i * count + j * count
            if start < half_list:
                part = low[start : start + count]
            else:
                start += keep_a.shape[0] - half_list
                part = got_a[start : start + count]
            gram[pl.ds(place, count), j * rank : (j + 1) * rank] = part


def gather_rows(bits, keep_a, got_a, keep_b, got_b, low):
    share, rank = keep_b.shape[0] // 2, keep_b.shape[1]
    shapes = [(share, rank), (share, rank), (share, 2 * rank), (rank, 2 * rank), (keep_a.shape[0] - 2 * share, rank)]
    return local(
        gather_body,
        bits,
        [keep_a, got_a, keep_b, got_b, low],
        [vmem(*s) for s in shapes],
        2 * keep_a.size,
        20 * keep_a.size,
    )


def sixth_body(bits, c1, c23, packed, value, gram, keep, send, coef):
    rank = c1.shape[1]
    share = c1.shape[0] // packed.shape[0]
    for j in range(2):
        coef[:, j * rank : (j + 1) * rank] = (
            packed[:, j * share : (j + 1) * share, :].reshape(c1.shape).astype(jnp.bfloat16)
        )
    lhs = jnp.concatenate([c1[...], c23[...], coef[...]], axis=1)
    emit_halves(bits[1], [value[i] - dot(lhs, gram[i]) for i in range(3)], keep, send)


def sixth(bits, c1, c23, packed, value, gram):
    rows, rank = c1.shape
    wide = 2 * rank
    return local(
        sixth_body,
        bits,
        [c1, c23, packed, value, gram],
        [vmem(rows // 2, 3 * wide)] * 2 + [vmem(rows, wide, dtype=jnp.bfloat16)],
        30 * rows * rank * wide,
        24 * rows * wide,
    )


def add_body(bits, left, right, out):
    out[...] = left[...] + right[...]


def add(bits, left, right):
    return local(add_body, bits, [left, right], [vmem(*left.shape)], left.size, 12 * left.size)[0]


def total_body(bits, parts, out):
    out[...] = parts[...].sum(axis=0)


def total(bits, parts):
    return local(total_body, bits, [parts], [vmem(*parts.shape[1:])], parts.size, 4 * parts.size)[0]


def lower_body(bits, state, c1, c23, c45, up, out):
    coef = jnp.concatenate([c1[...], c23[...], c45[...]], axis=1)
    depth, leaf = coef.shape[1], state.shape[1]
    width = leaf // STEPS
    for i in range(STEPS):
        here = slice(i * width, (i + 1) * width)
        basis = up[: depth // c1.shape[1], :, here].reshape(depth, width)
        out[:, here] = state[:, here].astype(jnp.float32) - dot(coef, basis)


def lower(bits, state, c1, c23, c45, up_basis):
    rows, leaf = state.shape
    return local(
        lower_body,
        bits,
        [state, c1, c23, c45, up_basis],
        [vmem(rows, leaf)],
        10 * rows * leaf * c1.shape[1],
        6 * rows * leaf,
    )[0]


def last_body(bits, state, mine, received, up, out, coef, block, done):
    rank, count = up.shape[1], mine.shape[0]
    for bit in range(2):

        @pl.when(bits[1] == bit)
        def _(bit=bit):
            here = slice(bit * count, (bit + 1) * count)
            there = slice((1 - bit) * count, (2 - bit) * count)
            coef[here, :] = mine[:, : 3 * rank].astype(jnp.bfloat16)
            coef[there, :rank] = received[:, 2 * rank :].astype(jnp.bfloat16)
            coef[there, rank:] = received[:, : 2 * rank].astype(jnp.bfloat16)

    basis = up[5:8].reshape(3 * rank, up.shape[2])
    share = state.shape[0] // STEPS
    copies = []
    for i in range(STEPS):
        here = pl.ds(i * share, share)
        block[here] = state[here] - dot(coef[here], basis)
        copies.append(pltpu.make_async_copy(block.at[here], out.at[here], done.at[i]))
        copies[-1].start()
    for copy in copies:
        copy.wait()


def last(bits, state, mine, received, up_basis):
    rows, leaf = state.shape
    rank = up_basis.shape[1]
    args = [pltpu.with_memory_space_constraint(a, pltpu.VMEM) for a in (state, mine, received, up_basis)]
    return pl.pallas_call(
        last_body,
        out_shape=f32(rows, leaf),
        in_specs=[pl.BlockSpec(memory_space=pltpu.SMEM)] + [pl.BlockSpec(memory_space=pltpu.VMEM)] * 4,
        out_specs=pl.BlockSpec(memory_space=pltpu.HBM),
        scratch_shapes=[
            pltpu.VMEM((rows, 3 * rank), jnp.bfloat16),
            pltpu.VMEM((rows, leaf), jnp.float32),
            pltpu.SemaphoreType.DMA((STEPS,)),
        ],
        compiler_params=pltpu.CompilerParams(vmem_limit_bytes=VMEM_BYTES),
        cost_estimate=pl.CostEstimate(
            flops=6 * rows * leaf * rank, bytes_accessed=6 * rows * leaf, transcendentals=0
        ),
    )(bits, *args)


def shards(groups_z, groups_zy, rhs, leaf_inverse, up_basis, projection):
    size_x, size_y = lax.axis_size("gx"), lax.axis_size("gy")
    rows = rhs.shape[0]
    rank = up_basis.shape[1]
    wide = 2 * rank
    gx, gy = lax.axis_index("gx"), lax.axis_index("gy")
    z0, z1, z2, y0, y1 = (gx >> i & 1 for i in range(5))
    core, x0, x1 = (gy >> i & 1 for i in range(3))
    bits = jnp.stack([z0, core, y0, z1, z1 ^ z2, z2, z1 + 2 * z2])
    over_x = functools.partial(swap, axis="gx", size=size_x)
    over_y = functools.partial(swap, axis="gy", size=size_y)
    ring = RING
    share = rows // ring
    by_y01, by_y1 = starts(y0 ^ y1, 3 * rank // 2), starts(y1, 3 * rank // 4)
    half_y1 = starts(y1, rank)
    half_core, half_x0, half_x1 = starts(core, rank), starts(x0, rank), starts(x1, rank)
    indices = (
        bits, by_y01, by_y1, half_y1,
        half_core, half_x0, half_x1, y1 == 0, (y0 ^ y1) == 0,
    )
    indices, rhs = lax.optimization_barrier((indices, rhs))
    (
        bits, by_y01, by_y1, half_y1,
        half_core, half_x0, half_x1, first_y1, first_y01,
    ) = indices

    state, own, other = leaf_solve(bits, rhs, leaf_inverse, projection)
    received = over_x(other, mask=1)
    value, gram, kept = project((2, 3), ((2, 3),), bits, state, up_basis, projection)
    value_45, gram_45, kept_45 = project((4, 5), ((4, 5),), bits, state, up_basis, projection)

    value_678, gram_678, kept_678 = project((6, 7, 8), ((6, 7), (6, 8), (7, 8)), bits, state, up_basis, projection)
    received, kept, kept_45, kept_678 = lax.optimization_barrier((received, kept, kept_45, kept_678))

    keep, send, c1 = second(bits, own, received, value, gram, kept, kept_45)
    received = over_x(send, mask=1)
    high, high_send = split(kept_678.reshape(3 * rank, wide), by_y01)
    high, high_send = split(high + over_x(high_send, mask=8), by_y1)
    high = high + over_x(high_send, mask=24)
    high = jnp.concatenate([high[:, :rank], high[:, rank:]])

    received, high = lax.optimization_barrier((received, high))
    own, send, low, left, gram_23 = third(bits, keep, received, rank)
    c2, own, send, low = correct(bits, own, over_x(send, mask=2), low, left, gram_23)
    received = over_x(send, mask=6)
    c3, low = own + received[: rows // 2], low + received[rows // 2 :]
    c3 = c3 + over_x(c3, mask=2)
    mine = jnp.concatenate([c2, c3], axis=1)
    received = over_x(mine, mask=1)

    keep_a, send_a, keep_b, send_b, c23 = fourth(bits, c1, mine, received, value_45, gram_45, low, high)
    turned = [(i & -RING) + ((i + 1 if i & 1 else i - 1) % RING) for i in range(size_x)]
    got_a, got_b = over_x(send_a, mask=1), lax.ppermute(send_b, "gx", list(enumerate(turned)))
    keep_a, send_a, keep_b, send_b, low = halve(bits, 2, keep_a, got_a, keep_b, got_b, low)
    got_a, got_b = over_x(send_a, mask=2), over_x(send_b, mask=6)
    keep_a, send_a, keep_b, send_b, low = halve(bits, 1, keep_a, got_a, keep_b, got_b, low)
    got_a, got_b = over_x(send_a, mask=6), over_x(send_b, mask=2)
    own, other, left, gram_45, high = gather_rows(bits, keep_a, got_a, keep_b, got_b, low)
    c4 = own + over_x(other, mask=8)
    left = left - dot(c4, gram_45)
    received = over_x(jnp.concatenate([half(left, half_y1[1]), high]), mask=24)
    c5 = half(left, half_y1[0]) + received[:share]
    high = join(high, received[share:], first_y1)
    received = over_x(jnp.concatenate([c5, high]), mask=8)
    c5 = c5 + received[:share]
    high = join(high, received[share:], first_y01)
    packed = jnp.concatenate([c4, c5, high], axis=0)
    packed = exchange(jnp.broadcast_to(packed, (ring, *packed.shape)), groups_z)

    keep, send, c45 = sixth(bits, c1, c23, packed, value_678, gram_678)
    left = add(bits, keep, over_y(send, mask=1))
    high = packed[:, 2 * share :].reshape(2, ring // 2, 4, 3 * rank // (2 * ring), rank)
    high = jnp.concatenate(list(high.transpose(0, 2, 1, 3, 4).reshape(2, 3 * rank, rank)), axis=1)
    high_there = over_y(high, mask=1)
    left, high, high_there = lax.optimization_barrier((left, high, high_there))
    half_rows = rows // 2
    count = half_rows // size_x
    left = total(bits, exchange(left.reshape(size_x, count, 3 * wide), groups_zy))
    left, c45 = lax.optimization_barrier((left, c45))
    high, high_there = high.reshape(3, rank, wide), high_there.reshape(3, rank, wide)
    c6, c6_there = half(left[:, :wide], half_core[0]), half(left[:, :wide], half_core[1])
    z7 = left[:, wide : 2 * wide] - exact_dot(c6, high[0]) - exact_dot(c6_there, high_there[0])
    z8 = left[:, 2 * wide :] - exact_dot(c6, high[1]) - exact_dot(c6_there, high_there[1])
    c7 = half(z7, half_x0[0]) + over_y(half(z7, half_x0[1]), mask=2)
    z8 = z8 - exact_dot(c7, high[2] + high_there[2])
    c8 = half(z8, half_x1[0]) + over_y(half(z8, half_x1[1]), mask=6)
    c8 = c8 + over_y(c8, mask=2)
    state = lower(bits, state, c1, c23, c45, up_basis)
    packed = jnp.concatenate([c6, c7, c8, c6_there], axis=1)
    packed, state = lax.optimization_barrier((packed, state))
    packed = exchange(jnp.broadcast_to(packed, (size_x, *packed.shape)), groups_zy)
    packed = packed.reshape(half_rows, 4 * rank)
    received = over_y(packed[:, rank:], mask=1)
    return last(bits, state, packed, received, up_basis)


def solution(mesh):
    size_x, size_y = mesh.shape["gx"], mesh.shape["gy"]
    ring = RING
    groups_z = [
        [gy * size_x + start + i for i in range(ring)]
        for gy in range(size_y)
        for start in range(0, size_x, ring)
    ]
    groups_zy = [[gy * size_x + i for i in range(size_x)] for gy in range(size_y)]
    return jax.shard_map(
        functools.partial(shards, groups_z, groups_zy),
        mesh=mesh,
        in_specs=(
            P(None, ("gy", "gx")),
            P(("gy", "gx"), None, None),
            P(None, None, ("gy", "gx")),
            P(None, None, ("gy", "gx")),
        ),
        out_specs=P(None, ("gy", "gx")),
        check_vma=False,
    )
```

```python
import functools

import jax
import jax.numpy as jnp
from jax import lax
from jax.experimental import pallas as pl
from jax.experimental.pallas import tpu as pltpu
from jax.sharding import PartitionSpec as P

AXES = ("gy", "gx")
STEPS = 4
RING = 8
VMEM_BYTES = 16 * 1024 * 1024


def dot(a, b):
    return jnp.dot(a, b, preferred_element_type=jnp.float32)


def dot_t(a, b):
    return lax.dot_general(a, b, (((1,), (1,)), ((), ())), preferred_element_type=jnp.float32)


def exact_dot(a, b):
    return jnp.dot(a, b, precision=lax.Precision.HIGHEST, preferred_element_type=jnp.float32)


def swap(value, axis, mask, size):
    return lax.ppermute(value, axis, [(source, source ^ mask) for source in range(size)])


def exchange(value, groups):
    return lax.all_to_all(value, AXES, 0, 0, tiled=True, axis_index_groups=groups)


def half(value, start):
    return lax.dynamic_slice_in_dim(value, start, value.shape[-1] // 2, value.ndim - 1)


def split(value, starts):
    count = value.shape[0] // 2
    return tuple(lax.dynamic_slice_in_dim(value, start, count, 0) for start in starts)


def join(mine, other, first):
    return jnp.where(first, jnp.concatenate([mine, other]), jnp.concatenate([other, mine]))


def starts(bit, count):
    return (bit * count).astype(jnp.uint32), ((1 - bit) * count).astype(jnp.uint32)


def hbm(value):
    return pltpu.with_memory_space_constraint(value, pltpu.HBM)


def whole(shape):
    return pl.BlockSpec(shape, lambda j, bits: (0,) * len(shape))


def block(shape, *index):
    return pl.BlockSpec(shape, lambda j, bits: index)


def columns(rows, width):
    return pl.BlockSpec((rows, width), lambda j, bits: (0, j))


def run(body, steps, bits, args, in_specs, out_shape, out_specs, scratch, flops, nbytes):
    return pl.pallas_call(
        body,
        out_shape=out_shape,
        grid_spec=pltpu.PrefetchScalarGridSpec(
            num_scalar_prefetch=1,
            grid=(steps,),
            in_specs=in_specs,
            out_specs=out_specs,
            scratch_shapes=scratch,
        ),
        compiler_params=pltpu.CompilerParams(
            dimension_semantics=("arbitrary",), vmem_limit_bytes=VMEM_BYTES
        ),
        cost_estimate=pl.CostEstimate(flops=flops, bytes_accessed=nbytes, transcendentals=0),
    )(bits, *args)


def f32(*shape):
    return jax.ShapeDtypeStruct(shape, jnp.float32)


def bf16(*shape):
    return jax.ShapeDtypeStruct(shape, jnp.bfloat16)


def vmem(*shape, dtype=jnp.float32):
    return pltpu.VMEM(shape, dtype)


def local(body, bits, args, outs, flops, nbytes, scratch=()):
    args = [pltpu.with_memory_space_constraint(a, pltpu.VMEM) for a in args]
    return pl.pallas_call(
        body,
        out_shape=outs,
        in_specs=[pl.BlockSpec(memory_space=pltpu.SMEM)]
        + [pl.BlockSpec(memory_space=pltpu.VMEM)] * len(args),
        out_specs=[pl.BlockSpec(memory_space=pltpu.VMEM)] * len(outs),
        scratch_shapes=scratch,
        compiler_params=pltpu.CompilerParams(vmem_limit_bytes=VMEM_BYTES),
        cost_estimate=pl.CostEstimate(flops=flops, bytes_accessed=nbytes, transcendentals=0),
    )(bits, *args)


def leaf_body(bits, rhs, inverse, own_rows, other_rows, state, own, other, sums):
    rank = own.shape[1]
    rounded = dot(rhs[...], inverse[...]).astype(jnp.bfloat16)
    state[...] = rounded
    part = dot_t(rounded, jnp.concatenate([own_rows[...], other_rows[...]], axis=0))

    @pl.when(pl.program_id(0) == 0)
    def _():
        sums[...] = part

    @pl.when(pl.program_id(0) > 0)
    def _():
        sums[...] += part

    @pl.when(pl.program_id(0) == STEPS - 1)
    def _():
        own[...] = sums[:, :rank]
        other[...] = sums[:, rank:]


def leaf_solve(bits, rhs, leaf_inverse, projection):
    rows, leaf = rhs.shape
    rank = projection.shape[1] // 2
    width = leaf // STEPS
    return run(
        leaf_body,
        STEPS,
        bits,
        [hbm(rhs), hbm(leaf_inverse), hbm(projection), hbm(projection)],
        [
            whole((rows, leaf)),
            pl.BlockSpec((None, leaf, width), lambda j, bits: (0, 0, j)),
            pl.BlockSpec((None, rank, width), lambda j, bits: (0, bits[0], j)),
            pl.BlockSpec((None, rank, width), lambda j, bits: (0, 1 - bits[0], j)),
        ],
        [vmem(rows, leaf, dtype=jnp.bfloat16), vmem(rows, rank), vmem(rows, rank)],
        [columns(rows, width), whole((rows, rank)), whole((rows, rank))],
        [pltpu.VMEM((rows, 2 * rank), jnp.float32)],
        2 * rows * leaf * (leaf + 2 * rank),
        leaf * (4 * rows + 2 * leaf),
    )


def project_body(heights, depth, pairs, bits, state, up, proj, value, gram, *kept):
    rank = up.shape[1]
    for i, h in enumerate(heights):
        rows = proj[h - 1]
        value[i] = dot_t(state[...], rows)
        gram[i] = dot_t(up[:depth].reshape(depth * rank, up.shape[2]), rows).astype(jnp.bfloat16)
        for j, (k, of) in enumerate(pairs):
            if of == h:
                kept[0][j] = dot_t(up[k - 1], rows)


def project(heights, pairs, bits, state, up_basis, projection):
    rows, leaf = state.shape
    rank = up_basis.shape[1]
    wide, count, depth = 2 * rank, len(heights), heights[0] - 1
    return local(
        functools.partial(project_body, heights, depth, pairs),
        bits,
        [state, up_basis, projection],
        [vmem(count, rows, wide), vmem(count, depth * rank, wide, dtype=jnp.bfloat16)]
        + ([vmem(len(pairs), rank, wide)] if pairs else []),
        2 * leaf * wide * (count * (rows + rank * depth) + rank * len(pairs)),
        2 * leaf * (rows + count * 3 * rank),
    )


def emit_halves(which, parts, keep, send):
    count, wide = parts[0].shape[0] // 2, parts[0].shape[1]
    for bit in range(2):

        @pl.when(which == bit)
        def _(bit=bit):
            for i, part in enumerate(parts):
                keep[:count, i * wide : (i + 1) * wide] = part[bit * count : (bit + 1) * count]
                send[:count, i * wide : (i + 1) * wide] = part[(1 - bit) * count : (2 - bit) * count]


def second_body(bits, mine, received, value, gram, pair, ring, keep, send, coef):
    c1 = (mine[...] + received[...]).astype(jnp.bfloat16)
    coef[...] = c1
    rows, rank = keep.shape[0] - 3 * pair.shape[1] // 4, mine.shape[1]
    count, wide = pair.shape[1] // 2, 2 * rank
    emit_halves(bits[0], [value[i] - dot(c1, gram[i]) for i in range(2)], keep, send)
    for ref in (keep, send):
        for j in range(2):
            ref[rows : rows + count, j * wide : (j + 1) * wide] = pair[0, j * count : (j + 1) * count]
    for bit in range(2):

        @pl.when(bits[0] == bit)
        def _(bit=bit):
            for ref, first in ((keep, bit * count), (send, (1 - bit) * count)):
                for j in range(2):
                    start = first + j * count // 2
                    ref[rows + count :, j * wide : (j + 1) * wide] = ring[0, start : start + count // 2]


def second(bits, mine, received, value, gram, pair, ring):
    rows, rank = mine.shape
    wide = 2 * rank
    return local(
        second_body,
        bits,
        [mine, received, value, gram, pair, ring],
        [vmem(rows // 2 + 3 * rank // 4, 2 * wide)] * 2 + [vmem(rows, rank, dtype=jnp.bfloat16)],
        4 * rows * rank * wide,
        16 * rows * wide,
    )


def choose(bit, left, right, keep, send):
    for b in range(2):

        @pl.when(bit == b)
        def _(b=b):
            keep[...] = (left, right)[b]
            send[...] = (left, right)[1 - b]


def stack(value, rank):
    return jnp.concatenate([value[:, :rank], value[:, rank:]], axis=0)


def third_body(bits, keep, received, own, send, low, left, gram):
    total = keep[...] + received[...]
    rows, rank = own.shape
    wide, count = 2 * rank, gram.shape[0] // 2
    choose(bits[3], total[:rows, :rank], total[:rows, rank:wide], own, send.at[:rows])
    tail = total[rows + count :]
    choose(bits[4], stack(tail[:, :wide], rank), stack(tail[:, wide:], rank), low, send.at[rows:])
    left[...] = total[:rows, wide:]
    for j in range(2):
        gram[j * count : (j + 1) * count] = total[rows : rows + count, j * wide : (j + 1) * wide].astype(jnp.bfloat16)


def third(bits, keep, received, rank):
    rows = keep.shape[0] - 3 * rank // 4
    return local(
        third_body,
        bits,
        [keep, received],
        [
            vmem(rows, rank), vmem(rows + rank // 2, rank), vmem(rank // 2, rank),
            vmem(rows, 2 * rank), vmem(rank, 2 * rank, dtype=jnp.bfloat16),
        ],
        keep.size,
        12 * keep.size,
    )


def correct_body(bits, own, received, low, left, gram, coef, mine, send, kept):
    rows, rank = own.shape
    count = low.shape[0] // 4
    c2 = own[...] + received[:rows]
    coef[...] = c2
    rest = left[...] - dot(c2.astype(jnp.bfloat16), gram[...])
    choose(bits[5], rest[:, :rank], rest[:, rank:], mine, send.at[:rows])
    total = low[...] + received[rows:]
    parts = [jnp.concatenate([total[i * count : (i + 1) * count], total[(i + 2) * count : (i + 3) * count]]) for i in range(2)]
    choose(bits[5], parts[0], parts[1], kept, send.at[rows:])


def correct(bits, own, received, low, left, gram):
    rows, rank = own.shape
    return local(
        correct_body,
        bits,
        [own, received, low, left, gram],
        [vmem(rows, rank), vmem(rows, rank), vmem(rows + rank // 4, rank), vmem(rank // 4, rank)],
        4 * rows * rank * rank,
        20 * rows * rank,
    )


def fourth_body(bits, c1, c2, c3, c2_there, c3_there, value, gram, low, high, keep_a, send_a, keep_b, send_b, coef, sums):
    count, rank = c2.shape
    for bit in range(2):

        @pl.when(bits[0] == bit)
        def _(bit=bit):
            for j, (mine, received) in enumerate(((c2, c2_there), (c3, c3_there))):
                here = slice(j * rank, (j + 1) * rank)
                coef[bit * count : (bit + 1) * count, here] = mine[...].astype(jnp.bfloat16)
                coef[(1 - bit) * count : (2 - bit) * count, here] = received[...].astype(jnp.bfloat16)

    rows, wide = value.shape[1:]
    share = rows // RING
    piece = high.shape[0] // RING
    lhs = jnp.concatenate([c1[...], coef[...]], axis=1)
    for i in range(2):
        sums[i] = value[i] - dot(lhs, gram[i])
    for keep, send, level in ((keep_a, send_a, 0), (keep_b, send_b, 1)):
        for ref, parity in ((keep, bits[0]), (send, 1 - bits[0])):
            for i in range(RING // 2):
                place = 2 * i + parity
                for j in range(2):
                    start = (2 * i + j) * share
                    ref[start : start + share] = sums[
                        level, pl.ds(pl.multiple_of(place * share, share), share), j * rank : (j + 1) * rank
                    ]
                if level == 0:
                    start = rows + i * piece
                    ref[start : start + piece] = high[pl.ds(pl.multiple_of(place * piece, piece), piece)]
    send_a[rows + RING // 2 * piece :] = low[...]


def fourth(bits, c1, c2, c3, c2_there, c3_there, value, gram, low, high):
    rows, rank = c1.shape
    wide = 2 * rank
    extra = high.shape[0] // 2
    return local(
        fourth_body,
        bits,
        [c1, c2, c3, c2_there, c3_there, value, gram, low, high],
        [
            vmem(rows + extra, rank), vmem(rows + extra + low.shape[0], rank),
            vmem(rows, rank), vmem(rows, rank), vmem(rows, wide, dtype=jnp.bfloat16),
        ],
        12 * rows * rank * wide,
        16 * rows * wide,
        [pltpu.VMEM((2, rows, wide), jnp.float32)],
    )


def halve_body(steps, far, near, bits, keep, got, *refs):
    low, (out, send, *lows) = refs[: len(refs) // 3], refs[len(refs) // 3 :]
    rank = keep.shape[1]
    extra = 3 * rank // 8 * steps if low else 0
    rows = keep.shape[0] - extra
    count, piece = rows // (2 * steps), extra // (2 * steps)
    if steps == 2:
        mine, theirs = [bits[6], bits[6] ^ near], [bits[6] ^ far, bits[6] ^ far ^ near]
    else:
        mine, theirs = [0], [1]
    for ref, slots in ((out, mine), (send, theirs)):
        for i, slot in enumerate(slots):
            here = pl.ds(slot * count, count)
            ref[i * count : (i + 1) * count] = keep[here] + got[here]
            if low:
                there = pl.ds(rows + slot * piece, piece)
                start = len(slots) * count + i * piece
                ref[start : start + piece] = keep[there] + got[there]
    if low:
        done = low[0].shape[0]
        lows[0][:done] = low[0][...]
        lows[0][done:] = got[keep.shape[0] :]
        send[out.shape[0] :] = lows[0][...]


def halve(bits, steps, far, near, keep, got, *low):
    rank, size = keep.shape[1], keep.shape[0] // 2
    lows = [2 * v.shape[0] for v in low]
    return local(
        functools.partial(halve_body, steps, far, near),
        bits,
        [keep, got, *low],
        [vmem(size, rank), vmem(size + sum(lows), rank)] + [vmem(v, rank) for v in lows],
        2 * keep.size,
        20 * keep.size,
    )


def fourth_rows_body(bits, keep, got, low, own, other, gram, high):
    share, rank = own.shape
    rows = 2 * share
    total = keep[...] + got[: keep.shape[0]]
    choose(bits[2], total[:share], total[share:rows], own, other)
    high[...] = total[rows:]
    count = gram.shape[0] // RING
    half_list = low.shape[0]
    z0, z1, z2 = bits[0], bits[3], bits[5]
    for i, mask in enumerate((0, 1, 2, 3, 6, 7, 4, 5)):
        p0, p1, p2 = z0 ^ (mask & 1), z1 ^ (mask >> 1 & 1), z2 ^ (mask >> 2)
        place = pl.multiple_of((p0 * 4 + (p1 ^ p2) * 2 + p2) * count, count)
        for j in range(2):
            start = 2 * i * count + j * count
            if start < half_list:
                part = low[start : start + count]
            else:
                start += keep.shape[0] - half_list
                part = got[start : start + count]
            gram[pl.ds(place, count), j * rank : (j + 1) * rank] = part


def fourth_rows(bits, keep, got, low, share):
    rank = keep.shape[1]
    return local(
        fourth_rows_body,
        bits,
        [keep, got, low],
        [vmem(share, rank), vmem(share, rank), vmem(rank, 2 * rank), vmem(keep.shape[0] - 2 * share, rank)],
        2 * keep.size,
        20 * keep.size,
    )


def fifth_rows_body(bits, keep, got, fifth):
    share, rank = fifth.shape[0], keep.shape[1]
    for j in range(2):
        here = slice(j * share, (j + 1) * share)
        fifth[:, j * rank : (j + 1) * rank] = keep[here] + got[here]


def sixth_body(bits, c1, c23, packed, value, gram, keep, send, coef):
    rank = c1.shape[1]
    share = c1.shape[0] // packed.shape[0]
    for j in range(2):
        coef[:, j * rank : (j + 1) * rank] = (
            packed[:, j * share : (j + 1) * share, :].reshape(c1.shape).astype(jnp.bfloat16)
        )
    lhs = jnp.concatenate([c1[...], c23[...], coef[...]], axis=1)
    emit_halves(bits[1], [value[i] - dot(lhs, gram[i]) for i in range(3)], keep, send)


def sixth(bits, c1, c23, packed, value, gram):
    rows, rank = c1.shape
    wide = 2 * rank
    return local(
        sixth_body,
        bits,
        [c1, c23, packed, value, gram],
        [vmem(rows // 2, 3 * wide)] * 2 + [vmem(rows, wide, dtype=jnp.bfloat16)],
        30 * rows * rank * wide,
        24 * rows * wide,
    )


def add_body(bits, left, right, out):
    out[...] = left[...] + right[...]


def add(bits, left, right):
    return local(add_body, bits, [left, right], [vmem(*left.shape)], left.size, 12 * left.size)[0]


def total_body(bits, parts, out):
    out[...] = parts[...].sum(axis=0)


def total(bits, parts):
    return local(total_body, bits, [parts], [vmem(*parts.shape[1:])], parts.size, 4 * parts.size)[0]


def lower_body(bits, state, c1, c23, c45, up, out):
    coef = jnp.concatenate([c1[...], c23[...], c45[...]], axis=1)
    depth, leaf = coef.shape[1], state.shape[1]
    width = leaf // STEPS
    for i in range(STEPS):
        here = slice(i * width, (i + 1) * width)
        basis = up[: depth // c1.shape[1], :, here].reshape(depth, width)
        out[:, here] = state[:, here].astype(jnp.float32) - dot(coef, basis)


def lower(bits, state, c1, c23, c45, up_basis):
    rows, leaf = state.shape
    return local(
        lower_body,
        bits,
        [state, c1, c23, c45, up_basis],
        [vmem(rows, leaf)],
        10 * rows * leaf * c1.shape[1],
        6 * rows * leaf,
    )[0]


def last_body(bits, state, mine, received, up, out, coef, block, done):
    rank, count = up.shape[1], mine.shape[0]
    for bit in range(2):

        @pl.when(bits[1] == bit)
        def _(bit=bit):
            here = slice(bit * count, (bit + 1) * count)
            there = slice((1 - bit) * count, (2 - bit) * count)
            coef[here, :] = mine[:, : 3 * rank].astype(jnp.bfloat16)
            coef[there, :rank] = received[:, 2 * rank :].astype(jnp.bfloat16)
            coef[there, rank:] = received[:, : 2 * rank].astype(jnp.bfloat16)

    basis = up[5:8].reshape(3 * rank, up.shape[2])
    share = state.shape[0] // STEPS
    copies = []
    for i in range(STEPS):
        here = pl.ds(i * share, share)
        block[here] = state[here] - dot(coef[here], basis)
        copies.append(pltpu.make_async_copy(block.at[here], out.at[here], done.at[i]))
        copies[-1].start()
    for copy in copies:
        copy.wait()


def last(bits, state, mine, received, up_basis):
    rows, leaf = state.shape
    rank = up_basis.shape[1]
    args = [pltpu.with_memory_space_constraint(a, pltpu.VMEM) for a in (state, mine, received, up_basis)]
    return pl.pallas_call(
        last_body,
        out_shape=f32(rows, leaf),
        in_specs=[pl.BlockSpec(memory_space=pltpu.SMEM)] + [pl.BlockSpec(memory_space=pltpu.VMEM)] * 4,
        out_specs=pl.BlockSpec(memory_space=pltpu.HBM),
        scratch_shapes=[
            pltpu.VMEM((rows, 3 * rank), jnp.bfloat16),
            pltpu.VMEM((rows, leaf), jnp.float32),
            pltpu.SemaphoreType.DMA((STEPS,)),
        ],
        compiler_params=pltpu.CompilerParams(vmem_limit_bytes=VMEM_BYTES),
        cost_estimate=pl.CostEstimate(
            flops=6 * rows * leaf * rank, bytes_accessed=6 * rows * leaf, transcendentals=0
        ),
    )(bits, *args)


def shards(groups_z, groups_zy, rhs, leaf_inverse, up_basis, projection):
    size_x, size_y = lax.axis_size("gx"), lax.axis_size("gy")
    rows = rhs.shape[0]
    rank = up_basis.shape[1]
    wide = 2 * rank
    gx, gy = lax.axis_index("gx"), lax.axis_index("gy")
    z0, z1, z2, y0, y1 = (gx >> i & 1 for i in range(5))
    core, x0, x1 = (gy >> i & 1 for i in range(3))
    bits = jnp.stack([z0, core, y0, z1, z1 ^ z2, z2, z1 + 2 * z2])
    over_x = functools.partial(swap, axis="gx", size=size_x)
    over_y = functools.partial(swap, axis="gy", size=size_y)
    ring = RING
    share = rows // ring
    by_y01, by_y1 = starts(y0 ^ y1, 3 * rank // 2), starts(y1, 3 * rank // 4)
    half_y1 = starts(y1, rank)
    half_core, half_x0, half_x1 = starts(core, rank), starts(x0, rank), starts(x1, rank)
    indices = (
        bits, by_y01, by_y1, half_y1,
        half_core, half_x0, half_x1, y1 == 0, (y0 ^ y1) == 0,
    )
    indices, rhs = lax.optimization_barrier((indices, rhs))
    (
        bits, by_y01, by_y1, half_y1,
        half_core, half_x0, half_x1, first_y1, first_y01,
    ) = indices

    state, own, other = leaf_solve(bits, rhs, leaf_inverse, projection)
    received = over_x(other, mask=1)
    value, gram, kept = project((2, 3), ((2, 3),), bits, state, up_basis, projection)
    value_45, gram_45, kept_45 = project((4, 5), ((4, 5),), bits, state, up_basis, projection)

    value_678, gram_678, kept_678 = project((6, 7, 8), ((6, 7), (6, 8), (7, 8)), bits, state, up_basis, projection)
    received, kept, kept_45, kept_678 = lax.optimization_barrier((received, kept, kept_45, kept_678))

    keep, send, c1 = second(bits, own, received, value, gram, kept, kept_45)
    received = over_x(send, mask=1)
    high, high_send = split(kept_678.reshape(3 * rank, wide), by_y01)
    high, high_send = split(high + over_x(high_send, mask=8), by_y1)
    high = high + over_x(high_send, mask=24)
    high = jnp.concatenate([high[:, :rank], high[:, rank:]])

    received, high = lax.optimization_barrier((received, high))
    own, send, low, left, gram_23 = third(bits, keep, received, rank)
    c2, own, send, low = correct(bits, own, over_x(send, mask=2), low, left, gram_23)
    received = over_x(send, mask=6)
    c3, low = own + received[: rows // 2], low + received[rows // 2 :]
    c3 = c3 + over_x(c3, mask=2)
    c2_there = over_x(c2, mask=1)
    c3_there = over_x(c3, mask=1)

    keep_a, send_a, keep_b, send_b, c23 = fourth(bits, c1, c2, c3, c2_there, c3_there, value_45, gram_45, low, high)
    turned = [(i & -RING) + ((i + 1 if i & 1 else i - 1) % RING) for i in range(size_x)]
    got_a, got_b = over_x(send_a, mask=1), lax.ppermute(send_b, "gx", list(enumerate(turned)))
    keep_a, send_a, low = halve(bits, 2, 1, 3, keep_a, got_a, low)
    got_a = over_x(send_a, mask=2)
    keep_b, send_b = halve(bits, 2, 3, 1, keep_b, got_b)
    got_b = over_x(send_b, mask=6)
    keep_a, send_a, low = halve(bits, 1, 0, 0, keep_a, got_a, low)
    got_a = over_x(send_a, mask=6)
    keep_b, send_b = halve(bits, 1, 0, 0, keep_b, got_b)
    got_b = over_x(send_b, mask=2)
    own, other, gram_45, high = fourth_rows(bits, keep_a, got_a, low, share)
    c4 = own + over_x(other, mask=8)
    left = local(fifth_rows_body, bits, [keep_b, got_b], [vmem(share, wide)], keep_b.size, 12 * keep_b.size)[0]
    left = left - dot(c4, gram_45)
    received = over_x(jnp.concatenate([half(left, half_y1[1]), high]), mask=24)
    c5 = half(left, half_y1[0]) + received[:share]
    high = join(high, received[share:], first_y1)
    received = over_x(jnp.concatenate([c5, high]), mask=8)
    c5 = c5 + received[:share]
    high = join(high, received[share:], first_y01)
    packed = jnp.concatenate([c4, c5, high], axis=0)
    packed = exchange(jnp.broadcast_to(packed, (ring, *packed.shape)), groups_z)

    keep, send, c45 = sixth(bits, c1, c23, packed, value_678, gram_678)
    left = add(bits, keep, over_y(send, mask=1))
    high = packed[:, 2 * share :].reshape(2, ring // 2, 4, 3 * rank // (2 * ring), rank)
    high = jnp.concatenate(list(high.transpose(0, 2, 1, 3, 4).reshape(2, 3 * rank, rank)), axis=1)
    high_there = over_y(high, mask=1)
    left, high, high_there = lax.optimization_barrier((left, high, high_there))
    half_rows = rows // 2
    count = half_rows // size_x
    left = total(bits, exchange(left.reshape(size_x, count, 3 * wide), groups_zy))
    left, c45 = lax.optimization_barrier((left, c45))
    high, high_there = high.reshape(3, rank, wide), high_there.reshape(3, rank, wide)
    c6, c6_there = half(left[:, :wide], half_core[0]), half(left[:, :wide], half_core[1])
    z7 = left[:, wide : 2 * wide] - exact_dot(c6, high[0]) - exact_dot(c6_there, high_there[0])
    z8 = left[:, 2 * wide :] - exact_dot(c6, high[1]) - exact_dot(c6_there, high_there[1])
    c7 = half(z7, half_x0[0]) + over_y(half(z7, half_x0[1]), mask=2)
    z8 = z8 - exact_dot(c7, high[2] + high_there[2])
    c8 = half(z8, half_x1[0]) + over_y(half(z8, half_x1[1]), mask=6)
    c8 = c8 + over_y(c8, mask=2)
    state = lower(bits, state, c1, c23, c45, up_basis)
    packed = jnp.concatenate([c6, c7, c8, c6_there], axis=1)
    packed, state = lax.optimization_barrier((packed, state))
    packed = exchange(jnp.broadcast_to(packed, (size_x, *packed.shape)), groups_zy)
    packed = packed.reshape(half_rows, 4 * rank)
    received = over_y(packed[:, rank:], mask=1)
    return last(bits, state, packed, received, up_basis)


def solution(mesh):
    size_x, size_y = mesh.shape["gx"], mesh.shape["gy"]
    ring = RING
    groups_z = [
        [gy * size_x + start + i for i in range(ring)]
        for gy in range(size_y)
        for start in range(0, size_x, ring)
    ]
    groups_zy = [[gy * size_x + i for i in range(size_x)] for gy in range(size_y)]
    return jax.shard_map(
        functools.partial(shards, groups_z, groups_zy),
        mesh=mesh,
        in_specs=(
            P(None, ("gy", "gx")),
            P(("gy", "gx"), None, None),
            P(None, None, ("gy", "gx")),
            P(None, None, ("gy", "gx")),
        ),
        out_specs=P(None, ("gy", "gx")),
        check_vma=False,
    )
```

```python
import functools

import jax
import jax.numpy as jnp
from jax import lax
from jax.experimental import pallas as pl
from jax.experimental.pallas import tpu as pltpu
from jax.sharding import PartitionSpec as P

AXES = ("gy", "gx")
STEPS = 4
RING = 8
VMEM_BYTES = 16 * 1024 * 1024


def dot(a, b):
    return jnp.dot(a, b, preferred_element_type=jnp.float32)


def dot_t(a, b):
    return lax.dot_general(a, b, (((1,), (1,)), ((), ())), preferred_element_type=jnp.float32)


def exact_dot(a, b):
    return jnp.dot(a, b, precision=lax.Precision.HIGHEST, preferred_element_type=jnp.float32)


def swap(value, axis, mask, size):
    return lax.ppermute(value, axis, [(source, source ^ mask) for source in range(size)])


def exchange(value, groups):
    return lax.all_to_all(value, AXES, 0, 0, tiled=True, axis_index_groups=groups)


def half(value, start):
    return lax.dynamic_slice_in_dim(value, start, value.shape[-1] // 2, value.ndim - 1)


def split(value, starts):
    count = value.shape[0] // 2
    return tuple(lax.dynamic_slice_in_dim(value, start, count, 0) for start in starts)


def join(mine, other, first):
    return jnp.where(first, jnp.concatenate([mine, other]), jnp.concatenate([other, mine]))


def starts(bit, count):
    return (bit * count).astype(jnp.uint32), ((1 - bit) * count).astype(jnp.uint32)


def hbm(value):
    return pltpu.with_memory_space_constraint(value, pltpu.HBM)


def whole(shape):
    return pl.BlockSpec(shape, lambda j, bits: (0,) * len(shape))


def block(shape, *index):
    return pl.BlockSpec(shape, lambda j, bits: index)


def columns(rows, width):
    return pl.BlockSpec((rows, width), lambda j, bits: (0, j))


def run(body, steps, bits, args, in_specs, out_shape, out_specs, scratch, flops, nbytes):
    return pl.pallas_call(
        body,
        out_shape=out_shape,
        grid_spec=pltpu.PrefetchScalarGridSpec(
            num_scalar_prefetch=1,
            grid=(steps,),
            in_specs=in_specs,
            out_specs=out_specs,
            scratch_shapes=scratch,
        ),
        compiler_params=pltpu.CompilerParams(
            dimension_semantics=("arbitrary",), vmem_limit_bytes=VMEM_BYTES
        ),
        cost_estimate=pl.CostEstimate(flops=flops, bytes_accessed=nbytes, transcendentals=0),
    )(bits, *args)


def f32(*shape):
    return jax.ShapeDtypeStruct(shape, jnp.float32)


def bf16(*shape):
    return jax.ShapeDtypeStruct(shape, jnp.bfloat16)


def vmem(*shape, dtype=jnp.float32):
    return pltpu.VMEM(shape, dtype)


def local(body, bits, args, outs, flops, nbytes, scratch=()):
    args = [pltpu.with_memory_space_constraint(a, pltpu.VMEM) for a in args]
    return pl.pallas_call(
        body,
        out_shape=outs,
        in_specs=[pl.BlockSpec(memory_space=pltpu.SMEM)]
        + [pl.BlockSpec(memory_space=pltpu.VMEM)] * len(args),
        out_specs=[pl.BlockSpec(memory_space=pltpu.VMEM)] * len(outs),
        scratch_shapes=scratch,
        compiler_params=pltpu.CompilerParams(vmem_limit_bytes=VMEM_BYTES),
        cost_estimate=pl.CostEstimate(flops=flops, bytes_accessed=nbytes, transcendentals=0),
    )(bits, *args)


def leaf_body(bits, rhs, inverse, own_rows, other_rows, state, own, other, sums):
    rank = own.shape[1]
    rounded = dot(rhs[...], inverse[...]).astype(jnp.bfloat16)
    state[...] = rounded
    part = dot_t(rounded, jnp.concatenate([own_rows[...], other_rows[...]], axis=0))

    @pl.when(pl.program_id(0) == 0)
    def _():
        sums[...] = part

    @pl.when(pl.program_id(0) > 0)
    def _():
        sums[...] += part

    @pl.when(pl.program_id(0) == STEPS - 1)
    def _():
        own[...] = sums[:, :rank]
        other[...] = sums[:, rank:]


def leaf_solve(bits, rhs, leaf_inverse, projection):
    rows, leaf = rhs.shape
    rank = projection.shape[1] // 2
    width = leaf // STEPS
    return run(
        leaf_body,
        STEPS,
        bits,
        [hbm(rhs), hbm(leaf_inverse), hbm(projection), hbm(projection)],
        [
            whole((rows, leaf)),
            pl.BlockSpec((None, leaf, width), lambda j, bits: (0, 0, j)),
            pl.BlockSpec((None, rank, width), lambda j, bits: (0, bits[0], j)),
            pl.BlockSpec((None, rank, width), lambda j, bits: (0, 1 - bits[0], j)),
        ],
        [vmem(rows, leaf, dtype=jnp.bfloat16), vmem(rows, rank), vmem(rows, rank)],
        [columns(rows, width), whole((rows, rank)), whole((rows, rank))],
        [pltpu.VMEM((rows, 2 * rank), jnp.float32)],
        2 * rows * leaf * (leaf + 2 * rank),
        leaf * (4 * rows + 2 * leaf),
    )


def project_body(heights, depth, pairs, bits, state, up, proj, value, gram, *kept):
    rank = up.shape[1]
    for i, h in enumerate(heights):
        rows = proj[h - 1]
        value[i] = dot_t(state[...], rows)
        gram[i] = dot_t(up[:depth].reshape(depth * rank, up.shape[2]), rows).astype(jnp.bfloat16)
        for j, (k, of) in enumerate(pairs):
            if of == h:
                kept[0][j] = dot_t(up[k - 1], rows)


def project(heights, pairs, bits, state, up_basis, projection):
    rows, leaf = state.shape
    rank = up_basis.shape[1]
    wide, count, depth = 2 * rank, len(heights), heights[0] - 1
    return local(
        functools.partial(project_body, heights, depth, pairs),
        bits,
        [state, up_basis, projection],
        [vmem(count, rows, wide), vmem(count, depth * rank, wide, dtype=jnp.bfloat16)]
        + ([vmem(len(pairs), rank, wide)] if pairs else []),
        2 * leaf * wide * (count * (rows + rank * depth) + rank * len(pairs)),
        2 * leaf * (rows + count * 3 * rank),
    )


def emit_halves(which, parts, keep, send):
    count, wide = parts[0].shape[0] // 2, parts[0].shape[1]
    for bit in range(2):

        @pl.when(which == bit)
        def _(bit=bit):
            for i, part in enumerate(parts):
                keep[:count, i * wide : (i + 1) * wide] = part[bit * count : (bit + 1) * count]
                send[:count, i * wide : (i + 1) * wide] = part[(1 - bit) * count : (2 - bit) * count]


def second_body(bits, mine, received, value, gram, pair, ring, keep_2, send_2, keep_3, send_3, coef):
    c1 = (mine[...] + received[...]).astype(jnp.bfloat16)
    coef[...] = c1
    rows, count = keep_2.shape[0] - pair.shape[1] // 2, pair.shape[1] // 2
    emit_halves(bits[0], [value[0] - dot(c1, gram[0])], keep_2, send_2)
    emit_halves(bits[0], [value[1] - dot(c1, gram[1])], keep_3, send_3)
    for ref in (keep_3, send_3):
        ref[rows:] = pair[0]
    for ref, which in ((keep_2, bits[0]), (send_2, 1 - bits[0])):
        ref[rows:] = ring[0, pl.ds(pl.multiple_of(which * count, count), count)]


def second(bits, mine, received, value, gram, pair, ring):
    rows, rank = mine.shape
    wide = 2 * rank
    return local(
        second_body,
        bits,
        [mine, received, value, gram, pair, ring],
        [vmem((rows + rank) // 2, wide)] * 2 + [vmem(rows // 2 + rank, wide)] * 2 + [vmem(rows, rank, dtype=jnp.bfloat16)],
        4 * rows * rank * wide,
        16 * rows * wide,
    )


def choose(bit, left, right, keep, send):
    for b in range(2):

        @pl.when(bit == b)
        def _(b=b):
            keep[...] = (left, right)[b]
            send[...] = (left, right)[1 - b]


def stack(value, rank):
    return jnp.concatenate([value[:, :rank], value[:, rank:]], axis=0)


def third_body(bits, keep, received, own, send, low):
    total = keep[...] + received[...]
    rows, rank = own.shape
    count = low.shape[0] // 2
    choose(bits[3], total[:rows, :rank], total[:rows, rank:], own, send.at[:rows])
    choose(bits[4], stack(total[rows : rows + count], rank), stack(total[rows + count :], rank), low, send.at[rows:])


def third(bits, keep, received):
    rank = keep.shape[1] // 2
    rows = keep.shape[0] - rank // 2
    return local(
        third_body,
        bits,
        [keep, received],
        [vmem(rows, rank), vmem(rows + rank // 2, rank), vmem(rank // 2, rank)],
        keep.size,
        12 * keep.size,
    )


def correct_body(bits, own, received, low, keep, left, coef, mine, send, kept):
    rows, rank = own.shape
    count = low.shape[0] // 4
    c2 = own[...] + received[:rows]
    coef[...] = c2
    total = keep[...] + left[...]
    rest = total[:rows] - dot(c2.astype(jnp.bfloat16), total[rows:].astype(jnp.bfloat16))
    choose(bits[5], rest[:, :rank], rest[:, rank:], mine, send.at[:rows])
    total = low[...] + received[rows:]
    parts = [jnp.concatenate([total[i * count : (i + 1) * count], total[(i + 2) * count : (i + 3) * count]]) for i in range(2)]
    choose(bits[5], parts[0], parts[1], kept, send.at[rows:])


def correct(bits, own, received, low, keep, left):
    rows, rank = own.shape
    return local(
        correct_body,
        bits,
        [own, received, low, keep, left],
        [vmem(rows, rank), vmem(rows, rank), vmem(rows + rank // 4, rank), vmem(rank // 4, rank)],
        4 * rows * rank * rank,
        20 * rows * rank,
    )


def fourth_body(bits, c1, c2, c3, c2_there, c3_there, value, gram, low, high, keep_a, send_a, keep_b, send_b, coef, sums):
    count, rank = c2.shape
    for bit in range(2):

        @pl.when(bits[0] == bit)
        def _(bit=bit):
            for j, (mine, received) in enumerate(((c2, c2_there), (c3, c3_there))):
                here = slice(j * rank, (j + 1) * rank)
                coef[bit * count : (bit + 1) * count, here] = mine[...].astype(jnp.bfloat16)
                coef[(1 - bit) * count : (2 - bit) * count, here] = received[...].astype(jnp.bfloat16)

    rows, wide = value.shape[1:]
    share = rows // RING
    piece = high.shape[0] // RING
    lhs = jnp.concatenate([c1[...], coef[...]], axis=1)
    for i in range(2):
        sums[i] = value[i] - dot(lhs, gram[i])
    for keep, send, level in ((keep_a, send_a, 0), (keep_b, send_b, 1)):
        for ref, parity in ((keep, bits[0]), (send, 1 - bits[0])):
            for i in range(RING // 2):
                place = 2 * i + parity
                for j in range(2):
                    start = (2 * i + j) * share
                    ref[start : start + share] = sums[
                        level, pl.ds(pl.multiple_of(place * share, share), share), j * rank : (j + 1) * rank
                    ]
                if level == 0:
                    start = rows + i * piece
                    ref[start : start + piece] = high[pl.ds(pl.multiple_of(place * piece, piece), piece)]
    send_a[rows + RING // 2 * piece :] = low[...]


def fourth(bits, c1, c2, c3, c2_there, c3_there, value, gram, low, high):
    rows, rank = c1.shape
    wide = 2 * rank
    extra = high.shape[0] // 2
    return local(
        fourth_body,
        bits,
        [c1, c2, c3, c2_there, c3_there, value, gram, low, high],
        [
            vmem(rows + extra, rank), vmem(rows + extra + low.shape[0], rank),
            vmem(rows, rank), vmem(rows, rank), vmem(rows, wide, dtype=jnp.bfloat16),
        ],
        12 * rows * rank * wide,
        16 * rows * wide,
        [pltpu.VMEM((2, rows, wide), jnp.float32)],
    )


def halve_body(steps, far, near, bits, keep, got, *refs):
    low, (out, send, *lows) = refs[: len(refs) // 3], refs[len(refs) // 3 :]
    rank = keep.shape[1]
    extra = 3 * rank // 8 * steps if low else 0
    rows = keep.shape[0] - extra
    count, piece = rows // (2 * steps), extra // (2 * steps)
    if steps == 2:
        mine, theirs = [bits[6], bits[6] ^ near], [bits[6] ^ far, bits[6] ^ far ^ near]
    else:
        mine, theirs = [0], [1]
    for ref, slots in ((out, mine), (send, theirs)):
        for i, slot in enumerate(slots):
            here = pl.ds(slot * count, count)
            ref[i * count : (i + 1) * count] = keep[here] + got[here]
            if low:
                there = pl.ds(rows + slot * piece, piece)
                start = len(slots) * count + i * piece
                ref[start : start + piece] = keep[there] + got[there]
    if low:
        done = low[0].shape[0]
        lows[0][:done] = low[0][...]
        lows[0][done:] = got[keep.shape[0] :]
        send[out.shape[0] :] = lows[0][...]


def halve(bits, steps, far, near, keep, got, *low):
    rank, size = keep.shape[1], keep.shape[0] // 2
    lows = [2 * v.shape[0] for v in low]
    return local(
        functools.partial(halve_body, steps, far, near),
        bits,
        [keep, got, *low],
        [vmem(size, rank), vmem(size + sum(lows), rank)] + [vmem(v, rank) for v in lows],
        2 * keep.size,
        20 * keep.size,
    )


def fourth_rows_body(bits, keep, got, low, own, other, gram, high):
    share, rank = own.shape
    rows = 2 * share
    total = keep[...] + got[: keep.shape[0]]
    choose(bits[2], total[:share], total[share:rows], own, other)
    high[...] = total[rows:]
    count = gram.shape[0] // RING
    half_list = low.shape[0]
    z0, z1, z2 = bits[0], bits[3], bits[5]
    for i, mask in enumerate((0, 1, 2, 3, 6, 7, 4, 5)):
        p0, p1, p2 = z0 ^ (mask & 1), z1 ^ (mask >> 1 & 1), z2 ^ (mask >> 2)
        place = pl.multiple_of((p0 * 4 + (p1 ^ p2) * 2 + p2) * count, count)
        for j in range(2):
            start = 2 * i * count + j * count
            if start < half_list:
                part = low[start : start + count]
            else:
                start += keep.shape[0] - half_list
                part = got[start : start + count]
            gram[pl.ds(place, count), j * rank : (j + 1) * rank] = part


def fourth_rows(bits, keep, got, low, share):
    rank = keep.shape[1]
    return local(
        fourth_rows_body,
        bits,
        [keep, got, low],
        [vmem(share, rank), vmem(share, rank), vmem(rank, 2 * rank), vmem(keep.shape[0] - 2 * share, rank)],
        2 * keep.size,
        20 * keep.size,
    )


def fifth_rows_body(bits, keep, got, fifth):
    share, rank = fifth.shape[0], keep.shape[1]
    for j in range(2):
        here = slice(j * share, (j + 1) * share)
        fifth[:, j * rank : (j + 1) * rank] = keep[here] + got[here]


def sixth_body(bits, c1, c23, packed, value, gram, keep, send, coef):
    rank = c1.shape[1]
    share = c1.shape[0] // packed.shape[0]
    for j in range(2):
        coef[:, j * rank : (j + 1) * rank] = (
            packed[:, j * share : (j + 1) * share, :].reshape(c1.shape).astype(jnp.bfloat16)
        )
    lhs = jnp.concatenate([c1[...], c23[...], coef[...]], axis=1)
    emit_halves(bits[1], [value[i] - dot(lhs, gram[i]) for i in range(3)], keep, send)


def sixth(bits, c1, c23, packed, value, gram):
    rows, rank = c1.shape
    wide = 2 * rank
    return local(
        sixth_body,
        bits,
        [c1, c23, packed, value, gram],
        [vmem(rows // 2, 3 * wide)] * 2 + [vmem(rows, wide, dtype=jnp.bfloat16)],
        30 * rows * rank * wide,
        24 * rows * wide,
    )


def add_body(bits, left, right, out):
    out[...] = left[...] + right[...]


def add(bits, left, right):
    return local(add_body, bits, [left, right], [vmem(*left.shape)], left.size, 12 * left.size)[0]


def total_body(bits, parts, out):
    out[...] = parts[...].sum(axis=0)


def total(bits, parts):
    return local(total_body, bits, [parts], [vmem(*parts.shape[1:])], parts.size, 4 * parts.size)[0]


def lower_body(bits, state, c1, c23, c45, up, out):
    coef = jnp.concatenate([c1[...], c23[...], c45[...]], axis=1)
    depth, leaf = coef.shape[1], state.shape[1]
    width = leaf // STEPS
    for i in range(STEPS):
        here = slice(i * width, (i + 1) * width)
        basis = up[: depth // c1.shape[1], :, here].reshape(depth, width)
        out[:, here] = state[:, here].astype(jnp.float32) - dot(coef, basis)


def lower(bits, state, c1, c23, c45, up_basis):
    rows, leaf = state.shape
    return local(
        lower_body,
        bits,
        [state, c1, c23, c45, up_basis],
        [vmem(rows, leaf)],
        10 * rows * leaf * c1.shape[1],
        6 * rows * leaf,
    )[0]


def last_body(bits, state, mine, received, up, out, coef, block, done):
    rank, count = up.shape[1], mine.shape[0]
    for bit in range(2):

        @pl.when(bits[1] == bit)
        def _(bit=bit):
            here = slice(bit * count, (bit + 1) * count)
            there = slice((1 - bit) * count, (2 - bit) * count)
            coef[here, :] = mine[:, : 3 * rank].astype(jnp.bfloat16)
            coef[there, :rank] = received[:, 2 * rank :].astype(jnp.bfloat16)
            coef[there, rank:] = received[:, : 2 * rank].astype(jnp.bfloat16)

    basis = up[5:8].reshape(3 * rank, up.shape[2])
    share = state.shape[0] // STEPS
    copies = []
    for i in range(STEPS):
        here = pl.ds(i * share, share)
        block[here] = state[here] - dot(coef[here], basis)
        copies.append(pltpu.make_async_copy(block.at[here], out.at[here], done.at[i]))
        copies[-1].start()
    for copy in copies:
        copy.wait()


def last(bits, state, mine, received, up_basis):
    rows, leaf = state.shape
    rank = up_basis.shape[1]
    args = [pltpu.with_memory_space_constraint(a, pltpu.VMEM) for a in (state, mine, received, up_basis)]
    return pl.pallas_call(
        last_body,
        out_shape=f32(rows, leaf),
        in_specs=[pl.BlockSpec(memory_space=pltpu.SMEM)] + [pl.BlockSpec(memory_space=pltpu.VMEM)] * 4,
        out_specs=pl.BlockSpec(memory_space=pltpu.HBM),
        scratch_shapes=[
            pltpu.VMEM((rows, 3 * rank), jnp.bfloat16),
            pltpu.VMEM((rows, leaf), jnp.float32),
            pltpu.SemaphoreType.DMA((STEPS,)),
        ],
        compiler_params=pltpu.CompilerParams(vmem_limit_bytes=VMEM_BYTES),
        cost_estimate=pl.CostEstimate(
            flops=6 * rows * leaf * rank, bytes_accessed=6 * rows * leaf, transcendentals=0
        ),
    )(bits, *args)


def shards(groups_z, groups_zy, rhs, leaf_inverse, up_basis, projection):
    size_x, size_y = lax.axis_size("gx"), lax.axis_size("gy")
    rows = rhs.shape[0]
    rank = up_basis.shape[1]
    wide = 2 * rank
    gx, gy = lax.axis_index("gx"), lax.axis_index("gy")
    z0, z1, z2, y0, y1 = (gx >> i & 1 for i in range(5))
    core, x0, x1 = (gy >> i & 1 for i in range(3))
    bits = jnp.stack([z0, core, y0, z1, z1 ^ z2, z2, z1 + 2 * z2])
    over_x = functools.partial(swap, axis="gx", size=size_x)
    over_y = functools.partial(swap, axis="gy", size=size_y)
    ring = RING
    share = rows // ring
    by_y01, by_y1 = starts(y0 ^ y1, 3 * rank // 2), starts(y1, 3 * rank // 4)
    half_y1 = starts(y1, rank)
    half_core, half_x0, half_x1 = starts(core, rank), starts(x0, rank), starts(x1, rank)
    indices = (
        bits, by_y01, by_y1, half_y1,
        half_core, half_x0, half_x1, y1 == 0, (y0 ^ y1) == 0,
    )
    indices, rhs = lax.optimization_barrier((indices, rhs))
    (
        bits, by_y01, by_y1, half_y1,
        half_core, half_x0, half_x1, first_y1, first_y01,
    ) = indices

    state, own, other = leaf_solve(bits, rhs, leaf_inverse, projection)
    received = over_x(other, mask=1)
    value, gram, kept = project((2, 3), ((2, 3),), bits, state, up_basis, projection)
    value_45, gram_45, kept_45 = project((4, 5), ((4, 5),), bits, state, up_basis, projection)

    value_678, gram_678, kept_678 = project((6, 7, 8), ((6, 7), (6, 8), (7, 8)), bits, state, up_basis, projection)
    received, kept, kept_45, kept_678 = lax.optimization_barrier((received, kept, kept_45, kept_678))

    keep, send, keep_3, send_3, c1 = second(bits, own, received, value, gram, kept, kept_45)
    received = over_x(send, mask=1)
    left = over_x(send_3, mask=1)
    high, high_send = split(kept_678.reshape(3 * rank, wide), by_y01)
    high, high_send = split(high + over_x(high_send, mask=8), by_y1)
    high = high + over_x(high_send, mask=24)
    high = jnp.concatenate([high[:, :rank], high[:, rank:]])

    own, send, low = third(bits, keep, received)
    left, high = lax.optimization_barrier((left, high))
    c2, own, send, low = correct(bits, own, over_x(send, mask=2), low, keep_3, left)
    received = over_x(send, mask=6)
    c3, low = own + received[: rows // 2], low + received[rows // 2 :]
    c3 = c3 + over_x(c3, mask=2)
    c2_there = over_x(c2, mask=1)
    c3_there = over_x(c3, mask=1)

    keep_a, send_a, keep_b, send_b, c23 = fourth(bits, c1, c2, c3, c2_there, c3_there, value_45, gram_45, low, high)
    turned = [(i & -RING) + ((i + 1 if i & 1 else i - 1) % RING) for i in range(size_x)]
    got_a, got_b = over_x(send_a, mask=1), lax.ppermute(send_b, "gx", list(enumerate(turned)))
    keep_a, send_a, low = halve(bits, 2, 1, 3, keep_a, got_a, low)
    got_a = over_x(send_a, mask=2)
    keep_b, send_b = halve(bits, 2, 3, 1, keep_b, got_b)
    got_b = over_x(send_b, mask=6)
    keep_a, send_a, low = halve(bits, 1, 0, 0, keep_a, got_a, low)
    got_a = over_x(send_a, mask=6)
    keep_b, send_b = halve(bits, 1, 0, 0, keep_b, got_b)
    got_b = over_x(send_b, mask=2)
    own, other, gram_45, high = fourth_rows(bits, keep_a, got_a, low, share)
    c4 = own + over_x(other, mask=8)
    left = local(fifth_rows_body, bits, [keep_b, got_b], [vmem(share, wide)], keep_b.size, 12 * keep_b.size)[0]
    left = left - dot(c4, gram_45)
    received = over_x(jnp.concatenate([half(left, half_y1[1]), high]), mask=24)
    c5 = half(left, half_y1[0]) + received[:share]
    high = join(high, received[share:], first_y1)
    received = over_x(jnp.concatenate([c5, high]), mask=8)
    c5 = c5 + received[:share]
    high = join(high, received[share:], first_y01)
    packed = jnp.concatenate([c4, c5, high], axis=0)
    packed = exchange(jnp.broadcast_to(packed, (ring, *packed.shape)), groups_z)

    keep, send, c45 = sixth(bits, c1, c23, packed, value_678, gram_678)
    left = add(bits, keep, over_y(send, mask=1))
    high = packed[:, 2 * share :].reshape(2, ring // 2, 4, 3 * rank // (2 * ring), rank)
    high = jnp.concatenate(list(high.transpose(0, 2, 1, 3, 4).reshape(2, 3 * rank, rank)), axis=1)
    high_there = over_y(high, mask=1)
    left, high, high_there = lax.optimization_barrier((left, high, high_there))
    half_rows = rows // 2
    count = half_rows // size_x
    left = total(bits, exchange(left.reshape(size_x, count, 3 * wide), groups_zy))
    left, c45 = lax.optimization_barrier((left, c45))
    high, high_there = high.reshape(3, rank, wide), high_there.reshape(3, rank, wide)
    c6, c6_there = half(left[:, :wide], half_core[0]), half(left[:, :wide], half_core[1])
    z7 = left[:, wide : 2 * wide] - exact_dot(c6, high[0]) - exact_dot(c6_there, high_there[0])
    z8 = left[:, 2 * wide :] - exact_dot(c6, high[1]) - exact_dot(c6_there, high_there[1])
    c7 = half(z7, half_x0[0]) + over_y(half(z7, half_x0[1]), mask=2)
    z8 = z8 - exact_dot(c7, high[2] + high_there[2])
    c8 = half(z8, half_x1[0]) + over_y(half(z8, half_x1[1]), mask=6)
    c8 = c8 + over_y(c8, mask=2)
    state = lower(bits, state, c1, c23, c45, up_basis)
    packed = jnp.concatenate([c6, c7, c8, c6_there], axis=1)
    packed, state = lax.optimization_barrier((packed, state))
    packed = exchange(jnp.broadcast_to(packed, (size_x, *packed.shape)), groups_zy)
    packed = packed.reshape(half_rows, 4 * rank)
    received = over_y(packed[:, rank:], mask=1)
    return last(bits, state, packed, received, up_basis)


def solution(mesh):
    size_x, size_y = mesh.shape["gx"], mesh.shape["gy"]
    ring = RING
    groups_z = [
        [gy * size_x + start + i for i in range(ring)]
        for gy in range(size_y)
        for start in range(0, size_x, ring)
    ]
    groups_zy = [[gy * size_x + i for i in range(size_x)] for gy in range(size_y)]
    return jax.shard_map(
        functools.partial(shards, groups_z, groups_zy),
        mesh=mesh,
        in_specs=(
            P(None, ("gy", "gx")),
            P(("gy", "gx"), None, None),
            P(None, None, ("gy", "gx")),
            P(None, None, ("gy", "gx")),
        ),
        out_specs=P(None, ("gy", "gx")),
        check_vma=False,
    )
```

```python
import functools

import jax
import jax.numpy as jnp
from jax import lax
from jax.experimental import pallas as pl
from jax.experimental.pallas import tpu as pltpu
from jax.sharding import PartitionSpec as P

AXES = ("gy", "gx")
STEPS = 4
RING = 8
VMEM_BYTES = 16 * 1024 * 1024


def dot(a, b):
    return jnp.dot(a, b, preferred_element_type=jnp.float32)


def dot_t(a, b):
    return lax.dot_general(a, b, (((1,), (1,)), ((), ())), preferred_element_type=jnp.float32)


def exact_dot(a, b):
    return jnp.dot(a, b, precision=lax.Precision.HIGHEST, preferred_element_type=jnp.float32)


def swap(value, axis, mask, size):
    return lax.ppermute(value, axis, [(source, source ^ mask) for source in range(size)])


def exchange(value, groups):
    return lax.all_to_all(value, AXES, 0, 0, tiled=True, axis_index_groups=groups)


def half(value, start):
    return lax.dynamic_slice_in_dim(value, start, value.shape[-1] // 2, value.ndim - 1)


def split(value, starts):
    count = value.shape[0] // 2
    return tuple(lax.dynamic_slice_in_dim(value, start, count, 0) for start in starts)


def join(mine, other, first):
    return jnp.where(first, jnp.concatenate([mine, other]), jnp.concatenate([other, mine]))


def starts(bit, count):
    return (bit * count).astype(jnp.uint32), ((1 - bit) * count).astype(jnp.uint32)


def hbm(value):
    return pltpu.with_memory_space_constraint(value, pltpu.HBM)


def whole(shape):
    return pl.BlockSpec(shape, lambda j, bits: (0,) * len(shape))


def block(shape, *index):
    return pl.BlockSpec(shape, lambda j, bits: index)


def columns(rows, width):
    return pl.BlockSpec((rows, width), lambda j, bits: (0, j))


def run(body, steps, bits, args, in_specs, out_shape, out_specs, scratch, flops, nbytes):
    return pl.pallas_call(
        body,
        out_shape=out_shape,
        grid_spec=pltpu.PrefetchScalarGridSpec(
            num_scalar_prefetch=1,
            grid=(steps,),
            in_specs=in_specs,
            out_specs=out_specs,
            scratch_shapes=scratch,
        ),
        compiler_params=pltpu.CompilerParams(
            dimension_semantics=("arbitrary",), vmem_limit_bytes=VMEM_BYTES
        ),
        cost_estimate=pl.CostEstimate(flops=flops, bytes_accessed=nbytes, transcendentals=0),
    )(bits, *args)


def f32(*shape):
    return jax.ShapeDtypeStruct(shape, jnp.float32)


def bf16(*shape):
    return jax.ShapeDtypeStruct(shape, jnp.bfloat16)


def vmem(*shape, dtype=jnp.float32):
    return pltpu.VMEM(shape, dtype)


def local(body, bits, args, outs, flops, nbytes, scratch=()):
    args = [pltpu.with_memory_space_constraint(a, pltpu.VMEM) for a in args]
    return pl.pallas_call(
        body,
        out_shape=outs,
        in_specs=[pl.BlockSpec(memory_space=pltpu.SMEM)]
        + [pl.BlockSpec(memory_space=pltpu.VMEM)] * len(args),
        out_specs=[pl.BlockSpec(memory_space=pltpu.VMEM)] * len(outs),
        scratch_shapes=scratch,
        compiler_params=pltpu.CompilerParams(vmem_limit_bytes=VMEM_BYTES),
        cost_estimate=pl.CostEstimate(flops=flops, bytes_accessed=nbytes, transcendentals=0),
    )(bits, *args)


def leaf_body(bits, rhs, inverse, own_rows, other_rows, state, own, other, sums):
    rank = own.shape[1]
    rounded = dot(rhs[...], inverse[...]).astype(jnp.bfloat16)
    state[...] = rounded
    part = dot_t(rounded, jnp.concatenate([own_rows[...], other_rows[...]], axis=0))

    @pl.when(pl.program_id(0) == 0)
    def _():
        sums[...] = part

    @pl.when(pl.program_id(0) > 0)
    def _():
        sums[...] += part

    @pl.when(pl.program_id(0) == STEPS - 1)
    def _():
        own[...] = sums[:, :rank]
        other[...] = sums[:, rank:]


def leaf_solve(bits, rhs, leaf_inverse, projection):
    rows, leaf = rhs.shape
    rank = projection.shape[1] // 2
    width = leaf // STEPS
    return run(
        leaf_body,
        STEPS,
        bits,
        [hbm(rhs), hbm(leaf_inverse), hbm(projection), hbm(projection)],
        [
            whole((rows, leaf)),
            pl.BlockSpec((None, leaf, width), lambda j, bits: (0, 0, j)),
            pl.BlockSpec((None, rank, width), lambda j, bits: (0, bits[0], j)),
            pl.BlockSpec((None, rank, width), lambda j, bits: (0, 1 - bits[0], j)),
        ],
        [vmem(rows, leaf, dtype=jnp.bfloat16), vmem(rows, rank), vmem(rows, rank)],
        [columns(rows, width), whole((rows, rank)), whole((rows, rank))],
        [pltpu.VMEM((rows, 2 * rank), jnp.float32)],
        2 * rows * leaf * (leaf + 2 * rank),
        leaf * (4 * rows + 2 * leaf),
    )


def project_body(heights, depth, pairs, bits, state, up, proj, value, gram, *kept):
    rank = up.shape[1]
    for i, h in enumerate(heights):
        rows = proj[h - 1]
        value[i] = dot_t(state[...], rows)
        gram[i] = dot_t(up[:depth].reshape(depth * rank, up.shape[2]), rows).astype(jnp.bfloat16)
        for j, (k, of) in enumerate(pairs):
            if of == h:
                kept[0][j] = dot_t(up[k - 1], rows)


def project(heights, pairs, bits, state, up_basis, projection):
    rows, leaf = state.shape
    rank = up_basis.shape[1]
    wide, count, depth = 2 * rank, len(heights), heights[0] - 1
    return local(
        functools.partial(project_body, heights, depth, pairs),
        bits,
        [state, up_basis, projection],
        [vmem(count, rows, wide), vmem(count, depth * rank, wide, dtype=jnp.bfloat16)]
        + ([vmem(len(pairs), rank, wide)] if pairs else []),
        2 * leaf * wide * (count * (rows + rank * depth) + rank * len(pairs)),
        2 * leaf * (rows + count * 3 * rank),
    )


def emit_halves(which, parts, keep, send):
    count, wide = parts[0].shape[0] // 2, parts[0].shape[1]
    for bit in range(2):

        @pl.when(which == bit)
        def _(bit=bit):
            for i, part in enumerate(parts):
                keep[:count, i * wide : (i + 1) * wide] = part[bit * count : (bit + 1) * count]
                send[:count, i * wide : (i + 1) * wide] = part[(1 - bit) * count : (2 - bit) * count]


def second_body(bits, mine, received, value, gram, pair, ring, keep_2, send_2, keep_3, send_3, coef):
    c1 = (mine[...] + received[...]).astype(jnp.bfloat16)
    coef[...] = c1
    rows, count = keep_2.shape[0] - pair.shape[1] // 2, pair.shape[1] // 2
    emit_halves(bits[0], [value[0] - dot(c1, gram[0])], keep_2, send_2)
    emit_halves(bits[0], [value[1] - dot(c1, gram[1])], keep_3, send_3)
    for ref in (keep_3, send_3):
        ref[rows:] = pair[0]
    for ref, which in ((keep_2, bits[0]), (send_2, 1 - bits[0])):
        ref[rows:] = ring[0, pl.ds(pl.multiple_of(which * count, count), count)]


def second(bits, mine, received, value, gram, pair, ring):
    rows, rank = mine.shape
    wide = 2 * rank
    return local(
        second_body,
        bits,
        [mine, received, value, gram, pair, ring],
        [vmem((rows + rank) // 2, wide)] * 2 + [vmem(rows // 2 + rank, wide)] * 2 + [vmem(rows, rank, dtype=jnp.bfloat16)],
        4 * rows * rank * wide,
        16 * rows * wide,
    )


def choose(bit, left, right, keep, send):
    for b in range(2):

        @pl.when(bit == b)
        def _(b=b):
            keep[...] = (left, right)[b]
            send[...] = (left, right)[1 - b]


def stack(value, rank):
    return jnp.concatenate([value[:, :rank], value[:, rank:]], axis=0)


def third_body(bits, keep, received, own, send, low):
    total = keep[...] + received[...]
    rows, rank = own.shape
    count = low.shape[0] // 2
    choose(bits[3], total[:rows, :rank], total[:rows, rank:], own, send.at[:rows])
    choose(bits[4], stack(total[rows : rows + count], rank), stack(total[rows + count :], rank), low, send.at[rows:])


def third(bits, keep, received):
    rank = keep.shape[1] // 2
    rows = keep.shape[0] - rank // 2
    return local(
        third_body,
        bits,
        [keep, received],
        [vmem(rows, rank), vmem(rows + rank // 2, rank), vmem(rank // 2, rank)],
        keep.size,
        12 * keep.size,
    )


def correct_body(bits, own, received, low, keep, left, coef, mine, send, kept):
    rows, rank = own.shape
    count = low.shape[0] // 4
    c2 = own[...] + received[:rows]
    coef[...] = c2
    total = keep[...] + left[...]
    rest = total[:rows] - dot(c2.astype(jnp.bfloat16), total[rows:].astype(jnp.bfloat16))
    choose(bits[5], rest[:, :rank], rest[:, rank:], mine, send.at[:rows])
    total = low[...] + received[rows:]
    parts = [jnp.concatenate([total[i * count : (i + 1) * count], total[(i + 2) * count : (i + 3) * count]]) for i in range(2)]
    choose(bits[5], parts[0], parts[1], kept, send.at[rows:])


def correct(bits, own, received, low, keep, left):
    rows, rank = own.shape
    return local(
        correct_body,
        bits,
        [own, received, low, keep, left],
        [vmem(rows, rank), vmem(rows, rank), vmem(rows + rank // 4, rank), vmem(rank // 4, rank)],
        4 * rows * rank * rank,
        20 * rows * rank,
    )


def fourth_body(bits, c1, c2, c3, c2_there, c3_there, value, gram, low, high, keep, send, coef, sums):
    count, rank = c2.shape
    for bit in range(2):

        @pl.when(bits[0] == bit)
        def _(bit=bit):
            for j, (mine, received) in enumerate(((c2, c2_there), (c3, c3_there))):
                here = slice(j * rank, (j + 1) * rank)
                coef[bit * count : (bit + 1) * count, here] = mine[...].astype(jnp.bfloat16)
                coef[(1 - bit) * count : (2 - bit) * count, here] = received[...].astype(jnp.bfloat16)

    rows, wide = value.shape[1:]
    share = rows // RING
    piece = high.shape[0] // RING
    lhs = jnp.concatenate([c1[...], coef[...]], axis=1)
    for i in range(2):
        sums[i] = value[i] - dot(lhs, gram[i])
    for ref, parity in ((keep, bits[0]), (send, 1 - bits[0])):
        for i in range(RING // 2):
            place = 2 * i + parity
            here = pl.ds(pl.multiple_of(place * share, share), share)
            for level in range(2):
                for j in range(2):
                    start = level * rows + (2 * i + j) * share
                    ref[start : start + share] = sums[level, here, j * rank : (j + 1) * rank]
            start = 2 * rows + i * piece
            ref[start : start + piece] = high[pl.ds(pl.multiple_of(place * piece, piece), piece)]
    send[keep.shape[0] :] = low[...]


def fourth(bits, c1, c2, c3, c2_there, c3_there, value, gram, low, high):
    rows, rank = c1.shape
    wide = 2 * rank
    extra = high.shape[0] // 2
    return local(
        fourth_body,
        bits,
        [c1, c2, c3, c2_there, c3_there, value, gram, low, high],
        [
            vmem(2 * rows + extra, rank), vmem(2 * rows + extra + low.shape[0], rank),
            vmem(rows, wide, dtype=jnp.bfloat16),
        ],
        12 * rows * rank * wide,
        16 * rows * wide,
        [pltpu.VMEM((2, rows, wide), jnp.float32)],
    )


def halve_body(steps, share, bits, keep, got, low, out, send, lows):
    unit = keep.shape[0] // (2 * steps)
    counts = (2 * share, 2 * share, unit - 4 * share)
    if steps == 2:
        far, near = 1 + 2 * bits[1], 3 - 2 * bits[1]
        mine, theirs = [bits[6], bits[6] ^ near], [bits[6] ^ far, bits[6] ^ far ^ near]
    else:
        mine, theirs = [0], [1]
    for ref, slots in ((out, mine), (send, theirs)):
        base = 0
        for count in counts:
            for i, slot in enumerate(slots):
                here = pl.ds(2 * steps * base + slot * count, count)
                start = steps * base + i * count
                ref[start : start + count] = keep[here] + got[here]
            base += count
    done = low.shape[0]
    lows[:done] = low[...]
    lows[done:] = got[keep.shape[0] :]
    send[out.shape[0] :] = lows[...]


def halve(bits, steps, share, keep, got, low):
    rank, size, lows = keep.shape[1], keep.shape[0] // 2, 2 * low.shape[0]
    return local(
        functools.partial(halve_body, steps, share),
        bits,
        [keep, got, low],
        [vmem(size, rank), vmem(size + lows, rank), vmem(lows, rank)],
        2 * keep.size,
        20 * keep.size,
    )


def turn(place):
    return (place + 2 * (place & 1) - 1) & (RING - 1)


def gather_body(bits, keep, got, low, own, other, fifth, gram, high):
    share, rank = own.shape
    rows = 2 * share
    total = keep[...] + got[: keep.shape[0]]
    choose(bits[2], total[:share], total[share:rows], own, other)
    for j in range(2):
        fifth[:, j * rank : (j + 1) * rank] = total[rows + j * share : rows + (j + 1) * share]
    high[...] = total[2 * rows :]
    count = gram.shape[0] // RING
    known = low.shape[0]
    here = bits[0] + 2 * bits[6]
    for i in range(RING):
        second, third = (0, 2, 6, 4)[i // 2], (0, 6, 2, 4)[i // 2]
        first = here ^ second
        last = here ^ third
        if i % 2:
            first, last = first ^ 1, turn(last)
        owner = jnp.where(bits[1] == 0, first, last)
        p0, p1, p2 = owner & 1, owner >> 1 & 1, owner >> 2
        place = pl.multiple_of((p0 * 4 + (p1 ^ p2) * 2 + p2) * count, count)
        for j in range(2):
            start = 2 * i * count + j * count
            if start < known:
                part = low[start : start + count]
            else:
                start += keep.shape[0] - known
                part = got[start : start + count]
            gram[pl.ds(place, count), j * rank : (j + 1) * rank] = part


def gather_rows(bits, keep, got, low, share):
    rank = keep.shape[1]
    return local(
        gather_body,
        bits,
        [keep, got, low],
        [
            vmem(share, rank), vmem(share, rank), vmem(share, 2 * rank), vmem(rank, 2 * rank),
            vmem(keep.shape[0] - 4 * share, rank),
        ],
        2 * keep.size,
        20 * keep.size,
    )


def sixth_body(bits, c1, c23, packed, value, gram, keep, send, coef):
    rank = c1.shape[1]
    share = c1.shape[0] // packed.shape[0]
    for j in range(2):
        coef[:, j * rank : (j + 1) * rank] = (
            packed[:, j * share : (j + 1) * share, :].reshape(c1.shape).astype(jnp.bfloat16)
        )
    lhs = jnp.concatenate([c1[...], c23[...], coef[...]], axis=1)
    emit_halves(bits[1], [value[i] - dot(lhs, gram[i]) for i in range(3)], keep, send)


def sixth(bits, c1, c23, packed, value, gram):
    rows, rank = c1.shape
    wide = 2 * rank
    return local(
        sixth_body,
        bits,
        [c1, c23, packed, value, gram],
        [vmem(rows // 2, 3 * wide)] * 2 + [vmem(rows, wide, dtype=jnp.bfloat16)],
        30 * rows * rank * wide,
        24 * rows * wide,
    )


def add_body(bits, left, right, out):
    out[...] = left[...] + right[...]


def add(bits, left, right):
    return local(add_body, bits, [left, right], [vmem(*left.shape)], left.size, 12 * left.size)[0]


def total_body(bits, parts, out):
    out[...] = parts[...].sum(axis=0)


def total(bits, parts):
    return local(total_body, bits, [parts], [vmem(*parts.shape[1:])], parts.size, 4 * parts.size)[0]


def lower_body(bits, state, c1, c23, c45, up, out):
    coef = jnp.concatenate([c1[...], c23[...], c45[...]], axis=1)
    depth, leaf = coef.shape[1], state.shape[1]
    width = leaf // STEPS
    for i in range(STEPS):
        here = slice(i * width, (i + 1) * width)
        basis = up[: depth // c1.shape[1], :, here].reshape(depth, width)
        out[:, here] = state[:, here].astype(jnp.float32) - dot(coef, basis)


def lower(bits, state, c1, c23, c45, up_basis):
    rows, leaf = state.shape
    return local(
        lower_body,
        bits,
        [state, c1, c23, c45, up_basis],
        [vmem(rows, leaf)],
        10 * rows * leaf * c1.shape[1],
        6 * rows * leaf,
    )[0]


def last_body(bits, state, mine, received, up, out, coef, block, done):
    rank, count = up.shape[1], mine.shape[0]
    for bit in range(2):

        @pl.when(bits[1] == bit)
        def _(bit=bit):
            here = slice(bit * count, (bit + 1) * count)
            there = slice((1 - bit) * count, (2 - bit) * count)
            coef[here, :] = mine[:, : 3 * rank].astype(jnp.bfloat16)
            coef[there, :rank] = received[:, 2 * rank :].astype(jnp.bfloat16)
            coef[there, rank:] = received[:, : 2 * rank].astype(jnp.bfloat16)

    basis = up[5:8].reshape(3 * rank, up.shape[2])
    share = state.shape[0] // STEPS
    copies = []
    for i in range(STEPS):
        here = pl.ds(i * share, share)
        block[here] = state[here] - dot(coef[here], basis)
        copies.append(pltpu.make_async_copy(block.at[here], out.at[here], done.at[i]))
        copies[-1].start()
    for copy in copies:
        copy.wait()


def last(bits, state, mine, received, up_basis):
    rows, leaf = state.shape
    rank = up_basis.shape[1]
    args = [pltpu.with_memory_space_constraint(a, pltpu.VMEM) for a in (state, mine, received, up_basis)]
    return pl.pallas_call(
        last_body,
        out_shape=f32(rows, leaf),
        in_specs=[pl.BlockSpec(memory_space=pltpu.SMEM)] + [pl.BlockSpec(memory_space=pltpu.VMEM)] * 4,
        out_specs=pl.BlockSpec(memory_space=pltpu.HBM),
        scratch_shapes=[
            pltpu.VMEM((rows, 3 * rank), jnp.bfloat16),
            pltpu.VMEM((rows, leaf), jnp.float32),
            pltpu.SemaphoreType.DMA((STEPS,)),
        ],
        compiler_params=pltpu.CompilerParams(vmem_limit_bytes=VMEM_BYTES),
        cost_estimate=pl.CostEstimate(
            flops=6 * rows * leaf * rank, bytes_accessed=6 * rows * leaf, transcendentals=0
        ),
    )(bits, *args)


def shards(groups_z, groups_zy, rhs, leaf_inverse, up_basis, projection):
    size_x, size_y = lax.axis_size("gx"), lax.axis_size("gy")
    rows = rhs.shape[0]
    rank = up_basis.shape[1]
    wide = 2 * rank
    gx, gy = lax.axis_index("gx"), lax.axis_index("gy")
    z0, z1, z2, y0, y1 = (gx >> i & 1 for i in range(5))
    core, x0, x1 = (gy >> i & 1 for i in range(3))
    bits = jnp.stack([z0, core, y0, z1, z1 ^ z2, z2, z1 + 2 * z2])
    over_x = functools.partial(swap, axis="gx", size=size_x)
    over_y = functools.partial(swap, axis="gy", size=size_y)

    def by_core(value, *targets):
        pairs = [
            (x * size_y + y, targets[y & 1](x) * size_y + y) for x in range(size_x) for y in range(size_y)
        ]
        return lax.ppermute(value, ("gx", "gy"), pairs)

    ring = RING
    share = rows // ring
    by_y01, by_y1 = starts(y0 ^ y1, 3 * rank // 2), starts(y1, 3 * rank // 4)
    half_y1 = starts(y1, rank)
    half_core, half_x0, half_x1 = starts(core, rank), starts(x0, rank), starts(x1, rank)
    indices = (
        bits, by_y01, by_y1, half_y1,
        half_core, half_x0, half_x1, y1 == 0, (y0 ^ y1) == 0,
    )
    indices, rhs = lax.optimization_barrier((indices, rhs))
    (
        bits, by_y01, by_y1, half_y1,
        half_core, half_x0, half_x1, first_y1, first_y01,
    ) = indices

    state, own, other = leaf_solve(bits, rhs, leaf_inverse, projection)
    received = over_x(other, mask=1)
    value, gram, kept = project((2, 3), ((2, 3),), bits, state, up_basis, projection)
    value_45, gram_45, kept_45 = project((4, 5), ((4, 5),), bits, state, up_basis, projection)

    value_678, gram_678, kept_678 = project((6, 7, 8), ((6, 7), (6, 8), (7, 8)), bits, state, up_basis, projection)
    received, kept, kept_45, kept_678 = lax.optimization_barrier((received, kept, kept_45, kept_678))

    keep, send, keep_3, send_3, c1 = second(bits, own, received, value, gram, kept, kept_45)
    received = over_x(send, mask=1)
    left = over_x(send_3, mask=1)
    high, high_send = split(kept_678.reshape(3 * rank, wide), by_y01)
    high, high_send = split(high + over_x(high_send, mask=8), by_y1)
    high = high + over_x(high_send, mask=24)
    high = jnp.concatenate([high[:, :rank], high[:, rank:]])

    own, send, low = third(bits, keep, received)
    left, high = lax.optimization_barrier((left, high))
    c2, own, send, low = correct(bits, own, over_x(send, mask=2), low, keep_3, left)
    received = over_x(send, mask=6)
    c3, low = own + received[: rows // 2], low + received[rows // 2 :]
    c3 = c3 + over_x(c3, mask=2)
    c2_there = over_x(c2, mask=1)
    c3_there = over_x(c3, mask=1)

    keep, send, c23 = fourth(bits, c1, c2, c3, c2_there, c3_there, value_45, gram_45, low, high)
    got = by_core(send, lambda i: i ^ 1, lambda i: (i & -RING) + turn(i & (RING - 1)))
    keep, send, low = halve(bits, 2, share, keep, got, low)
    got = by_core(send, lambda i: i ^ 2, lambda i: i ^ 6)
    keep, send, low = halve(bits, 1, share, keep, got, low)
    got = by_core(send, lambda i: i ^ 6, lambda i: i ^ 2)
    own, other, left, gram_45, high = gather_rows(bits, keep, got, low, share)
    c4 = own + over_x(other, mask=8)
    left = left - dot(c4, gram_45)
    received = over_x(jnp.concatenate([half(left, half_y1[1]), high]), mask=24)
    c5 = half(left, half_y1[0]) + received[:share]
    high = join(high, received[share:], first_y1)
    received = over_x(jnp.concatenate([c5, high]), mask=8)
    c5 = c5 + received[:share]
    high = join(high, received[share:], first_y01)
    packed = jnp.concatenate([c4, c5, high], axis=0)
    packed = exchange(jnp.broadcast_to(packed, (ring, *packed.shape)), groups_z)

    keep, send, c45 = sixth(bits, c1, c23, packed, value_678, gram_678)
    left = add(bits, keep, over_y(send, mask=1))
    high = packed[:, 2 * share :].reshape(2, ring // 2, 4, 3 * rank // (2 * ring), rank)
    high = jnp.concatenate(list(high.transpose(0, 2, 1, 3, 4).reshape(2, 3 * rank, rank)), axis=1)
    high_there = over_y(high, mask=1)
    left, high, high_there = lax.optimization_barrier((left, high, high_there))
    half_rows = rows // 2
    count = half_rows // size_x
    left = total(bits, exchange(left.reshape(size_x, count, 3 * wide), groups_zy))
    left, c45 = lax.optimization_barrier((left, c45))
    high, high_there = high.reshape(3, rank, wide), high_there.reshape(3, rank, wide)
    c6, c6_there = half(left[:, :wide], half_core[0]), half(left[:, :wide], half_core[1])
    z7 = left[:, wide : 2 * wide] - exact_dot(c6, high[0]) - exact_dot(c6_there, high_there[0])
    z8 = left[:, 2 * wide :] - exact_dot(c6, high[1]) - exact_dot(c6_there, high_there[1])
    c7 = half(z7, half_x0[0]) + over_y(half(z7, half_x0[1]), mask=2)
    z8 = z8 - exact_dot(c7, high[2] + high_there[2])
    c8 = half(z8, half_x1[0]) + over_y(half(z8, half_x1[1]), mask=6)
    c8 = c8 + over_y(c8, mask=2)
    state = lower(bits, state, c1, c23, c45, up_basis)
    packed = jnp.concatenate([c6, c7, c8, c6_there], axis=1)
    packed, state = lax.optimization_barrier((packed, state))
    packed = exchange(jnp.broadcast_to(packed, (size_x, *packed.shape)), groups_zy)
    packed = packed.reshape(half_rows, 4 * rank)
    received = over_y(packed[:, rank:], mask=1)
    return last(bits, state, packed, received, up_basis)


def solution(mesh):
    size_x, size_y = mesh.shape["gx"], mesh.shape["gy"]
    ring = RING
    groups_z = [
        [gy * size_x + start + i for i in range(ring)]
        for gy in range(size_y)
        for start in range(0, size_x, ring)
    ]
    groups_zy = [[gy * size_x + i for i in range(size_x)] for gy in range(size_y)]
    return jax.shard_map(
        functools.partial(shards, groups_z, groups_zy),
        mesh=mesh,
        in_specs=(
            P(None, ("gy", "gx")),
            P(("gy", "gx"), None, None),
            P(None, None, ("gy", "gx")),
            P(None, None, ("gy", "gx")),
        ),
        out_specs=P(None, ("gy", "gx")),
        check_vma=False,
    )
```

```python
import functools

import jax
import jax.numpy as jnp
from jax import lax
from jax.experimental import pallas as pl
from jax.experimental.pallas import tpu as pltpu
from jax.sharding import PartitionSpec as P

AXES = ("gy", "gx")
STEPS = 4
RING = 8
VMEM_BYTES = 16 * 1024 * 1024


def dot(a, b):
    return jnp.dot(a, b, preferred_element_type=jnp.float32)


def dot_t(a, b):
    return lax.dot_general(a, b, (((1,), (1,)), ((), ())), preferred_element_type=jnp.float32)


def exact_dot(a, b):
    return jnp.dot(a, b, precision=lax.Precision.HIGHEST, preferred_element_type=jnp.float32)


def swap(value, axis, mask, size):
    return lax.ppermute(value, axis, [(source, source ^ mask) for source in range(size)])


def exchange(value, groups):
    return lax.all_to_all(value, AXES, 0, 0, tiled=True, axis_index_groups=groups)


def half(value, start):
    return lax.dynamic_slice_in_dim(value, start, value.shape[-1] // 2, value.ndim - 1)


def split(value, starts):
    count = value.shape[0] // 2
    return tuple(lax.dynamic_slice_in_dim(value, start, count, 0) for start in starts)


def join(mine, other, first):
    return jnp.where(first, jnp.concatenate([mine, other]), jnp.concatenate([other, mine]))


def starts(bit, count):
    return (bit * count).astype(jnp.uint32), ((1 - bit) * count).astype(jnp.uint32)


def hbm(value):
    return pltpu.with_memory_space_constraint(value, pltpu.HBM)


def f32(*shape):
    return jax.ShapeDtypeStruct(shape, jnp.float32)


def vmem(*shape, dtype=jnp.float32):
    return pltpu.VMEM(shape, dtype)


def local(body, bits, args, outs, flops, nbytes, scratch=()):
    args = [pltpu.with_memory_space_constraint(a, pltpu.VMEM) for a in args]
    return pl.pallas_call(
        body,
        out_shape=outs,
        in_specs=[pl.BlockSpec(memory_space=pltpu.SMEM)]
        + [pl.BlockSpec(memory_space=pltpu.VMEM)] * len(args),
        out_specs=[pl.BlockSpec(memory_space=pltpu.VMEM)] * len(outs),
        scratch_shapes=scratch,
        compiler_params=pltpu.CompilerParams(vmem_limit_bytes=VMEM_BYTES),
        cost_estimate=pl.CostEstimate(flops=flops, bytes_accessed=nbytes, transcendentals=0),
    )(bits, *args)


def leaf_body(bits, rhs, inverse, proj, state, own, other, left, right, rows, sums, done):
    leaf, rank = state.shape[1], own.shape[1]
    width = leaf // STEPS
    copies = [pltpu.make_async_copy(rhs, left, done.at[0])]
    for i in range(STEPS):
        here = pl.ds(i * width, width)
        copies.append(pltpu.make_async_copy(inverse.at[0, :, here], right.at[:, here], done.at[i + 1]))
    copies.append(pltpu.make_async_copy(proj.at[0], rows, done.at[STEPS + 1]))
    for copy in copies:
        copy.start()
    copies[0].wait()
    for i in range(STEPS):
        copies[i + 1].wait()
        here = slice(i * width, (i + 1) * width)
        state[:, here] = dot(left[...], right[:, here]).astype(jnp.bfloat16)
    copies[-1].wait()
    sums[...] = dot_t(state[...], rows[...])
    choose(bits[0], sums[:, :rank], sums[:, rank:], own, other)


def leaf_solve(bits, rhs, leaf_inverse, projection):
    rows, leaf = rhs.shape
    wide = projection.shape[1]
    rank = wide // 2
    args = [hbm(rhs), hbm(leaf_inverse), hbm(projection)]
    return pl.pallas_call(
        leaf_body,
        out_shape=[vmem(rows, leaf, dtype=jnp.bfloat16), vmem(rows, rank), vmem(rows, rank)],
        in_specs=[pl.BlockSpec(memory_space=pltpu.SMEM)] + [pl.BlockSpec(memory_space=pltpu.HBM)] * 3,
        out_specs=[pl.BlockSpec(memory_space=pltpu.VMEM)] * 3,
        scratch_shapes=[
            pltpu.VMEM((rows, leaf), jnp.bfloat16),
            pltpu.VMEM((leaf, leaf), jnp.bfloat16),
            pltpu.VMEM((wide, leaf), jnp.bfloat16),
            pltpu.VMEM((rows, wide), jnp.float32),
            pltpu.SemaphoreType.DMA((STEPS + 2,)),
        ],
        compiler_params=pltpu.CompilerParams(vmem_limit_bytes=VMEM_BYTES),
        cost_estimate=pl.CostEstimate(
            flops=2 * rows * leaf * (leaf + wide), bytes_accessed=leaf * (4 * rows + 2 * leaf), transcendentals=0
        ),
    )(bits, *args)


def project_body(heights, depth, pairs, bits, state, up, proj, value, gram, *kept):
    rank = up.shape[1]
    for i, h in enumerate(heights):
        rows = proj[h - 1]
        value[i] = dot_t(state[...], rows)
        gram[i] = dot_t(up[:depth].reshape(depth * rank, up.shape[2]), rows).astype(jnp.bfloat16)
        for j, (k, of) in enumerate(pairs):
            if of == h:
                kept[0][j] = dot_t(up[k - 1], rows)


def project(heights, pairs, bits, state, up_basis, projection):
    rows, leaf = state.shape
    rank = up_basis.shape[1]
    wide, count, depth = 2 * rank, len(heights), heights[0] - 1
    return local(
        functools.partial(project_body, heights, depth, pairs),
        bits,
        [state, up_basis, projection],
        [vmem(count, rows, wide), vmem(count, depth * rank, wide, dtype=jnp.bfloat16)]
        + ([vmem(len(pairs), rank, wide)] if pairs else []),
        2 * leaf * wide * (count * (rows + rank * depth) + rank * len(pairs)),
        2 * leaf * (rows + count * 3 * rank),
    )


def emit_halves(which, parts, keep, send):
    count, wide = parts[0].shape[0] // 2, parts[0].shape[1]
    for bit in range(2):

        @pl.when(which == bit)
        def _(bit=bit):
            for i, part in enumerate(parts):
                keep[:count, i * wide : (i + 1) * wide] = part[bit * count : (bit + 1) * count]
                send[:count, i * wide : (i + 1) * wide] = part[(1 - bit) * count : (2 - bit) * count]


def second_body(bits, mine, received, value, gram, pair, ring, keep_2, send_2, keep_3, send_3, coef):
    c1 = (mine[...] + received[...]).astype(jnp.bfloat16)
    coef[...] = c1
    rows, count = keep_2.shape[0] - pair.shape[1] // 2, pair.shape[1] // 2
    emit_halves(bits[0], [value[0] - dot(c1, gram[0])], keep_2, send_2)
    emit_halves(bits[0], [value[1] - dot(c1, gram[1])], keep_3, send_3)
    for ref in (keep_3, send_3):
        ref[rows:] = pair[0]
    for ref, which in ((keep_2, bits[0]), (send_2, 1 - bits[0])):
        ref[rows:] = ring[0, pl.ds(pl.multiple_of(which * count, count), count)]


def second(bits, mine, received, value, gram, pair, ring):
    rows, rank = mine.shape
    wide = 2 * rank
    return local(
        second_body,
        bits,
        [mine, received, value, gram, pair, ring],
        [vmem((rows + rank) // 2, wide)] * 2 + [vmem(rows // 2 + rank, wide)] * 2 + [vmem(rows, rank, dtype=jnp.bfloat16)],
        4 * rows * rank * wide,
        16 * rows * wide,
    )


def choose(bit, left, right, keep, send):
    for b in range(2):

        @pl.when(bit == b)
        def _(b=b):
            keep[...] = (left, right)[b]
            send[...] = (left, right)[1 - b]


def stack(value, rank):
    return jnp.concatenate([value[:, :rank], value[:, rank:]], axis=0)


def third_body(bits, keep, received, own, send, low):
    total = keep[...] + received[...]
    rows, rank = own.shape
    count = low.shape[0] // 2
    choose(bits[3], total[:rows, :rank], total[:rows, rank:], own, send.at[:rows])
    choose(bits[4], stack(total[rows : rows + count], rank), stack(total[rows + count :], rank), low, send.at[rows:])


def third(bits, keep, received):
    rank = keep.shape[1] // 2
    rows = keep.shape[0] - rank // 2
    return local(
        third_body,
        bits,
        [keep, received],
        [vmem(rows, rank), vmem(rows + rank // 2, rank), vmem(rank // 2, rank)],
        keep.size,
        12 * keep.size,
    )


def correct_body(bits, own, received, low, keep, left, coef, mine, send, kept):
    rows, rank = own.shape
    count = low.shape[0] // 4
    c2 = own[...] + received[:rows]
    coef[...] = c2
    total = keep[...] + left[...]
    rest = total[:rows] - dot(c2.astype(jnp.bfloat16), total[rows:].astype(jnp.bfloat16))
    choose(bits[5], rest[:, :rank], rest[:, rank:], mine, send.at[:rows])
    total = low[...] + received[rows:]
    parts = [jnp.concatenate([total[i * count : (i + 1) * count], total[(i + 2) * count : (i + 3) * count]]) for i in range(2)]
    choose(bits[5], parts[0], parts[1], kept, send.at[rows:])


def correct(bits, own, received, low, keep, left):
    rows, rank = own.shape
    return local(
        correct_body,
        bits,
        [own, received, low, keep, left],
        [vmem(rows, rank), vmem(rows, rank), vmem(rows + rank // 4, rank), vmem(rank // 4, rank)],
        4 * rows * rank * rank,
        20 * rows * rank,
    )


def fourth_body(bits, c1, c2, c3, c2_there, c3_there, value, gram, low, high, keep_a, send_a, keep_b, send_b, coef, sums):
    count, rank = c2.shape
    for bit in range(2):

        @pl.when(bits[0] == bit)
        def _(bit=bit):
            for j, (mine, received) in enumerate(((c2, c2_there), (c3, c3_there))):
                here = slice(j * rank, (j + 1) * rank)
                coef[bit * count : (bit + 1) * count, here] = mine[...].astype(jnp.bfloat16)
                coef[(1 - bit) * count : (2 - bit) * count, here] = received[...].astype(jnp.bfloat16)

    rows, wide = value.shape[1:]
    share = rows // RING
    piece = high.shape[0] // RING
    lhs = jnp.concatenate([c1[...], coef[...]], axis=1)
    for i in range(2):
        sums[i] = value[i] - dot(lhs, gram[i])
    for keep, send, level in ((keep_a, send_a, 0), (keep_b, send_b, 1)):
        for ref, parity in ((keep, bits[0]), (send, 1 - bits[0])):
            for i in range(RING // 2):
                place = 2 * i + parity
                for j in range(2):
                    start = (2 * i + j) * share
                    ref[start : start + share] = sums[
                        level, pl.ds(pl.multiple_of(place * share, share), share), j * rank : (j + 1) * rank
                    ]
                if level == 0:
                    start = rows + i * piece
                    ref[start : start + piece] = high[pl.ds(pl.multiple_of(place * piece, piece), piece)]
    send_a[rows + RING // 2 * piece :] = low[...]


def fourth(bits, c1, c2, c3, c2_there, c3_there, value, gram, low, high):
    rows, rank = c1.shape
    wide = 2 * rank
    extra = high.shape[0] // 2
    return local(
        fourth_body,
        bits,
        [c1, c2, c3, c2_there, c3_there, value, gram, low, high],
        [
            vmem(rows + extra, rank), vmem(rows + extra + low.shape[0], rank),
            vmem(rows, rank), vmem(rows, rank), vmem(rows, wide, dtype=jnp.bfloat16),
        ],
        12 * rows * rank * wide,
        16 * rows * wide,
        [pltpu.VMEM((2, rows, wide), jnp.float32)],
    )


def halve_body(steps, far, near, bits, keep, got, *refs):
    low, (out, send, *lows) = refs[: len(refs) // 3], refs[len(refs) // 3 :]
    rank = keep.shape[1]
    extra = 3 * rank // 8 * steps if low else 0
    rows = keep.shape[0] - extra
    count, piece = rows // (2 * steps), extra // (2 * steps)
    if steps == 2:
        mine, theirs = [bits[6], bits[6] ^ near], [bits[6] ^ far, bits[6] ^ far ^ near]
    else:
        mine, theirs = [0], [1]
    for ref, slots in ((out, mine), (send, theirs)):
        for i, slot in enumerate(slots):
            here = pl.ds(slot * count, count)
            ref[i * count : (i + 1) * count] = keep[here] + got[here]
            if low:
                there = pl.ds(rows + slot * piece, piece)
                start = len(slots) * count + i * piece
                ref[start : start + piece] = keep[there] + got[there]
    if low:
        done = low[0].shape[0]
        lows[0][:done] = low[0][...]
        lows[0][done:] = got[keep.shape[0] :]
        send[out.shape[0] :] = lows[0][...]


def halve(bits, steps, far, near, keep, got, *low):
    rank, size = keep.shape[1], keep.shape[0] // 2
    lows = [2 * v.shape[0] for v in low]
    return local(
        functools.partial(halve_body, steps, far, near),
        bits,
        [keep, got, *low],
        [vmem(size, rank), vmem(size + sum(lows), rank)] + [vmem(v, rank) for v in lows],
        2 * keep.size,
        20 * keep.size,
    )


def fourth_rows_body(bits, keep, got, low, own, other, gram, high):
    share, rank = own.shape
    rows = 2 * share
    total = keep[...] + got[: keep.shape[0]]
    choose(bits[2], total[:share], total[share:rows], own, other)
    high[...] = total[rows:]
    count = gram.shape[0] // RING
    half_list = low.shape[0]
    z0, z1, z2 = bits[0], bits[3], bits[5]
    for i, mask in enumerate((0, 1, 2, 3, 6, 7, 4, 5)):
        p0, p1, p2 = z0 ^ (mask & 1), z1 ^ (mask >> 1 & 1), z2 ^ (mask >> 2)
        place = pl.multiple_of((p0 * 4 + (p1 ^ p2) * 2 + p2) * count, count)
        for j in range(2):
            start = 2 * i * count + j * count
            if start < half_list:
                part = low[start : start + count]
            else:
                start += keep.shape[0] - half_list
                part = got[start : start + count]
            gram[pl.ds(place, count), j * rank : (j + 1) * rank] = part


def fourth_rows(bits, keep, got, low, share):
    rank = keep.shape[1]
    return local(
        fourth_rows_body,
        bits,
        [keep, got, low],
        [vmem(share, rank), vmem(share, rank), vmem(rank, 2 * rank), vmem(keep.shape[0] - 2 * share, rank)],
        2 * keep.size,
        20 * keep.size,
    )


def fifth_rows_body(bits, keep, got, fifth):
    share, rank = fifth.shape[0], keep.shape[1]
    for j in range(2):
        here = slice(j * share, (j + 1) * share)
        fifth[:, j * rank : (j + 1) * rank] = keep[here] + got[here]


def sixth_body(bits, c1, c23, packed, value, gram, keep, send, coef):
    rank = c1.shape[1]
    share = c1.shape[0] // packed.shape[0]
    for j in range(2):
        coef[:, j * rank : (j + 1) * rank] = (
            packed[:, j * share : (j + 1) * share, :].reshape(c1.shape).astype(jnp.bfloat16)
        )
    lhs = jnp.concatenate([c1[...], c23[...], coef[...]], axis=1)
    emit_halves(bits[1], [value[i] - dot(lhs, gram[i]) for i in range(3)], keep, send)


def sixth(bits, c1, c23, packed, value, gram):
    rows, rank = c1.shape
    wide = 2 * rank
    return local(
        sixth_body,
        bits,
        [c1, c23, packed, value, gram],
        [vmem(rows // 2, 3 * wide)] * 2 + [vmem(rows, wide, dtype=jnp.bfloat16)],
        30 * rows * rank * wide,
        24 * rows * wide,
    )


def add_body(bits, left, right, out):
    out[...] = left[...] + right[...]


def add(bits, left, right):
    return local(add_body, bits, [left, right], [vmem(*left.shape)], left.size, 12 * left.size)[0]


def total_body(bits, parts, out):
    out[...] = parts[...].sum(axis=0)


def total(bits, parts):
    return local(total_body, bits, [parts], [vmem(*parts.shape[1:])], parts.size, 4 * parts.size)[0]


def lower_body(bits, state, c1, c23, c45, up, out):
    coef = jnp.concatenate([c1[...], c23[...], c45[...]], axis=1)
    depth, leaf = coef.shape[1], state.shape[1]
    width = leaf // STEPS
    for i in range(STEPS):
        here = slice(i * width, (i + 1) * width)
        basis = up[: depth // c1.shape[1], :, here].reshape(depth, width)
        out[:, here] = state[:, here].astype(jnp.float32) - dot(coef, basis)


def lower(bits, state, c1, c23, c45, up_basis):
    rows, leaf = state.shape
    return local(
        lower_body,
        bits,
        [state, c1, c23, c45, up_basis],
        [vmem(rows, leaf)],
        10 * rows * leaf * c1.shape[1],
        6 * rows * leaf,
    )[0]


def last_body(bits, state, mine, received, up, out, coef, block, done):
    rank, count = up.shape[1], mine.shape[0]
    for bit in range(2):

        @pl.when(bits[1] == bit)
        def _(bit=bit):
            here = slice(bit * count, (bit + 1) * count)
            there = slice((1 - bit) * count, (2 - bit) * count)
            coef[here, :] = mine[:, : 3 * rank].astype(jnp.bfloat16)
            coef[there, :rank] = received[:, 2 * rank :].astype(jnp.bfloat16)
            coef[there, rank:] = received[:, : 2 * rank].astype(jnp.bfloat16)

    basis = up[5:8].reshape(3 * rank, up.shape[2])
    share = state.shape[0] // STEPS
    copies = []
    for i in range(STEPS):
        here = pl.ds(i * share, share)
        block[here] = state[here] - dot(coef[here], basis)
        copies.append(pltpu.make_async_copy(block.at[here], out.at[here], done.at[i]))
        copies[-1].start()
    for copy in copies:
        copy.wait()


def last(bits, state, mine, received, up_basis):
    rows, leaf = state.shape
    rank = up_basis.shape[1]
    args = [pltpu.with_memory_space_constraint(a, pltpu.VMEM) for a in (state, mine, received, up_basis)]
    return pl.pallas_call(
        last_body,
        out_shape=f32(rows, leaf),
        in_specs=[pl.BlockSpec(memory_space=pltpu.SMEM)] + [pl.BlockSpec(memory_space=pltpu.VMEM)] * 4,
        out_specs=pl.BlockSpec(memory_space=pltpu.HBM),
        scratch_shapes=[
            pltpu.VMEM((rows, 3 * rank), jnp.bfloat16),
            pltpu.VMEM((rows, leaf), jnp.float32),
            pltpu.SemaphoreType.DMA((STEPS,)),
        ],
        compiler_params=pltpu.CompilerParams(vmem_limit_bytes=VMEM_BYTES),
        cost_estimate=pl.CostEstimate(
            flops=6 * rows * leaf * rank, bytes_accessed=6 * rows * leaf, transcendentals=0
        ),
    )(bits, *args)


def shards(groups_z, groups_zy, rhs, leaf_inverse, up_basis, projection):
    size_x, size_y = lax.axis_size("gx"), lax.axis_size("gy")
    rows = rhs.shape[0]
    rank = up_basis.shape[1]
    wide = 2 * rank
    gx, gy = lax.axis_index("gx"), lax.axis_index("gy")
    z0, z1, z2, y0, y1 = (gx >> i & 1 for i in range(5))
    core, x0, x1 = (gy >> i & 1 for i in range(3))
    bits = jnp.stack([z0, core, y0, z1, z1 ^ z2, z2, z1 + 2 * z2])
    over_x = functools.partial(swap, axis="gx", size=size_x)
    over_y = functools.partial(swap, axis="gy", size=size_y)
    ring = RING
    share = rows // ring
    by_y01, by_y1 = starts(y0 ^ y1, 3 * rank // 2), starts(y1, 3 * rank // 4)
    half_y1 = starts(y1, rank)
    half_core, half_x0, half_x1 = starts(core, rank), starts(x0, rank), starts(x1, rank)
    indices = (
        bits, by_y01, by_y1, half_y1,
        half_core, half_x0, half_x1, y1 == 0, (y0 ^ y1) == 0,
    )
    indices, rhs = lax.optimization_barrier((indices, rhs))
    (
        bits, by_y01, by_y1, half_y1,
        half_core, half_x0, half_x1, first_y1, first_y01,
    ) = indices

    state, own, other = leaf_solve(bits, rhs, leaf_inverse, projection)
    received = over_x(other, mask=1)
    value, gram, kept = project((2, 3), ((2, 3),), bits, state, up_basis, projection)
    value_45, gram_45, kept_45 = project((4, 5), ((4, 5),), bits, state, up_basis, projection)

    value_678, gram_678, kept_678 = project((6, 7, 8), ((6, 7), (6, 8), (7, 8)), bits, state, up_basis, projection)
    received, kept, kept_45, kept_678 = lax.optimization_barrier((received, kept, kept_45, kept_678))

    keep, send, keep_3, send_3, c1 = second(bits, own, received, value, gram, kept, kept_45)
    received = over_x(send, mask=1)
    left = over_x(send_3, mask=1)
    high, high_send = split(kept_678.reshape(3 * rank, wide), by_y01)
    high, high_send = split(high + over_x(high_send, mask=8), by_y1)
    high = high + over_x(high_send, mask=24)
    high = jnp.concatenate([high[:, :rank], high[:, rank:]])

    own, send, low = third(bits, keep, received)
    left, high = lax.optimization_barrier((left, high))
    c2, own, send, low = correct(bits, own, over_x(send, mask=2), low, keep_3, left)
    received = over_x(send, mask=6)
    c3, low = own + received[: rows // 2], low + received[rows // 2 :]
    c3 = c3 + over_x(c3, mask=2)
    c2_there = over_x(c2, mask=1)
    c3_there = over_x(c3, mask=1)

    keep_a, send_a, keep_b, send_b, c23 = fourth(bits, c1, c2, c3, c2_there, c3_there, value_45, gram_45, low, high)
    turned = [(i & -RING) + ((i + 1 if i & 1 else i - 1) % RING) for i in range(size_x)]
    got_a, got_b = over_x(send_a, mask=1), lax.ppermute(send_b, "gx", list(enumerate(turned)))
    keep_a, send_a, low = halve(bits, 2, 1, 3, keep_a, got_a, low)
    got_a = over_x(send_a, mask=2)
    keep_b, send_b = halve(bits, 2, 3, 1, keep_b, got_b)
    got_b = over_x(send_b, mask=6)
    keep_a, send_a, low = halve(bits, 1, 0, 0, keep_a, got_a, low)
    got_a = over_x(send_a, mask=6)
    keep_b, send_b = halve(bits, 1, 0, 0, keep_b, got_b)
    got_b = over_x(send_b, mask=2)
    own, other, gram_45, high = fourth_rows(bits, keep_a, got_a, low, share)
    c4 = own + over_x(other, mask=8)
    left = local(fifth_rows_body, bits, [keep_b, got_b], [vmem(share, wide)], keep_b.size, 12 * keep_b.size)[0]
    left = left - dot(c4, gram_45)
    received = over_x(jnp.concatenate([half(left, half_y1[1]), high]), mask=24)
    c5 = half(left, half_y1[0]) + received[:share]
    high = join(high, received[share:], first_y1)
    received = over_x(jnp.concatenate([c5, high]), mask=8)
    c5 = c5 + received[:share]
    high = join(high, received[share:], first_y01)
    packed = jnp.concatenate([c4, c5, high], axis=0)
    packed = exchange(jnp.broadcast_to(packed, (ring, *packed.shape)), groups_z)

    keep, send, c45 = sixth(bits, c1, c23, packed, value_678, gram_678)
    left = add(bits, keep, over_y(send, mask=1))
    high = packed[:, 2 * share :].reshape(2, ring // 2, 4, 3 * rank // (2 * ring), rank)
    high = jnp.concatenate(list(high.transpose(0, 2, 1, 3, 4).reshape(2, 3 * rank, rank)), axis=1)
    high_there = over_y(high, mask=1)
    left, high, high_there = lax.optimization_barrier((left, high, high_there))
    half_rows = rows // 2
    count = half_rows // size_x
    left = total(bits, exchange(left.reshape(size_x, count, 3 * wide), groups_zy))
    left, c45 = lax.optimization_barrier((left, c45))
    high, high_there = high.reshape(3, rank, wide), high_there.reshape(3, rank, wide)
    c6, c6_there = half(left[:, :wide], half_core[0]), half(left[:, :wide], half_core[1])
    z7 = left[:, wide : 2 * wide] - exact_dot(c6, high[0]) - exact_dot(c6_there, high_there[0])
    z8 = left[:, 2 * wide :] - exact_dot(c6, high[1]) - exact_dot(c6_there, high_there[1])
    c7 = half(z7, half_x0[0]) + over_y(half(z7, half_x0[1]), mask=2)
    z8 = z8 - exact_dot(c7, high[2] + high_there[2])
    c8 = half(z8, half_x1[0]) + over_y(half(z8, half_x1[1]), mask=6)
    c8 = c8 + over_y(c8, mask=2)
    state = lower(bits, state, c1, c23, c45, up_basis)
    packed = jnp.concatenate([c6, c7, c8, c6_there], axis=1)
    packed, state = lax.optimization_barrier((packed, state))
    packed = exchange(jnp.broadcast_to(packed, (size_x, *packed.shape)), groups_zy)
    packed = packed.reshape(half_rows, 4 * rank)
    received = over_y(packed[:, rank:], mask=1)
    return last(bits, state, packed, received, up_basis)


def solution(mesh):
    size_x, size_y = mesh.shape["gx"], mesh.shape["gy"]
    ring = RING
    groups_z = [
        [gy * size_x + start + i for i in range(ring)]
        for gy in range(size_y)
        for start in range(0, size_x, ring)
    ]
    groups_zy = [[gy * size_x + i for i in range(size_x)] for gy in range(size_y)]
    return jax.shard_map(
        functools.partial(shards, groups_z, groups_zy),
        mesh=mesh,
        in_specs=(
            P(None, ("gy", "gx")),
            P(("gy", "gx"), None, None),
            P(None, None, ("gy", "gx")),
            P(None, None, ("gy", "gx")),
        ),
        out_specs=P(None, ("gy", "gx")),
        check_vma=False,
    )
```

```python
import functools

import jax
import jax.numpy as jnp
from jax import lax
from jax.experimental import pallas as pl
from jax.experimental.pallas import tpu as pltpu
from jax.sharding import PartitionSpec as P

AXES = ("gy", "gx")
STEPS = 4
RING = 8
VMEM_BYTES = 16 * 1024 * 1024


def dot(a, b):
    return jnp.dot(a, b, preferred_element_type=jnp.float32)


def dot_t(a, b):
    return lax.dot_general(a, b, (((1,), (1,)), ((), ())), preferred_element_type=jnp.float32)


def exact_dot(a, b):
    return jnp.dot(a, b, precision=lax.Precision.HIGHEST, preferred_element_type=jnp.float32)


def swap(value, axis, mask, size):
    return lax.ppermute(value, axis, [(source, source ^ mask) for source in range(size)])


def exchange(value, groups):
    return lax.all_to_all(value, AXES, 0, 0, tiled=True, axis_index_groups=groups)


def half(value, start):
    return lax.dynamic_slice_in_dim(value, start, value.shape[-1] // 2, value.ndim - 1)


def split(value, starts):
    count = value.shape[0] // 2
    return tuple(lax.dynamic_slice_in_dim(value, start, count, 0) for start in starts)


def join(mine, other, first):
    return jnp.where(first, jnp.concatenate([mine, other]), jnp.concatenate([other, mine]))


def starts(bit, count):
    return (bit * count).astype(jnp.uint32), ((1 - bit) * count).astype(jnp.uint32)


def hbm(value):
    return pltpu.with_memory_space_constraint(value, pltpu.HBM)


def f32(*shape):
    return jax.ShapeDtypeStruct(shape, jnp.float32)


def vmem(*shape, dtype=jnp.float32):
    return pltpu.VMEM(shape, dtype)


def local(body, bits, args, outs, flops, nbytes, scratch=()):
    args = [pltpu.with_memory_space_constraint(a, pltpu.VMEM) for a in args]
    return pl.pallas_call(
        body,
        out_shape=outs,
        in_specs=[pl.BlockSpec(memory_space=pltpu.SMEM)]
        + [pl.BlockSpec(memory_space=pltpu.VMEM)] * len(args),
        out_specs=[pl.BlockSpec(memory_space=pltpu.VMEM)] * len(outs),
        scratch_shapes=scratch,
        compiler_params=pltpu.CompilerParams(vmem_limit_bytes=VMEM_BYTES),
        cost_estimate=pl.CostEstimate(flops=flops, bytes_accessed=nbytes, transcendentals=0),
    )(bits, *args)


def leaf_body(bits, rhs, inverse, proj, state, own, other, left, right, rows, sums, done):
    leaf, rank = state.shape[1], own.shape[1]
    width = leaf // STEPS
    copies = [pltpu.make_async_copy(rhs, left, done.at[0])]
    for i in range(STEPS):
        here = pl.ds(i * width, width)
        copies.append(pltpu.make_async_copy(inverse.at[0, :, here], right.at[:, here], done.at[i + 1]))
    copies.append(pltpu.make_async_copy(proj.at[0], rows, done.at[STEPS + 1]))
    for copy in copies:
        copy.start()
    copies[0].wait()
    for i in range(STEPS):
        copies[i + 1].wait()
        here = slice(i * width, (i + 1) * width)
        state[:, here] = dot(left[...], right[:, here]).astype(jnp.bfloat16)
    copies[-1].wait()
    sums[...] = dot_t(state[...], rows[...])
    choose(bits[0], sums[:, :rank], sums[:, rank:], own, other)


def leaf_solve(bits, rhs, leaf_inverse, projection):
    rows, leaf = rhs.shape
    wide = projection.shape[1]
    rank = wide // 2
    args = [hbm(rhs), hbm(leaf_inverse), hbm(projection)]
    return pl.pallas_call(
        leaf_body,
        out_shape=[vmem(rows, leaf, dtype=jnp.bfloat16), vmem(rows, rank), vmem(rows, rank)],
        in_specs=[pl.BlockSpec(memory_space=pltpu.SMEM)] + [pl.BlockSpec(memory_space=pltpu.HBM)] * 3,
        out_specs=[pl.BlockSpec(memory_space=pltpu.VMEM)] * 3,
        scratch_shapes=[
            pltpu.VMEM((rows, leaf), jnp.bfloat16),
            pltpu.VMEM((leaf, leaf), jnp.bfloat16),
            pltpu.VMEM((wide, leaf), jnp.bfloat16),
            pltpu.VMEM((rows, wide), jnp.float32),
            pltpu.SemaphoreType.DMA((STEPS + 2,)),
        ],
        compiler_params=pltpu.CompilerParams(vmem_limit_bytes=VMEM_BYTES),
        cost_estimate=pl.CostEstimate(
            flops=2 * rows * leaf * (leaf + wide), bytes_accessed=leaf * (4 * rows + 2 * leaf), transcendentals=0
        ),
    )(bits, *args)


def project_body(heights, depth, pairs, bits, state, up, proj, value, gram, *kept):
    rank = up.shape[1]
    for i, h in enumerate(heights):
        rows = proj[h - 1]
        value[i] = dot_t(state[...], rows)
        gram[i] = dot_t(up[:depth].reshape(depth * rank, up.shape[2]), rows).astype(jnp.bfloat16)
        for j, (k, of) in enumerate(pairs):
            if of == h:
                kept[0][j] = dot_t(up[k - 1], rows)


def project(heights, pairs, bits, state, up_basis, projection):
    rows, leaf = state.shape
    rank = up_basis.shape[1]
    wide, count, depth = 2 * rank, len(heights), heights[0] - 1
    return local(
        functools.partial(project_body, heights, depth, pairs),
        bits,
        [state, up_basis, projection],
        [vmem(count, rows, wide), vmem(count, depth * rank, wide, dtype=jnp.bfloat16)]
        + ([vmem(len(pairs), rank, wide)] if pairs else []),
        2 * leaf * wide * (count * (rows + rank * depth) + rank * len(pairs)),
        2 * leaf * (rows + count * 3 * rank),
    )


def emit_halves(which, parts, keep, send):
    count, wide = parts[0].shape[0] // 2, parts[0].shape[1]
    for bit in range(2):

        @pl.when(which == bit)
        def _(bit=bit):
            for i, part in enumerate(parts):
                keep[:count, i * wide : (i + 1) * wide] = part[bit * count : (bit + 1) * count]
                send[:count, i * wide : (i + 1) * wide] = part[(1 - bit) * count : (2 - bit) * count]


def second_body(bits, mine, received, value, gram, pair, ring, keep_2, send_2, keep_3, send_3, coef):
    c1 = (mine[...] + received[...]).astype(jnp.bfloat16)
    coef[...] = c1
    rows, count = keep_2.shape[0] - pair.shape[1] // 2, pair.shape[1] // 2
    emit_halves(bits[0], [value[0] - dot(c1, gram[0])], keep_2, send_2)
    emit_halves(bits[0], [value[1] - dot(c1, gram[1])], keep_3, send_3)
    for ref in (keep_3, send_3):
        ref[rows:] = pair[0]
    for ref, which in ((keep_2, bits[0]), (send_2, 1 - bits[0])):
        ref[rows:] = ring[0, pl.ds(pl.multiple_of(which * count, count), count)]


def second(bits, mine, received, value, gram, pair, ring):
    rows, rank = mine.shape
    wide = 2 * rank
    return local(
        second_body,
        bits,
        [mine, received, value, gram, pair, ring],
        [vmem((rows + rank) // 2, wide)] * 2 + [vmem(rows // 2 + rank, wide)] * 2 + [vmem(rows, rank, dtype=jnp.bfloat16)],
        4 * rows * rank * wide,
        16 * rows * wide,
    )


def choose(bit, left, right, keep, send):
    for b in range(2):

        @pl.when(bit == b)
        def _(b=b):
            keep[...] = (left, right)[b]
            send[...] = (left, right)[1 - b]


def stack(value, rank):
    return jnp.concatenate([value[:, :rank], value[:, rank:]], axis=0)


def third_body(bits, keep, received, own, send, low):
    total = keep[...] + received[...]
    rows, rank = own.shape
    count = low.shape[0] // 2
    choose(bits[3], total[:rows, :rank], total[:rows, rank:], own, send.at[:rows])
    choose(bits[4], stack(total[rows : rows + count], rank), stack(total[rows + count :], rank), low, send.at[rows:])


def third(bits, keep, received):
    rank = keep.shape[1] // 2
    rows = keep.shape[0] - rank // 2
    return local(
        third_body,
        bits,
        [keep, received],
        [vmem(rows, rank), vmem(rows + rank // 2, rank), vmem(rank // 2, rank)],
        keep.size,
        12 * keep.size,
    )


def correct_body(bits, own, received, low, keep, left, coef, mine, send, kept):
    rows, rank = own.shape
    count = low.shape[0] // 4
    c2 = own[...] + received[:rows]
    coef[...] = c2
    total = keep[...] + left[...]
    rest = total[:rows] - dot(c2.astype(jnp.bfloat16), total[rows:].astype(jnp.bfloat16))
    choose(bits[5], rest[:, :rank], rest[:, rank:], mine, send.at[:rows])
    total = low[...] + received[rows:]
    parts = [jnp.concatenate([total[i * count : (i + 1) * count], total[(i + 2) * count : (i + 3) * count]]) for i in range(2)]
    choose(bits[5], parts[0], parts[1], kept, send.at[rows:])


def correct(bits, own, received, low, keep, left):
    rows, rank = own.shape
    return local(
        correct_body,
        bits,
        [own, received, low, keep, left],
        [vmem(rows, rank), vmem(rows, rank), vmem(rows + rank // 4, rank), vmem(rank // 4, rank)],
        4 * rows * rank * rank,
        20 * rows * rank,
    )


def fourth_body(bits, c1, c2, c3, c2_there, c3_there, value, gram, low, high, keep_a, send_a, keep_b, send_b, coef, sums):
    count, rank = c2.shape
    for bit in range(2):

        @pl.when(bits[0] == bit)
        def _(bit=bit):
            for j, (mine, received) in enumerate(((c2, c2_there), (c3, c3_there))):
                here = slice(j * rank, (j + 1) * rank)
                coef[bit * count : (bit + 1) * count, here] = mine[...].astype(jnp.bfloat16)
                coef[(1 - bit) * count : (2 - bit) * count, here] = received[...].astype(jnp.bfloat16)

    rows, wide = value.shape[1:]
    share = rows // RING
    piece = high.shape[0] // RING
    lhs = jnp.concatenate([c1[...], coef[...]], axis=1)
    for i in range(2):
        sums[i] = value[i] - dot(lhs, gram[i])
    for keep, send, level in ((keep_a, send_a, 0), (keep_b, send_b, 1)):
        for ref, parity in ((keep, bits[0]), (send, 1 - bits[0])):
            for i in range(RING // 2):
                place = 2 * i + parity
                for j in range(2):
                    start = (2 * i + j) * share
                    ref[start : start + share] = sums[
                        level, pl.ds(pl.multiple_of(place * share, share), share), j * rank : (j + 1) * rank
                    ]
                if level == 0:
                    start = rows + i * piece
                    ref[start : start + piece] = high[pl.ds(pl.multiple_of(place * piece, piece), piece)]
    send_a[rows + RING // 2 * piece :] = low[...]


def fourth(bits, c1, c2, c3, c2_there, c3_there, value, gram, low, high):
    rows, rank = c1.shape
    wide = 2 * rank
    extra = high.shape[0] // 2
    return local(
        fourth_body,
        bits,
        [c1, c2, c3, c2_there, c3_there, value, gram, low, high],
        [
            vmem(rows + extra, rank), vmem(rows + extra + low.shape[0], rank),
            vmem(rows, rank), vmem(rows, rank), vmem(rows, wide, dtype=jnp.bfloat16),
        ],
        12 * rows * rank * wide,
        16 * rows * wide,
        [pltpu.VMEM((2, rows, wide), jnp.float32)],
    )


def halve_body(steps, far, near, bits, keep, got, *refs):
    low, (out, send, *lows) = refs[: len(refs) // 3], refs[len(refs) // 3 :]
    rank = keep.shape[1]
    extra = 3 * rank // 8 * steps if low else 0
    rows = keep.shape[0] - extra
    count, piece = rows // (2 * steps), extra // (2 * steps)
    if steps == 2:
        mine, theirs = [bits[6], bits[6] ^ near], [bits[6] ^ far, bits[6] ^ far ^ near]
    else:
        mine, theirs = [0], [1]
    for ref, slots in ((out, mine), (send, theirs)):
        for i, slot in enumerate(slots):
            here = pl.ds(slot * count, count)
            ref[i * count : (i + 1) * count] = keep[here] + got[here]
            if low:
                there = pl.ds(rows + slot * piece, piece)
                start = len(slots) * count + i * piece
                ref[start : start + piece] = keep[there] + got[there]
    if low:
        done = low[0].shape[0]
        lows[0][:done] = low[0][...]
        lows[0][done:] = got[keep.shape[0] :]
        send[out.shape[0] :] = lows[0][...]


def halve(bits, steps, far, near, keep, got, *low):
    rank, size = keep.shape[1], keep.shape[0] // 2
    lows = [2 * v.shape[0] for v in low]
    return local(
        functools.partial(halve_body, steps, far, near),
        bits,
        [keep, got, *low],
        [vmem(size, rank), vmem(size + sum(lows), rank)] + [vmem(v, rank) for v in lows],
        2 * keep.size,
        20 * keep.size,
    )


def fourth_rows_body(bits, keep, got, low, own, other, gram, high):
    share, rank = own.shape
    rows = 2 * share
    total = keep[...] + got[: keep.shape[0]]
    choose(bits[2], total[:share], total[share:rows], own, other)
    high[...] = total[rows:]
    count = gram.shape[0] // RING
    half_list = low.shape[0]
    z0, z1, z2 = bits[0], bits[3], bits[5]
    for i, mask in enumerate((0, 1, 2, 3, 6, 7, 4, 5)):
        p0, p1, p2 = z0 ^ (mask & 1), z1 ^ (mask >> 1 & 1), z2 ^ (mask >> 2)
        place = pl.multiple_of((p0 * 4 + (p1 ^ p2) * 2 + p2) * count, count)
        for j in range(2):
            start = 2 * i * count + j * count
            if start < half_list:
                part = low[start : start + count]
            else:
                start += keep.shape[0] - half_list
                part = got[start : start + count]
            gram[pl.ds(place, count), j * rank : (j + 1) * rank] = part


def fourth_rows(bits, keep, got, low, share):
    rank = keep.shape[1]
    return local(
        fourth_rows_body,
        bits,
        [keep, got, low],
        [vmem(share, rank), vmem(share, rank), vmem(rank, 2 * rank), vmem(keep.shape[0] - 2 * share, rank)],
        2 * keep.size,
        20 * keep.size,
    )


def fifth_rows_body(bits, keep, got, fifth):
    share, rank = fifth.shape[0], keep.shape[1]
    for j in range(2):
        here = slice(j * share, (j + 1) * share)
        fifth[:, j * rank : (j + 1) * rank] = keep[here] + got[here]


def sixth_body(bits, c1, c23, packed, value, gram, keep, send, coef):
    rank = c1.shape[1]
    share = c1.shape[0] // packed.shape[0]
    for j in range(2):
        coef[:, j * rank : (j + 1) * rank] = (
            packed[:, j * share : (j + 1) * share, :].reshape(c1.shape).astype(jnp.bfloat16)
        )
    lhs = jnp.concatenate([c1[...], c23[...], coef[...]], axis=1)
    emit_halves(bits[1], [value[i] - dot(lhs, gram[i]) for i in range(3)], keep, send)


def sixth(bits, c1, c23, packed, value, gram):
    rows, rank = c1.shape
    wide = 2 * rank
    return local(
        sixth_body,
        bits,
        [c1, c23, packed, value, gram],
        [vmem(rows // 2, 3 * wide)] * 2 + [vmem(rows, wide, dtype=jnp.bfloat16)],
        30 * rows * rank * wide,
        24 * rows * wide,
    )


def add_body(bits, left, right, out):
    out[...] = left[...] + right[...]


def add(bits, left, right):
    return local(add_body, bits, [left, right], [vmem(*left.shape)], left.size, 12 * left.size)[0]


def total_body(bits, parts, out):
    out[...] = parts[...].sum(axis=0)


def total(bits, parts):
    return local(total_body, bits, [parts], [vmem(*parts.shape[1:])], parts.size, 4 * parts.size)[0]


def lower_body(bits, state, c1, c23, c45, up, out):
    coef = jnp.concatenate([c1[...], c23[...], c45[...]], axis=1)
    depth, leaf = coef.shape[1], state.shape[1]
    width = leaf // STEPS
    for i in range(STEPS):
        here = slice(i * width, (i + 1) * width)
        basis = up[: depth // c1.shape[1], :, here].reshape(depth, width)
        out[:, here] = state[:, here].astype(jnp.float32) - dot(coef, basis)


def lower(bits, state, c1, c23, c45, up_basis):
    rows, leaf = state.shape
    return local(
        lower_body,
        bits,
        [state, c1, c23, c45, up_basis],
        [vmem(rows, leaf)],
        10 * rows * leaf * c1.shape[1],
        6 * rows * leaf,
    )[0]


def last_body(bits, state, mine, received, up, out, coef, block, done):
    rank, count = up.shape[1], mine.shape[0]
    for bit in range(2):

        @pl.when(bits[1] == bit)
        def _(bit=bit):
            here = slice(bit * count, (bit + 1) * count)
            there = slice((1 - bit) * count, (2 - bit) * count)
            coef[here, :] = mine[:, : 3 * rank].astype(jnp.bfloat16)
            coef[there, :rank] = received[:, 2 * rank :].astype(jnp.bfloat16)
            coef[there, rank:] = received[:, : 2 * rank].astype(jnp.bfloat16)

    basis = up[5:8].reshape(3 * rank, up.shape[2])
    share = state.shape[0] // STEPS
    copies = []
    for i in range(STEPS):
        here = pl.ds(i * share, share)
        block[here] = state[here] - dot(coef[here], basis)
        copies.append(pltpu.make_async_copy(block.at[here], out.at[here], done.at[i]))
        copies[-1].start()
    for copy in copies:
        copy.wait()


def last(bits, state, mine, received, up_basis):
    rows, leaf = state.shape
    rank = up_basis.shape[1]
    args = [pltpu.with_memory_space_constraint(a, pltpu.VMEM) for a in (state, mine, received, up_basis)]
    return pl.pallas_call(
        last_body,
        out_shape=f32(rows, leaf),
        in_specs=[pl.BlockSpec(memory_space=pltpu.SMEM)] + [pl.BlockSpec(memory_space=pltpu.VMEM)] * 4,
        out_specs=pl.BlockSpec(memory_space=pltpu.HBM),
        scratch_shapes=[
            pltpu.VMEM((rows, 3 * rank), jnp.bfloat16),
            pltpu.VMEM((rows, leaf), jnp.float32),
            pltpu.SemaphoreType.DMA((STEPS,)),
        ],
        compiler_params=pltpu.CompilerParams(vmem_limit_bytes=VMEM_BYTES),
        cost_estimate=pl.CostEstimate(
            flops=6 * rows * leaf * rank, bytes_accessed=6 * rows * leaf, transcendentals=0
        ),
    )(bits, *args)


def shards(groups_z, groups_zy, rhs, leaf_inverse, up_basis, projection):
    size_x, size_y = lax.axis_size("gx"), lax.axis_size("gy")
    rows = rhs.shape[0]
    rank = up_basis.shape[1]
    wide = 2 * rank
    gx, gy = lax.axis_index("gx"), lax.axis_index("gy")
    z0, z1, z2, y0, y1 = (gx >> i & 1 for i in range(5))
    core, x0, x1 = (gy >> i & 1 for i in range(3))
    bits = jnp.stack([z0, core, y0, z1, z1 ^ z2, z2, z1 + 2 * z2])
    over_x = functools.partial(swap, axis="gx", size=size_x)
    over_y = functools.partial(swap, axis="gy", size=size_y)
    ring = RING
    share = rows // ring
    by_y01, by_y1 = starts(y0 ^ y1, 3 * rank // 2), starts(y1, 3 * rank // 4)
    half_y1 = starts(y1, rank)
    half_core, half_x0, half_x1 = starts(core, rank), starts(x0, rank), starts(x1, rank)
    indices = (
        bits, by_y01, by_y1, half_y1,
        half_core, half_x0, half_x1, y1 == 0, (y0 ^ y1) == 0,
    )
    indices, rhs = lax.optimization_barrier((indices, rhs))
    (
        bits, by_y01, by_y1, half_y1,
        half_core, half_x0, half_x1, first_y1, first_y01,
    ) = indices

    state, own, other = leaf_solve(bits, rhs, leaf_inverse, projection)
    received = over_x(other, mask=1)
    value, gram, kept = project((2, 3), ((2, 3),), bits, state, up_basis, projection)
    value_45, gram_45, kept_45 = project((4, 5), ((4, 5),), bits, state, up_basis, projection)

    value_678, gram_678, kept_678 = project((6, 7, 8), ((6, 7), (6, 8), (7, 8)), bits, state, up_basis, projection)
    received, kept, kept_45, kept_678 = lax.optimization_barrier((received, kept, kept_45, kept_678))

    keep, send, keep_3, send_3, c1 = second(bits, own, received, value, gram, kept, kept_45)
    received = over_x(send, mask=1)
    left = over_x(send_3, mask=1)
    own, send, low = third(bits, keep, received)
    send, kept_678 = lax.optimization_barrier((send, kept_678))
    high, high_send = split(kept_678.reshape(3 * rank, wide), by_y01)
    high, high_send = split(high + over_x(high_send, mask=8), by_y1)
    high = high + over_x(high_send, mask=24)
    high = jnp.concatenate([high[:, :rank], high[:, rank:]])

    c2, own, send, low = correct(bits, own, over_x(send, mask=2), low, keep_3, left)
    received = over_x(send, mask=6)
    c3, low = own + received[: rows // 2], low + received[rows // 2 :]
    c3 = c3 + over_x(c3, mask=2)
    c2_there = over_x(c2, mask=1)
    c3_there = over_x(c3, mask=1)

    keep_a, send_a, keep_b, send_b, c23 = fourth(bits, c1, c2, c3, c2_there, c3_there, value_45, gram_45, low, high)
    turned = [(i & -RING) + ((i + 1 if i & 1 else i - 1) % RING) for i in range(size_x)]
    got_a, got_b = over_x(send_a, mask=1), lax.ppermute(send_b, "gx", list(enumerate(turned)))
    keep_a, send_a, low = halve(bits, 2, 1, 3, keep_a, got_a, low)
    got_a = over_x(send_a, mask=2)
    keep_b, send_b = halve(bits, 2, 3, 1, keep_b, got_b)
    got_b = over_x(send_b, mask=6)
    keep_a, send_a, low = halve(bits, 1, 0, 0, keep_a, got_a, low)
    got_a = over_x(send_a, mask=6)
    keep_b, send_b = halve(bits, 1, 0, 0, keep_b, got_b)
    got_b = over_x(send_b, mask=2)
    own, other, gram_45, high = fourth_rows(bits, keep_a, got_a, low, share)
    c4 = own + over_x(other, mask=8)
    left = local(fifth_rows_body, bits, [keep_b, got_b], [vmem(share, wide)], keep_b.size, 12 * keep_b.size)[0]
    left = left - dot(c4, gram_45)
    received = over_x(jnp.concatenate([half(left, half_y1[1]), high]), mask=24)
    c5 = half(left, half_y1[0]) + received[:share]
    high = join(high, received[share:], first_y1)
    received = over_x(jnp.concatenate([c5, high]), mask=8)
    c5 = c5 + received[:share]
    high = join(high, received[share:], first_y01)
    packed = jnp.concatenate([c4, c5, high], axis=0)
    packed = exchange(jnp.broadcast_to(packed, (ring, *packed.shape)), groups_z)

    keep, send, c45 = sixth(bits, c1, c23, packed, value_678, gram_678)
    left = add(bits, keep, over_y(send, mask=1))
    high = packed[:, 2 * share :].reshape(2, ring // 2, 4, 3 * rank // (2 * ring), rank)
    high = jnp.concatenate(list(high.transpose(0, 2, 1, 3, 4).reshape(2, 3 * rank, rank)), axis=1)
    high_there = over_y(high, mask=1)
    left, high, high_there = lax.optimization_barrier((left, high, high_there))
    half_rows = rows // 2
    count = half_rows // size_x
    left = total(bits, exchange(left.reshape(size_x, count, 3 * wide), groups_zy))
    left, c45 = lax.optimization_barrier((left, c45))
    high, high_there = high.reshape(3, rank, wide), high_there.reshape(3, rank, wide)
    c6, c6_there = half(left[:, :wide], half_core[0]), half(left[:, :wide], half_core[1])
    z7 = left[:, wide : 2 * wide] - exact_dot(c6, high[0]) - exact_dot(c6_there, high_there[0])
    z8 = left[:, 2 * wide :] - exact_dot(c6, high[1]) - exact_dot(c6_there, high_there[1])
    c7 = half(z7, half_x0[0]) + over_y(half(z7, half_x0[1]), mask=2)
    z8 = z8 - exact_dot(c7, high[2] + high_there[2])
    c8 = half(z8, half_x1[0]) + over_y(half(z8, half_x1[1]), mask=6)
    c8 = c8 + over_y(c8, mask=2)
    state = lower(bits, state, c1, c23, c45, up_basis)
    packed = jnp.concatenate([c6, c7, c8, c6_there], axis=1)
    packed, state = lax.optimization_barrier((packed, state))
    packed = exchange(jnp.broadcast_to(packed, (size_x, *packed.shape)), groups_zy)
    packed = packed.reshape(half_rows, 4 * rank)
    received = over_y(packed[:, rank:], mask=1)
    return last(bits, state, packed, received, up_basis)


def solution(mesh):
    size_x, size_y = mesh.shape["gx"], mesh.shape["gy"]
    ring = RING
    groups_z = [
        [gy * size_x + start + i for i in range(ring)]
        for gy in range(size_y)
        for start in range(0, size_x, ring)
    ]
    groups_zy = [[gy * size_x + i for i in range(size_x)] for gy in range(size_y)]
    return jax.shard_map(
        functools.partial(shards, groups_z, groups_zy),
        mesh=mesh,
        in_specs=(
            P(None, ("gy", "gx")),
            P(("gy", "gx"), None, None),
            P(None, None, ("gy", "gx")),
            P(None, None, ("gy", "gx")),
        ),
        out_specs=P(None, ("gy", "gx")),
        check_vma=False,
    )
```
